32 devices in a mesh: frames: 8 (over y, x, core), pos: 4 (over z).
Axes of the slice: x: 2, y: 2, z: 4, core: 2. Of those that a mesh axis runs over, the one named last changes fastest.
Arguments:
- frames_in: bfloat16 [512, 16, 1024], P(('frames', 'pos')), may hold values from -6 to 6
- frame_valid: int32 [512], P(('frames', 'pos')), may hold values 0 or 1
- last_position: int32 [512], P(('frames', 'pos')), may hold values from 0 to 15
- weight_qkv: bfloat16 [16, 1024, 3072], P('pos', 'frames'), may hold values from -0.1875 to 0.1875
- weight_out: bfloat16 [16, 1024, 1024], P('pos', 'frames'), may hold values from -0.5 to 0.5
- weight_ffn: bfloat16 [16, 1024, 5632], P('pos', 'frames'), may hold values from -0.1875 to 0.1875
- weight_down: bfloat16 [16, 2816, 1024], P('pos', 'frames'), may hold values from -0.109375 to 0.109375
- gain_attn: bfloat16 [16, 1024], P('pos', 'frames'), may hold values from 0.5 to 1.5
- gain_ffn: bfloat16 [16, 1024], P('pos', 'frames'), may hold values from 0.5 to 1.5
- grad_out: bfloat16 [512, 16, 1024], P(('frames', 'pos')), may hold values from -6 to 6
Outputs:
- output: bfloat16 [512, 16, 1024], P(('frames', 'pos'))
- grad_input: bfloat16 [512, 16, 1024], P(('frames', 'pos'))
- grad_qkv: float32 [16, 1024, 3072], P('pos', 'frames')
- grad_wout: float32 [16, 1024, 1024], P('pos', 'frames')
- grad_ffn: float32 [16, 1024, 5632], P('pos', 'frames')
- grad_down: float32 [16, 2816, 1024], P('pos', 'frames')
- grad_gain_attn: float32 [16, 1024], P('pos', 'frames')
- grad_gain_ffn: float32 [16, 1024], P('pos', 'frames')
The draws below stay inside these ranges and needn't reach their ends.
All inputs are finite; a program needn't handle non-finite values. No bound on the sum of `frame_valid` on one device may be relied on, other than what follows from the above.
Results may differ from the reference program's by a relative error of at most 0.015.
Values may be sent and summed in bfloat16 or wider, within the bound.
No kernel may reach another device: no remote copies, remote signals or barrier semaphores. Data moves between devices by JAX's collectives and lax.ppermute only.
A program may use at most 384 MiB of HBM per device.

```python
import math
import jax
import jax.numpy as jnp
from jax import lax

D = 1024
HEADS = 16
HEAD = 64
FF = 2816
POS = 16
FRAMES = 512


def set_ends(array, rng, least, high):
    spot = [jax.random.randint(jax.random.fold_in(rng, axis), (), 0, length) for axis, length in enumerate(array.shape)]
    main_axis = array.shape.index(max(array.shape))
    next_to = spot[:main_axis] + [(spot[main_axis] + 1) % array.shape[main_axis]] + spot[main_axis + 1:]
    return array.at[tuple(spot)].set(least).at[tuple(next_to)].set(high)


def level_of(rng, extent, cuts, low, top_value):
    gain, own = 1.0, jax.random.fold_in(rng, 6)
    for position, parts in cuts:
        steps = jnp.exp(jax.random.uniform(jax.random.fold_in(own, position), (parts,), jnp.float32, low / len(cuts), top_value / len(cuts)))
        gain = gain * jnp.repeat(steps, extent[position] // parts).reshape([-1 if axis == position else 1 for axis in range(len(extent))])
    return gain


def centred(rng, shape, deviation, most, split=(), dtype=jnp.bfloat16):
    array = deviation * jax.random.normal(rng, shape, jnp.float32)
    if split:
        array = array * level_of(rng, shape, split, -0.22, 0.18)
    return jnp.clip(array, -most, most).astype(dtype)


def setup_inputs(seed: int = 0) -> dict:
    seeds = jax.random.split(jax.random.key(seed), 11)
    return {
        "frames_in": centred(seeds[0], (FRAMES, POS, D), 1.0, 6.0, ((0, 32),)),
        "frame_valid": set_ends((jax.random.randint(seeds[1], (FRAMES,), 0, 8) < 7).astype(jnp.int32), jax.random.fold_in(seeds[1], 1), 0, 1),
        "last_position": set_ends(jax.random.randint(seeds[2], (FRAMES,), 0, POS), jax.random.fold_in(seeds[2], 1), 0, POS - 1).astype(jnp.int32),
        "weight_qkv": centred(seeds[3], (POS, D, 3 * D), D ** -0.5, 0.1875, ((0, 4), (1, 8))),
        "weight_out": centred(seeds[4], (POS, D, D), (D // 8) ** -0.5, 0.5, ((0, 4), (1, 8))),
        "weight_ffn": centred(seeds[5], (POS, D, 2 * FF), D ** -0.5, 0.1875, ((0, 4), (1, 8))),
        "weight_down": centred(seeds[6], (POS, FF, D), FF ** -0.5, 0.109375, ((0, 4), (1, 8))),
        "gain_attn": jnp.clip(1.0 + 0.1 * jax.random.normal(seeds[7], (POS, D), jnp.float32), 0.5, 1.5).astype(jnp.bfloat16),
        "gain_ffn": jnp.clip(1.0 + 0.1 * jax.random.normal(seeds[8], (POS, D), jnp.float32), 0.5, 1.5).astype(jnp.bfloat16),
        "grad_out": centred(seeds[9], (FRAMES, POS, D), 1.0, 6.0, ((0, 32),)),
    }


EPSILON = 1e-06

@jax.custom_vjp
def low(v):
    return lax.optimization_barrier(v.astype(jnp.bfloat16)).astype(jnp.float32)

@jax.custom_vjp
def low_back(v):
    return v

def low_keep(v):
    return (low(v), None)

def low_pass(kept, grad):
    return (grad,)

def back_keep(v):
    return (v, None)

def back_low(kept, grad):
    return (low(grad),)
low.defvjp(low_keep, low_pass)
low_back.defvjp(back_keep, back_low)

def matmul(pattern, left_side, right_side):
    return jnp.einsum(pattern, left_side, right_side, precision=lax.Precision.HIGHEST)

def rms_scaled(values, gain_row):
    inverse = lax.rsqrt(lax.optimization_barrier(jnp.mean(values * values, axis=-1, keepdims=True)) + EPSILON)
    return values * inverse * gain_row[None]

def layer(inputs, weight_qkv, weight_out, weight_ffn, weight_down, gain_attn, gain_ffn, live_mask):
    blocks = inputs.shape[0]
    length = inputs.shape[1]
    inputs = low_back(inputs)
    normed_one = low(rms_scaled(inputs, gain_attn))
    qkv_rows = low_back(low(matmul('bpd,pde->bpe', normed_one, weight_qkv)))
    pieces = qkv_rows.reshape(blocks, length, 3, HEADS, HEAD)
    query, key_part, value_part = (pieces[:, :, 0], pieces[:, :, 1], pieces[:, :, 2])
    scores = low_back(matmul('bqhe,bkhe->bhqk', query, key_part) * HEAD ** (-0.5))
    allowed = jnp.arange(length)[:, None] >= jnp.arange(length)[None, :]
    scores = jnp.where(allowed, scores, -1e+30)
    attend = jax.nn.softmax(scores, axis=-1)
    mixed_heads = low_back(low(matmul('bhqk,bkhe->bqhe', low(attend), value_part)))
    mixed_heads = mixed_heads.reshape(blocks, length, D)
    branch = low_back(matmul('bpd,pde->bpe', mixed_heads, weight_out))
    middle = inputs + branch
    normed_two = low(rms_scaled(middle, gain_ffn))
    gate_up = low_back(matmul('bpd,pde->bpe', normed_two, weight_ffn))
    hidden = low(jax.nn.silu(gate_up[..., :FF]) * gate_up[..., FF:])
    result = middle + matmul('bpf,pfd->bpd', hidden, weight_down)
    return result * live_mask[:, :, None]

def reference(frames_in, frame_valid, last_position, weight_qkv, weight_out, weight_ffn, weight_down, gain_attn, gain_ffn, grad_out):
    params = tuple((item.astype(jnp.float32) for item in (weight_qkv, weight_out, weight_ffn, weight_down, gain_attn, gain_ffn)))
    block = math.gcd(FRAMES, 256)
    count = FRAMES // block
    slot_index = jnp.arange(POS)
    live_mask = ((frame_valid[:, None] > 0) & (slot_index[None, :] <= last_position[:, None])).astype(jnp.float32)
    input_blocks = frames_in.astype(jnp.float32).reshape(count, block, POS, D)
    grad_blocks = grad_out.astype(jnp.float32).reshape(count, block, POS, D)
    live_blocks = live_mask.reshape(count, block, POS)

    def step(totals, bundle):
        inputs_block, grad_block, live_block = bundle

        def apply_layer(inputs_now, *weights_now):
            return layer(inputs_now, *weights_now, live_block)
        result, pullback = jax.vjp(apply_layer, inputs_block, *params)
        grads = pullback(grad_block)
        summed = tuple((left_side + right_side for left_side, right_side in zip(totals, grads[1:])))
        return (summed, (result.astype(jnp.bfloat16), grads[0].astype(jnp.bfloat16)))
    start = tuple((jnp.zeros(item.shape, jnp.float32) for item in params))
    sums, (outputs, grad_inputs) = lax.scan(step, start, (input_blocks, grad_blocks, live_blocks))
    output = outputs.reshape(FRAMES, POS, D)
    grad_input = grad_inputs.reshape(FRAMES, POS, D)
    return (output, grad_input, sums[0], sums[1], sums[2], sums[3], sums[4], sums[5])
```

```python
import jax
import jax.numpy as jnp
from jax import lax
from jax.sharding import Mesh, PartitionSpec as P

HEAD = 64
EPSILON = 1e-06
NEGATIVE = -1e30

ROWS = ("pos", "spot")
PLANE = ("spot", "half")


def project(left, right, contract):
    return lax.dot_general(left, right, (contract, ((), ())), preferred_element_type=jnp.float32)


def plain(left, right):
    return project(left, right, ((1,), (0,)))


def by_columns(left, right):
    return project(left, right, ((1,), (1,)))


def over_rows(left, right):
    return project(left, right, ((0,), (0,)))


def rms(values):
    inverse = lax.rsqrt(jnp.mean(values * values, axis=-1, keepdims=True) + EPSILON)
    return values * inverse, inverse


def rms_backward(upstream, normed, inverse, gain):
    scaled = upstream * gain
    inner = jnp.mean(scaled * normed, axis=-1, keepdims=True)
    return inverse * (scaled - normed * inner)


def shift(value, step, size):
    return lax.ppermute(value, "half", [(u, (u + step) % size) for u in range(size)])


def gather_halves(own, size):
    return jnp.stack([own] + [shift(own, step, size) for step in range(1, size)])


def sum_own(partial, size):
    total = partial[0]
    for step in range(1, size):
        total = total + shift(partial[step], -step, size)
    return total


def sum_all(partial, size):
    if size == 2:
        return partial + shift(partial, 1, size)[::-1]
    return gather_halves(sum_own(partial, size), size)


def to_spots(weight, local, halves, plane):
    mine = lax.axis_index("spot")
    index = lax.axis_index(PLANE)
    out = jnp.zeros((local,) + weight.shape[1:], weight.dtype)
    for step in range(local):
        pairs = [(f, (f % local + step) % local * halves + f // local) for f in range(plane)]
        piece = lax.dynamic_index_in_dim(weight, (index + step) % local, 0, keepdims=False)
        piece = lax.ppermute(piece, PLANE, pairs)
        out = lax.dynamic_update_index_in_dim(out, piece, (mine - step) % local, 0)
    return out.reshape(-1, weight.shape[-1])


def from_spots(grad, local, halves, plane):
    mine = lax.axis_index("spot")
    index = lax.axis_index(PLANE)
    grad = grad.reshape(local, -1, grad.shape[-1])
    pieces = []
    for step in range(local):
        pairs = [((f % local + step) % local * halves + f // local, f) for f in range(plane)]
        piece = lax.dynamic_index_in_dim(grad, (mine - step) % local, 0, keepdims=False)
        pieces.append(lax.ppermute(piece, PLANE, pairs))
    pieces = jnp.stack(pieces)
    placed = [
        lax.dynamic_index_in_dim(pieces, (position - index) % local, 0, keepdims=False)
        for position in range(local)
    ]
    return jnp.stack(placed).astype(jnp.float32)


def columns_to_spots(weight, groups, halves):
    local, depth, width = weight.shape
    split = weight.reshape(local, depth, groups, halves, width // groups // halves)
    split = jnp.transpose(split, (0, 3, 1, 2, 4)).reshape(local * halves, depth, width // halves)
    moved = lax.all_to_all(split, PLANE, split_axis=0, concat_axis=0, tiled=True)
    return moved.reshape(-1, width // halves)


def columns_from_spots(grad, groups, halves, plane):
    depth = grad.shape[0] // plane
    width = grad.shape[1] * halves
    moved = lax.all_to_all(
        grad.reshape(plane, depth, grad.shape[1]), PLANE, split_axis=0, concat_axis=0, tiled=True
    )
    moved = moved.reshape(plane // halves, halves, depth, groups, width // groups // halves)
    return jnp.transpose(moved, (0, 2, 3, 1, 4)).reshape(-1, depth, width).astype(jnp.float32)


def rows_to_spots(values):
    moved = lax.all_to_all(values, ROWS, split_axis=1, concat_axis=0, tiled=True)
    return moved.reshape(moved.shape[0], moved.shape[2])


def rows_from_spots(values):
    return lax.all_to_all(values[:, None], ROWS, split_axis=0, concat_axis=1, tiled=True)


def swap(values, blocks):
    return lax.all_to_all(
        values.reshape(blocks, -1, values.shape[-1]), ROWS, split_axis=0, concat_axis=0, tiled=True
    )


def scores_of(query, key_part):
    raw = jnp.einsum("qfhe,kfhe->fhqk", query, key_part, preferred_element_type=jnp.float32)
    length = raw.shape[-1]
    allowed = lax.broadcasted_iota(jnp.int32, (length, length), 0) >= lax.broadcasted_iota(
        jnp.int32, (length, length), 1
    )
    return jnp.where(allowed, raw * HEAD ** (-0.5), NEGATIVE)


def pieces_of(qkv):
    positions, frames, width = qkv.shape
    pieces = qkv.reshape(positions, frames, 3, width // 3 // HEAD, HEAD)
    return pieces[:, :, 0], pieces[:, :, 1], pieces[:, :, 2]


def attend(qkv):
    query, key_part, value_part = pieces_of(qkv)
    scores = scores_of(query, key_part)
    top = jnp.max(scores, axis=-1, keepdims=True)
    exponent = jnp.exp(scores - top)
    total = jnp.sum(exponent, axis=-1, keepdims=True)
    low = (exponent / total).astype(jnp.bfloat16)
    mixed = jnp.einsum("fhqk,kfhe->qfhe", low, value_part, preferred_element_type=jnp.float32)
    return mixed.reshape(qkv.shape[0], qkv.shape[1], -1).astype(jnp.bfloat16), top + jnp.log(total)


def attend_backward(qkv, log_total, grad_mixed):
    query, key_part, value_part = pieces_of(qkv)
    grad_heads = grad_mixed.reshape(query.shape)
    f32 = jnp.float32
    probs = jnp.exp(scores_of(query, key_part) - log_total)
    grad_value = jnp.einsum(
        "fhqk,qfhe->kfhe", probs.astype(jnp.bfloat16), grad_heads, preferred_element_type=f32
    )
    grad_probs = jnp.einsum("qfhe,kfhe->fhqk", grad_heads, value_part, preferred_element_type=f32)
    inner = jnp.sum(probs * grad_probs, axis=-1, keepdims=True)
    grad_scores = (probs * (grad_probs - inner)).astype(jnp.bfloat16)
    scale = HEAD ** (-0.5)
    grad_query = jnp.einsum("fhqk,kfhe->qfhe", grad_scores, key_part, preferred_element_type=f32)
    grad_key = jnp.einsum("fhqk,qfhe->kfhe", grad_scores, query, preferred_element_type=f32)
    stacked = jnp.stack([grad_query * scale, grad_key * scale, grad_value], axis=2)
    return stacked.reshape(qkv.shape).astype(jnp.bfloat16)


def on_device(
    frames_in,
    frame_valid,
    last_position,
    weight_qkv,
    weight_out,
    weight_ffn,
    weight_down,
    gain_attn,
    gain_ffn,
    grad_out,
):
    f32, bf16 = jnp.float32, jnp.bfloat16
    frames, positions, depth = frames_in.shape
    local = weight_qkv.shape[0]
    plane = depth // weight_qkv.shape[1]
    halves = plane // local
    slot = lax.broadcasted_iota(jnp.int32, (frames, positions), 1)
    live = ((frame_valid[:, None] > 0) & (slot <= last_position[:, None]))[:, :, None]

    gains = jnp.stack([gain_attn, gain_ffn], axis=1)
    gains = jnp.repeat(gains, halves, axis=0)
    gains = lax.all_to_all(gains, PLANE, split_axis=0, concat_axis=0, tiled=True)
    gain_one, gain_two = jnp.transpose(gains, (1, 0, 2)).reshape(2, 1, depth).astype(f32)
    own_rows = rows_to_spots(frames_in)
    full_qkv = columns_to_spots(weight_qkv, 3, halves)
    full_out = to_spots(weight_out, local, halves, plane)
    upstream_own = rows_to_spots(jnp.where(live, grad_out, jnp.zeros_like(grad_out)))
    full_ffn = columns_to_spots(weight_ffn, 2, halves)
    full_down = to_spots(weight_down, local, halves, plane)

    own_count = own_rows.shape[0]
    count = own_count * halves
    rows = gather_halves(own_rows, halves).reshape(count, depth)
    residual = rows.astype(f32)
    unit_one, _ = rms(residual)
    normed_one = (unit_one * gain_one).astype(bf16)
    qkv_rows = plain(normed_one, full_qkv).astype(bf16)
    qkv = swap(qkv_rows, positions)
    mixed_frames, log_total = attend(qkv)
    mixed = swap(mixed_frames, positions).reshape(count, -1)
    branch = sum_all(plain(mixed, full_out).reshape(halves, own_count, depth), halves)
    middle = residual + branch.reshape(count, depth)

    unit_two, inverse_two = rms(middle)
    normed_two = (unit_two * gain_two).astype(bf16)
    gate_up = plain(normed_two, full_ffn)
    width = gate_up.shape[1] // 2
    gate, upward = gate_up[:, :width], gate_up[:, width:]
    gate_sig = jax.nn.sigmoid(gate)
    hidden = (gate * gate_sig * upward).astype(bf16)
    down = plain(hidden, full_down).reshape(halves, own_count, depth)
    result = middle[:own_count] + sum_own(down, halves)
    result = rows_from_spots(result.astype(bf16))
    output = jnp.where(live, result, jnp.zeros_like(result))

    upstream = gather_halves(upstream_own, halves).reshape(count, depth)
    sum_down = from_spots(over_rows(hidden, upstream).astype(bf16), local, halves, plane)
    grad_hidden = by_columns(upstream, full_down)
    grad_upward = grad_hidden * gate * gate_sig
    grad_gate = grad_hidden * upward * gate_sig * (1.0 + gate * (1.0 - gate_sig))
    grad_gate_up = jnp.concatenate([grad_gate, grad_upward], axis=-1).astype(bf16)
    sum_ffn = columns_from_spots(over_rows(normed_two, grad_gate_up).astype(bf16), 2, halves, plane)
    grad_normed_two = by_columns(grad_gate_up, full_ffn).reshape(halves, own_count, depth)
    grad_normed_two = sum_all(grad_normed_two, halves).reshape(count, depth)
    term_two = jnp.sum((grad_normed_two * unit_two)[:own_count], axis=0)
    grad_middle = upstream.astype(f32) + rms_backward(
        grad_normed_two, unit_two, inverse_two, gain_two
    )

    grad_branch = grad_middle.astype(bf16)
    grad_mixed = by_columns(grad_branch, full_out).astype(bf16)
    grad_qkv_frames = attend_backward(qkv, log_total, swap(grad_mixed, positions))
    sum_out = from_spots(over_rows(mixed, grad_branch).astype(bf16), local, halves, plane)
    grad_qkv_rows = swap(grad_qkv_frames, positions).reshape(count, -1)
    sum_qkv = columns_from_spots(
        over_rows(normed_one, grad_qkv_rows).astype(bf16), 3, halves, plane
    )
    grad_normed_one = by_columns(grad_qkv_rows, full_qkv).reshape(halves, own_count, depth)
    grad_normed_one = sum_own(grad_normed_one, halves)
    own_unit, own_inverse = rms(own_rows.astype(f32))
    term_one = jnp.sum(grad_normed_one * own_unit, axis=0)
    grad_rows = grad_middle[:own_count] + rms_backward(
        grad_normed_one, own_unit, own_inverse, gain_one
    )
    grad_input = rows_from_spots(grad_rows.astype(bf16))

    terms = jnp.stack([term_one, term_two]).reshape(2, plane, depth // plane)
    terms = lax.all_to_all(
        jnp.transpose(terms, (1, 0, 2)), PLANE, split_axis=0, concat_axis=0, tiled=True
    )
    terms = jnp.sum(terms.reshape(local, halves, 2, depth // plane), axis=1)
    return (output, grad_input, sum_qkv, sum_out, sum_ffn, sum_down, terms[:, 0], terms[:, 1])


def solution(mesh):
    plane, lines = mesh.shape["frames"], mesh.shape["pos"]

    def run(*arrays):
        local = arrays[0].shape[1] // lines
        inner = Mesh(
            mesh.devices.reshape(local, plane // local, lines), ("spot", "half", "pos")
        )
        by_frame = P(("spot", "half", "pos"))
        weight = P("pos", ("spot", "half"))
        return jax.shard_map(
            on_device,
            mesh=inner,
            in_specs=(by_frame,) * 3 + (weight,) * 6 + (by_frame,),
            out_specs=(by_frame,) * 2 + (weight,) * 6,
            check_vma=False,
        )(*arrays)

    return run
```

```python
import functools

import jax
import jax.numpy as jnp
from jax import lax
from jax.experimental import pallas as pl
from jax.experimental.pallas import tpu as pltpu
from jax.sharding import Mesh, PartitionSpec as P

HEADS = 16
HEAD = 64
LANES = 128
EPSILON = 1e-06
NEGATIVE = -1e30


def rms_forward(values, gain_row):
    inverse = lax.rsqrt(jnp.mean(values * values, axis=-1, keepdims=True) + EPSILON)
    normed = values * inverse
    return (normed * gain_row[None], normed, inverse)


def rms_backward(upstream, normed, inverse, gain_row):
    scaled = upstream * gain_row[None]
    row_inner = jnp.mean(scaled * normed, axis=-1, keepdims=True)
    return (inverse * (scaled - normed * row_inner), jnp.sum(upstream * normed, axis=0))


def project(pattern, left_side, right_side):
    return jnp.einsum(pattern, left_side, right_side, preferred_element_type=jnp.float32)


def split_heads(qkv_frames):
    frames = qkv_frames.shape[0]
    length = qkv_frames.shape[1]
    pieces = qkv_frames.reshape(frames, length, 3, HEADS, HEAD)
    return (pieces[:, :, 0], pieces[:, :, 1], pieces[:, :, 2])


def masked_scores(query, key_part):
    raw_scores = project("fqhe,fkhe->fhqk", query, key_part) * HEAD ** (-0.5)
    length = raw_scores.shape[-1]
    allowed = lax.broadcasted_iota(jnp.int32, (length, length), 0) >= lax.broadcasted_iota(
        jnp.int32, (length, length), 1
    )
    return jnp.where(allowed, raw_scores, NEGATIVE)


def gathered_plan(
    frames_in,
    frame_valid,
    last_position,
    weight_qkv,
    weight_out,
    weight_ffn,
    weight_down,
    gain_attn,
    gain_ffn,
    grad_out,
):
    scale = HEAD ** (-0.5)
    slot_index = lax.broadcasted_iota(jnp.int32, (frames_in.shape[0], frames_in.shape[1]), 1)
    live_mask = (frame_valid[:, None] > 0) & (slot_index <= last_position[:, None])
    pos_rows = lax.all_to_all(frames_in, "pos", split_axis=1, concat_axis=0, tiled=True)
    full_qkv, full_out, full_gain_a = (
        lax.all_gather(weight_qkv, "frames", axis=1, tiled=True),
        lax.all_gather(weight_out, "frames", axis=1, tiled=True),
        lax.all_gather(gain_attn, "frames", axis=1, tiled=True),
    )
    gain_one = full_gain_a.astype(jnp.float32)
    residual = pos_rows.astype(jnp.float32)
    scaled_one, normed_one, inverse_one = rms_forward(residual, gain_one)
    normed_one_low = scaled_one.astype(jnp.bfloat16)
    qkv_rows = project("rpd,pde->rpe", normed_one_low, full_qkv).astype(jnp.bfloat16)
    qkv_frames = lax.all_to_all(qkv_rows, "pos", split_axis=0, concat_axis=1, tiled=True)
    query, key_part, value_part = split_heads(qkv_frames)
    scores = masked_scores(query, key_part)
    row_top = jnp.max(scores, axis=-1, keepdims=True)
    exponent = jnp.exp(scores - row_top)
    row_total = jnp.sum(exponent, axis=-1, keepdims=True)
    log_total = row_top + jnp.log(row_total)
    attend_low = (exponent / row_total).astype(jnp.bfloat16)
    mixed_heads = project("fhqk,fkhe->fqhe", attend_low, value_part)
    mixed_low = mixed_heads.reshape(frames_in.shape).astype(jnp.bfloat16)
    mixed_rows = lax.all_to_all(mixed_low, "pos", split_axis=1, concat_axis=0, tiled=True)
    middle = residual + project("rpd,pde->rpe", mixed_rows, full_out)
    full_ffn, full_down, full_gain_f = (
        lax.all_gather(weight_ffn, "frames", axis=1, tiled=True),
        lax.all_gather(weight_down, "frames", axis=1, tiled=True),
        lax.all_gather(gain_ffn, "frames", axis=1, tiled=True),
    )
    gain_two = full_gain_f.astype(jnp.float32)
    scaled_two, normed_two, inverse_two = rms_forward(middle, gain_two)
    normed_two_low = scaled_two.astype(jnp.bfloat16)
    gate_up = project("rpd,pde->rpe", normed_two_low, full_ffn)
    width = gate_up.shape[-1] // 2
    gate = gate_up[..., :width]
    upward = gate_up[..., width:]
    gate_sig = jax.nn.sigmoid(gate)
    hidden = (gate * gate_sig * upward).astype(jnp.bfloat16)
    result = middle + project("rpf,pfd->rpd", hidden, full_down)
    result_frames = lax.all_to_all(
        result.astype(jnp.bfloat16), "pos", split_axis=0, concat_axis=1, tiled=True
    )
    output = jnp.where(live_mask[:, :, None], result_frames, jnp.zeros_like(result_frames))
    upstream = jnp.where(live_mask[:, :, None], grad_out, jnp.zeros_like(grad_out))
    upstream_rows = lax.all_to_all(upstream, "pos", split_axis=1, concat_axis=0, tiled=True)
    back_ffn, back_down = (
        lax.all_gather(weight_ffn, "frames", axis=1, tiled=True),
        lax.all_gather(weight_down, "frames", axis=1, tiled=True),
    )
    grad_hidden = project("rpd,pfd->rpf", upstream_rows, back_down)
    term_down = project("rpf,rpd->pfd", hidden, upstream_rows)
    grad_upward = grad_hidden * gate * gate_sig
    grad_gate = grad_hidden * upward * gate_sig * (1.0 + gate * (1.0 - gate_sig))
    grad_gate_up = jnp.concatenate([grad_gate, grad_upward], axis=-1).astype(jnp.bfloat16)
    grad_normed_two = project("rpe,pde->rpd", grad_gate_up, back_ffn)
    term_ffn = project("rpd,rpe->pde", normed_two_low, grad_gate_up)
    grad_middle_norm, term_gain_f = rms_backward(grad_normed_two, normed_two, inverse_two, gain_two)
    grad_middle = upstream_rows.astype(jnp.float32) + grad_middle_norm
    sum_ffn, sum_down, sum_gain_f = (
        lax.psum_scatter(
            term_ffn.astype(jnp.bfloat16), "frames", scatter_dimension=1, tiled=True
        ).astype(jnp.float32),
        lax.psum_scatter(
            term_down.astype(jnp.bfloat16), "frames", scatter_dimension=1, tiled=True
        ).astype(jnp.float32),
        lax.psum_scatter(
            term_gain_f.astype(jnp.bfloat16), "frames", scatter_dimension=1, tiled=True
        ).astype(jnp.float32),
    )
    back_qkv, back_out = (
        lax.all_gather(weight_qkv, "frames", axis=1, tiled=True),
        lax.all_gather(weight_out, "frames", axis=1, tiled=True),
    )
    grad_branch = grad_middle.astype(jnp.bfloat16)
    grad_mixed = project("rpe,pde->rpd", grad_branch, back_out).astype(jnp.bfloat16)
    term_out = project("rpd,rpe->pde", mixed_rows, grad_branch)
    grad_mixed_frames = lax.all_to_all(grad_mixed, "pos", split_axis=0, concat_axis=1, tiled=True)
    grad_heads = grad_mixed_frames.reshape(query.shape)
    again_scores = masked_scores(query, key_part)
    attend = jnp.exp(again_scores - log_total)
    grad_value = project("fhqk,fqhe->fkhe", attend.astype(jnp.bfloat16), grad_heads)
    grad_attend = project("fqhe,fkhe->fhqk", grad_heads, value_part)
    row_inner = jnp.sum(attend * grad_attend, axis=-1, keepdims=True)
    grad_scores = (attend * (grad_attend - row_inner)).astype(jnp.bfloat16)
    grad_query = project("fhqk,fkhe->fqhe", grad_scores, key_part) * scale
    grad_key = project("fhqk,fqhe->fkhe", grad_scores, query) * scale
    grad_qkv_frames = (
        jnp.stack([grad_query, grad_key, grad_value], axis=2)
        .reshape(qkv_frames.shape)
        .astype(jnp.bfloat16)
    )
    grad_qkv_rows = lax.all_to_all(grad_qkv_frames, "pos", split_axis=1, concat_axis=0, tiled=True)
    grad_normed_one = project("rpe,pde->rpd", grad_qkv_rows, back_qkv)
    term_qkv = project("rpd,rpe->pde", normed_one_low, grad_qkv_rows)
    grad_input_norm, term_gain_a = rms_backward(grad_normed_one, normed_one, inverse_one, gain_one)
    grad_rows = (grad_middle + grad_input_norm).astype(jnp.bfloat16)
    grad_frames = lax.all_to_all(grad_rows, "pos", split_axis=0, concat_axis=1, tiled=True)
    sum_qkv, sum_out, sum_gain_a = (
        lax.psum_scatter(
            term_qkv.astype(jnp.bfloat16), "frames", scatter_dimension=1, tiled=True
        ).astype(jnp.float32),
        lax.psum_scatter(
            term_out.astype(jnp.bfloat16), "frames", scatter_dimension=1, tiled=True
        ).astype(jnp.float32),
        lax.psum_scatter(
            term_gain_a.astype(jnp.bfloat16), "frames", scatter_dimension=1, tiled=True
        ).astype(jnp.float32),
    )
    return (output, grad_frames, sum_qkv, sum_out, sum_ffn, sum_down, sum_gain_a, sum_gain_f)


ROWS = ("pos", "spot")
PLANE = ("spot", "half")


def plain(left, right):
    return lax.dot_general(left, right, (((1,), (0,)), ((), ())), preferred_element_type=jnp.float32)


def by_columns(left, right):
    return lax.dot_general(left, right, (((1,), (1,)), ((), ())), preferred_element_type=jnp.float32)


def over_rows(left, right):
    return lax.dot_general(left, right, (((0,), (0,)), ((), ())), preferred_element_type=jnp.float32)


def tie(*values):
    return lax.optimization_barrier(values)


def pick(stack, index):
    return lax.dynamic_index_in_dim(stack, index, 0, keepdims=False)


def hop(value, k, spots):
    return value if k == 0 else lax.ppermute(value, "spot", [(i, i ^ k) for i in range(spots)])


def trade(value):
    return lax.ppermute(value, "half", [(0, 1), (1, 0)])


def rows_to_spots(values):
    moved = lax.all_to_all(values, ROWS, split_axis=1, concat_axis=0, tiled=True)
    return moved.reshape(moved.shape[0], moved.shape[2])


def rows_from_spots(values):
    return lax.all_to_all(values[:, None], ROWS, split_axis=0, concat_axis=1, tiled=True)


def swap(values, blocks):
    return lax.all_to_all(
        values.reshape(blocks, -1, values.shape[-1]), ROWS, split_axis=0, concat_axis=0, tiled=True
    )


def head_runs(width, groups, spots):
    size = width // groups // spots // 2
    return [((g * spots + a) * 2 * size, ((g * spots + a) * 2 + 1) * size) for g in range(groups) for a in range(spots)], size


def unit_runs(width, groups):
    size = width // groups // 2
    return [(g * 2 * size, (g * 2 + 1) * size) for g in range(groups)], size


def call(kernel, name, grid, inputs, outputs, scalars, scratch=()):
    moved = sum(a.size * a.dtype.itemsize for a, _, _ in inputs)
    return pl.pallas_call(
        kernel,
        grid_spec=pltpu.PrefetchScalarGridSpec(
            num_scalar_prefetch=1,
            grid=grid,
            in_specs=[pl.BlockSpec(block, where) for _, block, where in inputs],
            out_specs=[pl.BlockSpec(block, where) for _, _, block, where in outputs],
            scratch_shapes=list(scratch),
        ),
        out_shape=[jax.ShapeDtypeStruct(shape, dtype) for shape, dtype, _, _ in outputs],
        compiler_params=pltpu.CompilerParams(vmem_limit_bytes=48 << 20),
        cost_estimate=pl.CostEstimate(flops=0, transcendentals=0, bytes_accessed=moved // 8),
        name=name,
    )(scalars, *[a for a, _, _ in inputs])


def aligned(start, size):
    return pl.ds(pl.multiple_of(start, LANES), size)


def split_kernel(runs, count, per, rests, scalars, *refs):
    starts, size = runs
    pieces, outs = refs[: count * per], refs[count * per :]
    half = scalars[0]
    for k in range(count):
        at = scalars[1 + k]
        for i, (even, odd) in enumerate(starts):
            piece, even, odd = (
                (pieces[k * per + i], 0, size) if per > 1 else (pieces[k], even, odd)
            )
            for out, first, second in ((outs[0], even, odd), (outs[1], odd, even)):
                columns = aligned(first + half * (second - first), size)
                out[pl.ds(at, 1), :, i * size : (i + 1) * size] = piece[:, columns][None]
        for out, (start, width) in zip(outs[2:], rests):
            out[pl.ds(at, 1)] = pieces[k][:, start : start + width][None]


def split_columns(pieces, runs, scalars, rests=()):
    starts, size = runs
    per = len(pieces[0])
    rows, width = pieces[0][0].shape
    count, step = len(pieces), rows // 4
    widths = [len(starts) * size] * 2 + [n for _, n in rests]
    outs = call(
        functools.partial(split_kernel, runs, count, per, rests),
        "split_columns",
        (4,),
        [(a, (step, width), lambda r, s: (r, 0)) for piece in pieces for a in piece],
        [
            ((count, rows, n), pieces[0][0].dtype, (count, step, n), lambda r, s: (0, r, 0))
            for n in widths
        ],
        scalars,
    )
    return [out.reshape(count * rows, -1) for out in outs]


def place_kernel(runs, parts, skip, scalars, *refs):
    out = refs[-1]
    half = scalars[0]
    for k in range((len(refs) - 1) // parts):

        @pl.when(pl.program_id(0) == k)
        def _():
            for p in range(parts):
                ref = refs[k * parts + p]
                if runs is None:
                    out[0] = ref[:, skip:].astype(jnp.float32)
                    continue
                starts, size = runs
                for i, pair in enumerate(starts):
                    first, second = pair[::-1] if p else pair
                    columns = aligned(first + half * (second - first), size)
                    out[0, :, columns] = ref[:, i * size : (i + 1) * size].astype(jnp.float32)


def place(pieces, scalars, rows, width, runs=None, skip=0):
    count, parts = len(pieces), len(pieces[0])
    cuts = 2 if rows * width > (1 << 19) else 1
    step = rows // cuts

    def spec(k, first):
        base = first // step
        return lambda j, r, s: (base + jnp.where(j == k, r, jnp.where(j < k, 0, cuts - 1)), 0)

    return call(
        functools.partial(place_kernel, runs, parts, skip),
        "place",
        (count, cuts),
        [
            (a, (step, a.shape[1]), spec(k, first))
            for k, piece in enumerate(pieces)
            for a, first in piece
        ],
        [
            (
                (count, rows, width),
                jnp.float32,
                (1, step, width),
                lambda j, r, s: (s[1 + j], r, 0),
            )
        ],
        scalars,
    )[0]


def halves_rows(step, own):
    count = own.shape[0] // step
    return (
        lambda r, *s: (jnp.minimum(r, count - 1), 0),
        lambda r, *s: (jnp.maximum(r - count, 0), 0),
    )


def unit_of(values):
    inverse = lax.rsqrt(jnp.mean(values * values, axis=-1, keepdims=True) + EPSILON)
    return values * inverse, inverse


def spread(values, scratch, half, own, other):
    scratch[...] = values.astype(scratch.dtype)
    for a in range(own.shape[1] // LANES):
        own[:, a * LANES : (a + 1) * LANES] = scratch[:, aligned((2 * a + half) * LANES, LANES)]
        other[:, a * LANES : (a + 1) * LANES] = scratch[:, aligned((2 * a + 1 - half) * LANES, LANES)]


def gather(own, other, scratch, half):
    for a in range(own[0].shape[1] // LANES):
        block = slice(a * LANES, (a + 1) * LANES)
        scratch[:, aligned((2 * a + half) * LANES, LANES)] = own[0][:, block] + own[1][:, block]
        scratch[:, aligned((2 * a + 1 - half) * LANES, LANES)] = other[0][:, block] + other[1][:, block]
    return scratch[...]


def either(own_ref, got_ref):
    mine = pl.program_id(0) < pl.num_programs(0) // 2
    return jnp.where(mine, own_ref[...].astype(jnp.float32), got_ref[...].astype(jnp.float32))


def norm_kernel(scalars, own_rows, got_rows, gain, own, other, scratch):
    unit, _ = unit_of(either(own_rows, got_rows))
    spread(unit * gain[...], scratch, scalars[0], own, other)


def middle_kernel(scalars, own_rows, got_rows, branch, got_branch, gain, middle, own, other, scratch):
    values = either(own_rows, got_rows) + (branch[...] + got_branch[...])
    middle[...] = values
    unit, _ = unit_of(values)
    spread(unit * gain[...], scratch, scalars[0], own, other)


def pull(values, upstream, gain):
    unit, inverse = unit_of(values)
    scaled = upstream * gain
    inner = jnp.mean(scaled * unit, axis=-1, keepdims=True)
    return inverse * (scaled - unit * inner), jnp.sum(upstream * unit, axis=0, keepdims=True)


def accumulate(term, value, when):
    @pl.when(pl.program_id(0) == 0)
    def _():
        term[...] = jnp.zeros_like(term)

    @pl.when(when)
    def _():
        term[...] += value


def middle_back_kernel(
    scalars, middle, own, other, got_own, got_other, own_up, got_up, gain, whole, low, term, scratch
):
    upstream = gather((own, got_other), (other, got_own), scratch, scalars[0])
    grad, value = pull(middle[...], upstream, gain[...])
    grad = grad + either(own_up, got_up)
    whole[...] = grad
    low[...] = grad.astype(low.dtype)
    accumulate(term, value, pl.program_id(0) < pl.num_programs(0) // 2)


def input_back_kernel(
    scalars, rows, own, other, got_own, got_other, grad_middle, gain, out, term, scratch
):
    upstream = gather((own, got_other), (other, got_own), scratch, scalars[0])
    grad, value = pull(rows[...].astype(jnp.float32), upstream, gain[...])
    out[...] = (grad_middle[...] + grad).astype(out.dtype)
    accumulate(term, value, True)


def softmax_of(query, keys, allowed):
    scores = jnp.where(allowed, by_columns(query, keys) * HEAD ** (-0.5), NEGATIVE)
    exponent = jnp.exp(scores - jnp.max(scores, axis=-1, keepdims=True))
    return exponent / jnp.sum(exponent, axis=-1, keepdims=True)


def frame_mask(positions, frames):
    count = positions * frames
    row = lax.broadcasted_iota(jnp.int32, (count, count), 0)
    column = lax.broadcasted_iota(jnp.int32, (count, count), 1)
    return (row % frames == column % frames) & (row >= column)


def attend_kernel(qkv_ref, mixed_ref):
    positions, frames, width = qkv_ref.shape
    count, third = positions * frames, width // 3
    allowed = frame_mask(positions, frames)
    lane = lax.broadcasted_iota(jnp.int32, (count, LANES), 1)
    for first in range(0, third, LANES):
        query, keys, values = (
            qkv_ref[:, :, part * third + first : part * third + first + LANES].reshape(count, LANES)
            for part in range(3)
        )
        mixed = jnp.zeros((count, LANES), jnp.float32)
        for start in range(0, LANES, HEAD):
            inside = (lane >= start) & (lane < start + HEAD)
            probs = softmax_of(jnp.where(inside, query, jnp.zeros_like(query)), keys, allowed)
            mixed = jnp.where(inside, plain(probs.astype(jnp.bfloat16), values), mixed)
        mixed_ref[:, :, first : first + LANES] = mixed.astype(mixed_ref.dtype).reshape(
            positions, frames, LANES
        )


def attend_back_kernel(qkv_ref, grad_ref, out_ref):
    positions, frames, width = qkv_ref.shape
    count, third = positions * frames, width // 3
    scale = HEAD ** (-0.5)
    allowed = frame_mask(positions, frames)
    lane = lax.broadcasted_iota(jnp.int32, (count, LANES), 1)
    for first in range(0, third, LANES):
        query, keys, values = (
            qkv_ref[:, :, part * third + first : part * third + first + LANES].reshape(count, LANES)
            for part in range(3)
        )
        upstream = grad_ref[:, :, first : first + LANES].reshape(count, LANES)
        grads = [jnp.zeros((count, LANES), jnp.float32)] * 3
        for start in range(0, LANES, HEAD):
            inside = (lane >= start) & (lane < start + HEAD)
            probs = softmax_of(jnp.where(inside, query, jnp.zeros_like(query)), keys, allowed)
            grad_probs = by_columns(jnp.where(inside, upstream, jnp.zeros_like(upstream)), values)
            inner = jnp.sum(probs * grad_probs, axis=-1, keepdims=True)
            grad_scores = (probs * (grad_probs - inner)).astype(jnp.bfloat16)
            new = (
                plain(grad_scores, keys) * scale,
                over_rows(grad_scores, query) * scale,
                over_rows(probs.astype(jnp.bfloat16), upstream),
            )
            grads = [jnp.where(inside, value, old) for value, old in zip(new, grads)]
        for part, grad in enumerate(grads):
            out_ref[:, :, part * third + first : part * third + first + LANES] = grad.astype(
                out_ref.dtype
            ).reshape(positions, frames, LANES)


def over_frames(kernel, out_width, *arrays):
    positions, frames, width = arrays[0].shape
    step = min(frames, 256 // positions)
    heads = width // 3 // HEAD
    work = frames // step * heads * (step * positions) ** 2
    return pl.pallas_call(
        kernel,
        grid=(frames // step,),
        in_specs=[
            pl.BlockSpec((positions, step, a.shape[2]), lambda i: (0, i, 0)) for a in arrays
        ],
        out_specs=pl.BlockSpec((positions, step, out_width), lambda i: (0, i, 0)),
        out_shape=jax.ShapeDtypeStruct((positions, frames, out_width), arrays[0].dtype),
        compiler_params=pltpu.CompilerParams(vmem_limit_bytes=48 << 20),
        cost_estimate=pl.CostEstimate(
            flops=4 * LANES * work,
            transcendentals=work,
            bytes_accessed=2 * positions * frames * (width + out_width),
        ),
        name=kernel.__name__,
    )(*arrays)


def spots_plan(
    frames_in,
    frame_valid,
    last_position,
    weight_qkv,
    weight_out,
    weight_ffn,
    weight_down,
    gain_attn,
    gain_ffn,
    grad_out,
):
    f32, bf16 = jnp.float32, jnp.bfloat16
    frames, positions, depth = frames_in.shape
    spots, slice_rows = weight_qkv.shape[:2]
    plane, near = spots * 2, spots - 1
    spot, half = lax.axis_index("spot"), lax.axis_index("half")
    heads = head_runs(3 * depth, 3, spots)
    units = unit_runs(weight_ffn.shape[2], 2)
    hidden_units = weight_ffn.shape[2] // 2
    down_index = lax.axis_index(PLANE) % spots
    down_pairs = [
        [(f, (f % spots ^ k) * 2 + f // spots) for f in range(plane)] for k in range(spots)
    ]
    early = spots // 2
    by_spot = jnp.stack([half] + [spot ^ k for k in range(spots)]).astype(jnp.int32)
    by_slice = jnp.stack([half] + [down_index ^ k for k in range(spots)]).astype(jnp.int32)
    slot = lax.broadcasted_iota(jnp.int32, (frames, positions), 1)
    live = ((frame_valid[:, None] > 0) & (slot <= last_position[:, None]))[:, :, None]

    gains = jnp.stack([gain_attn, gain_ffn], axis=2)
    gains = jnp.pad(gains, ((0, 0), (0, 0), (0, LANES - 2)))
    first = [
        jnp.concatenate([pick(part, spot ^ k) for part in (weight_qkv, weight_out, gains)], axis=1)
        for k in range(spots)
    ]
    *first, rows_in = tie(*first, frames_in)
    first = [hop(piece, k, spots) for k, piece in enumerate(first)]
    own_rows = rows_to_spots(rows_in)
    gates = [pick(weight_ffn, spot ^ k)[:, :hidden_units] for k in range(spots)]
    ups = [pick(weight_ffn, spot ^ k)[:, hidden_units:] for k in range(spots)]
    tied = tie(own_rows, *first, *gates)
    own_rows, first, gates = tied[0], tied[1 : spots + 1], list(tied[spots + 1 :])
    gates[:near] = [hop(piece, k, spots) for k, piece in enumerate(gates[:near])]
    got_rows = trade(own_rows)

    own_count = own_rows.shape[0]
    count = own_count * 2
    step = own_count // 2
    qkv_own, qkv_sent, full_out, gains = split_columns(
        [[piece] for piece in first], heads, by_spot, ((3 * depth, depth), (4 * depth, LANES))
    )
    qkv_other = trade(qkv_sent)
    gains = gains[:, :2]
    pair = [part.reshape(spots, slice_rows, 2) for part in (gains, trade(gains))]
    even, odd = (jnp.where(half == h, *pair) for h in range(2))
    gains = jnp.stack([even, odd], axis=1).reshape(depth, 2).T.astype(f32)
    gain_one, gain_two = gains[:1], gains[1:]
    qkv_other, *gates[:near] = tie(qkv_other, *gates[:near])
    mine, theirs = halves_rows(step, own_rows)
    straight = lambda r, *s: (r, 0)
    crossed = lambda r, *s: ((r + 2) % 4, 0)
    top = lambda r, *s: (0, 0)
    rows = [(own_rows, (step, depth), mine), (got_rows, (step, depth), theirs)]
    split_rows = [((count, depth // 2), bf16, (step, depth // 2), straight)] * 2
    low_scratch, scratch = pltpu.VMEM((step, depth), bf16), pltpu.VMEM((step, depth), f32)
    one_own, one_other = call(
        norm_kernel, "norm", (4,), rows + [(gain_one, (1, depth), top)], split_rows, by_spot, [low_scratch]
    )
    qkv_rows = (plain(one_own, qkv_own) + plain(one_other, qkv_other)).astype(bf16)
    tied = tie(*gates, *ups[:near])
    gates, ups[:near] = list(tied[:spots]), tied[spots:]
    ups[:near] = [hop(piece, k, spots) for k, piece in enumerate(ups[:near])]
    gates[near] = hop(gates[near], near, spots)
    qkv = swap(qkv_rows, positions)
    mixed = over_frames(attend_kernel, depth // 2, qkv)
    mixed, *ups[:near], gates[near] = tie(mixed, *ups[:near], gates[near])
    ups[near], gates[near] = tie(ups[near], gates[near])
    ups[near] = hop(ups[near], near, spots)
    third = [pick(weight_down, down_index ^ k) for k in range(spots)]
    gates[near], *third = tie(gates[near], *third)
    third = [lax.ppermute(p, PLANE, down_pairs[k]) for k, p in enumerate(third)]
    mixed = swap(mixed, positions).reshape(count, -1)
    upstream = jnp.where(live, grad_out, jnp.zeros_like(grad_out))
    mixed, upstream = tie(mixed, upstream)
    own_up = rows_to_spots(upstream)
    branch = plain(mixed, full_out)
    branch, ups[near] = tie(branch, ups[near])
    middle, two_own, two_other = call(
        middle_kernel,
        "middle",
        (4,),
        rows
        + [(branch, (step, depth), straight), (trade(branch), (step, depth), crossed)]
        + [(gain_two, (1, depth), top)],
        [((count, depth), f32, (step, depth), straight)] + split_rows,
        by_spot,
        [low_scratch],
    )

    ffn_own, ffn_sent = split_columns(list(zip(gates, ups)), units, by_spot)
    ffn_other = trade(ffn_sent)
    ffn_other, *third[:early] = tie(ffn_other, *third[:early])
    gate_up = plain(two_own, ffn_own) + plain(two_other, ffn_other)
    gate_up, *third = tie(gate_up, *third)
    width = gate_up.shape[1] // 2
    gate, upward = gate_up[:, :width], gate_up[:, width:]
    gate_sig = jax.nn.sigmoid(gate)
    hidden = (gate * gate_sig * upward).astype(bf16)
    got_up = trade(own_up)
    upstream = jnp.concatenate([own_up, got_up])
    down_grad = over_rows(hidden, upstream).astype(bf16).reshape(spots, -1, depth)
    down_sent = [pick(down_grad, spot ^ k) for k in range(spots)]
    hidden, *down_sent = tie(hidden, *down_sent)
    down_back = [[(b, a) for a, b in pairs] for pairs in down_pairs]
    for k in range(0, spots, 2):
        down_sent[k] = lax.ppermute(down_sent[k], PLANE, down_back[k])
    down_sent = list(tie(*down_sent))
    for k in range(1, spots, 2):
        down_sent[k] = lax.ppermute(down_sent[k], PLANE, down_back[k])
    full_down = jnp.zeros((spots,) + third[0].shape, bf16)
    for k, piece in enumerate(third):
        full_down = lax.dynamic_update_index_in_dim(full_down, piece, spot ^ k, 0)
    full_down = full_down.reshape(-1, depth)

    grad_hidden = by_columns(upstream, full_down)
    grad_upward = grad_hidden * gate * gate_sig
    grad_gate = grad_hidden * upward * gate_sig * (1.0 + gate * (1.0 - gate_sig))
    grad_gate_up = jnp.concatenate([grad_gate, grad_upward], axis=-1).astype(bf16)
    back_own = by_columns(grad_gate_up, ffn_own)
    back_other = by_columns(grad_gate_up, ffn_other)
    got_own, got_other = trade(back_own), trade(back_other)
    got_other, grad_gate_up, *down_sent[::2] = tie(got_other, grad_gate_up, *down_sent[::2])
    wide, narrow = (step, depth), (step, depth // 2)
    grad_middle, grad_branch, term_two = call(
        middle_back_kernel,
        "middle_back",
        (4,),
        [(middle, wide, straight), (back_own, narrow, straight), (back_other, narrow, straight)]
        + [(got_own, narrow, crossed), (got_other, narrow, crossed)]
        + [(own_up, wide, mine), (got_up, wide, theirs), (gain_two, (1, depth), top)],
        [
            ((count, depth), f32, wide, straight),
            ((count, depth), bf16, wide, straight),
            ((1, depth), f32, (1, depth), top),
        ],
        by_spot,
        [scratch],
    )

    cut = lambda grad: [pick(grad.reshape(spots, slice_rows, -1), spot ^ k) for k in range(spots)]
    grad_mixed = by_columns(grad_branch, full_out).astype(bf16)
    grad_mixed, *down_sent = tie(grad_mixed, *down_sent)
    grad_mixed_frames = swap(grad_mixed, positions)
    ffn_grad_own = cut(over_rows(two_own, grad_gate_up).astype(bf16))
    ffn_grad_got = cut(trade(over_rows(two_other, grad_gate_up).astype(bf16)))
    tied = tie(*down_sent, *ffn_grad_own)
    down_sent, ffn_grad_own = tied[:spots], list(tied[spots:])
    ffn_grad_own = [hop(piece, k, spots) for k, piece in enumerate(ffn_grad_own)]
    grad_mixed_frames, *ffn_grad_own[:near] = tie(grad_mixed_frames, *ffn_grad_own[:near])
    grad_qkv = over_frames(attend_back_kernel, 3 * depth // 2, qkv, grad_mixed_frames)
    late = [
        jnp.concatenate(pair, axis=1)
        for pair in zip(ffn_grad_got, cut(over_rows(mixed, grad_branch).astype(bf16)))
    ]
    grad_qkv, ffn_grad_own[near], *late = tie(grad_qkv, ffn_grad_own[near], *late)
    late[:near] = [hop(piece, k, spots) for k, piece in enumerate(late[:near])]
    result = plain(hidden, full_down)
    result = (middle[:own_count] + result[:own_count] + trade(result[own_count:])).astype(bf16)
    sum_down = place([[(piece, 0)] for piece in down_sent], by_slice, *weight_down.shape[1:])
    grad_qkv_rows = swap(grad_qkv, positions).reshape(count, -1)
    grad_qkv_rows, result, sum_down, *late = tie(grad_qkv_rows, result, sum_down, *late)
    late[near] = hop(late[near], near, spots)
    result = rows_from_spots(result)
    qkv_grad_got = trade(over_rows(one_other, grad_qkv_rows).astype(bf16))
    qkv_grad_own = over_rows(one_own, grad_qkv_rows).astype(bf16)
    qkv_sent = [jnp.concatenate(pair) for pair in zip(cut(qkv_grad_own), cut(qkv_grad_got))]
    *qkv_sent, grad_qkv_rows = tie(*qkv_sent, grad_qkv_rows)
    qkv_sent = [hop(piece, k, spots) for k, piece in enumerate(qkv_sent)]
    back_own = by_columns(grad_qkv_rows, qkv_own)
    back_other = by_columns(grad_qkv_rows, qkv_other)
    got_own, got_other = trade(back_own[own_count:]), trade(back_other[own_count:])
    got_other, result, late[near] = tie(got_other, result, late[near])
    grad_rows, term_one = call(
        input_back_kernel,
        "input_back",
        (2,),
        [(own_rows, wide, straight), (back_own, narrow, straight), (back_other, narrow, straight)]
        + [(got_own, narrow, straight), (got_other, narrow, straight)]
        + [(grad_middle, wide, straight), (gain_one, (1, depth), top)],
        [((own_count, depth), bf16, wide, straight), ((1, depth), f32, (1, depth), top)],
        by_spot,
        [scratch],
    )
    grad_rows, *qkv_sent[:near] = tie(grad_rows, *qkv_sent[:near])
    grad_input = rows_from_spots(grad_rows)
    grad_input, term_one = tie(grad_input, term_one)
    output = jnp.where(live, result, jnp.zeros_like(result))

    sum_ffn = place(
        [[(own, 0), (got, 0)] for own, got in zip(ffn_grad_own, late)],
        by_spot,
        slice_rows,
        2 * hidden_units,
        units,
    )
    sum_out = place([[(piece, 0)] for piece in late], by_spot, slice_rows, depth, skip=hidden_units)
    sum_qkv = place(
        [[(piece, 0), (piece, slice_rows)] for piece in qkv_sent], by_spot, slice_rows, 3 * depth, heads
    )
    terms = jnp.stack([term_one, term_two]).reshape(2, plane, depth // plane)
    terms = lax.all_to_all(
        jnp.transpose(terms, (1, 0, 2)), PLANE, split_axis=0, concat_axis=0, tiled=True
    )
    terms = jnp.sum(terms.reshape(spots, 2, 2, depth // plane), axis=1)
    return (output, grad_input, sum_qkv, sum_out, sum_ffn, sum_down, terms[:, 0], terms[:, 1])


def solution(mesh):
    plane, lines = mesh.shape["frames"], mesh.shape["pos"]

    def run(*arrays):
        positions, depth = arrays[0].shape[1:]
        spots = positions // lines
        slice_rows = depth // plane
        shares = arrays[5].shape[2] // 4
        fits = plane == 2 * spots and spots & (spots - 1) == 0
        fits = fits and slice_rows % LANES == 0 and shares % LANES == 0
        if fits:
            inner = Mesh(mesh.devices.reshape(spots, 2, lines), PLANE + ("pos",))
            by_frame, weight, plan = P(PLANE + ("pos",)), P("pos", PLANE), spots_plan
        else:
            inner, plan = mesh, gathered_plan
            by_frame, weight = P(("frames", "pos")), P("pos", "frames")
        return jax.shard_map(
            plan,
            mesh=inner,
            in_specs=(by_frame,) * 3 + (weight,) * 6 + (by_frame,),
            out_specs=(by_frame,) * 2 + (weight,) * 6,
            check_vma=False,
        )(*arrays)

    return run
```

```python
import functools

import jax
import jax.numpy as jnp
from jax import lax
from jax.experimental import pallas as pl
from jax.experimental.pallas import tpu as pltpu
from jax.sharding import Mesh, PartitionSpec as P

HEADS = 16
HEAD = 64
LANES = 128
EPSILON = 1e-06
NEGATIVE = -1e30


def rms_forward(values, gain_row):
    inverse = lax.rsqrt(jnp.mean(values * values, axis=-1, keepdims=True) + EPSILON)
    normed = values * inverse
    return (normed * gain_row[None], normed, inverse)


def rms_backward(upstream, normed, inverse, gain_row):
    scaled = upstream * gain_row[None]
    row_inner = jnp.mean(scaled * normed, axis=-1, keepdims=True)
    return (inverse * (scaled - normed * row_inner), jnp.sum(upstream * normed, axis=0))


def project(pattern, left_side, right_side):
    return jnp.einsum(pattern, left_side, right_side, preferred_element_type=jnp.float32)


def split_heads(qkv_frames):
    frames = qkv_frames.shape[0]
    length = qkv_frames.shape[1]
    pieces = qkv_frames.reshape(frames, length, 3, HEADS, HEAD)
    return (pieces[:, :, 0], pieces[:, :, 1], pieces[:, :, 2])


def masked_scores(query, key_part):
    raw_scores = project("fqhe,fkhe->fhqk", query, key_part) * HEAD ** (-0.5)
    length = raw_scores.shape[-1]
    allowed = lax.broadcasted_iota(jnp.int32, (length, length), 0) >= lax.broadcasted_iota(
        jnp.int32, (length, length), 1
    )
    return jnp.where(allowed, raw_scores, NEGATIVE)


def gathered_plan(
    frames_in,
    frame_valid,
    last_position,
    weight_qkv,
    weight_out,
    weight_ffn,
    weight_down,
    gain_attn,
    gain_ffn,
    grad_out,
):
    scale = HEAD ** (-0.5)
    slot_index = lax.broadcasted_iota(jnp.int32, (frames_in.shape[0], frames_in.shape[1]), 1)
    live_mask = (frame_valid[:, None] > 0) & (slot_index <= last_position[:, None])
    pos_rows = lax.all_to_all(frames_in, "pos", split_axis=1, concat_axis=0, tiled=True)
    full_qkv, full_out, full_gain_a = (
        lax.all_gather(weight_qkv, "frames", axis=1, tiled=True),
        lax.all_gather(weight_out, "frames", axis=1, tiled=True),
        lax.all_gather(gain_attn, "frames", axis=1, tiled=True),
    )
    gain_one = full_gain_a.astype(jnp.float32)
    residual = pos_rows.astype(jnp.float32)
    scaled_one, normed_one, inverse_one = rms_forward(residual, gain_one)
    normed_one_low = scaled_one.astype(jnp.bfloat16)
    qkv_rows = project("rpd,pde->rpe", normed_one_low, full_qkv).astype(jnp.bfloat16)
    qkv_frames = lax.all_to_all(qkv_rows, "pos", split_axis=0, concat_axis=1, tiled=True)
    query, key_part, value_part = split_heads(qkv_frames)
    scores = masked_scores(query, key_part)
    row_top = jnp.max(scores, axis=-1, keepdims=True)
    exponent = jnp.exp(scores - row_top)
    row_total = jnp.sum(exponent, axis=-1, keepdims=True)
    log_total = row_top + jnp.log(row_total)
    attend_low = (exponent / row_total).astype(jnp.bfloat16)
    mixed_heads = project("fhqk,fkhe->fqhe", attend_low, value_part)
    mixed_low = mixed_heads.reshape(frames_in.shape).astype(jnp.bfloat16)
    mixed_rows = lax.all_to_all(mixed_low, "pos", split_axis=1, concat_axis=0, tiled=True)
    middle = residual + project("rpd,pde->rpe", mixed_rows, full_out)
    full_ffn, full_down, full_gain_f = (
        lax.all_gather(weight_ffn, "frames", axis=1, tiled=True),
        lax.all_gather(weight_down, "frames", axis=1, tiled=True),
        lax.all_gather(gain_ffn, "frames", axis=1, tiled=True),
    )
    gain_two = full_gain_f.astype(jnp.float32)
    scaled_two, normed_two, inverse_two = rms_forward(middle, gain_two)
    normed_two_low = scaled_two.astype(jnp.bfloat16)
    gate_up = project("rpd,pde->rpe", normed_two_low, full_ffn)
    width = gate_up.shape[-1] // 2
    gate = gate_up[..., :width]
    upward = gate_up[..., width:]
    gate_sig = jax.nn.sigmoid(gate)
    hidden = (gate * gate_sig * upward).astype(jnp.bfloat16)
    result = middle + project("rpf,pfd->rpd", hidden, full_down)
    result_frames = lax.all_to_all(
        result.astype(jnp.bfloat16), "pos", split_axis=0, concat_axis=1, tiled=True
    )
    output = jnp.where(live_mask[:, :, None], result_frames, jnp.zeros_like(result_frames))
    upstream = jnp.where(live_mask[:, :, None], grad_out, jnp.zeros_like(grad_out))
    upstream_rows = lax.all_to_all(upstream, "pos", split_axis=1, concat_axis=0, tiled=True)
    back_ffn, back_down = (
        lax.all_gather(weight_ffn, "frames", axis=1, tiled=True),
        lax.all_gather(weight_down, "frames", axis=1, tiled=True),
    )
    grad_hidden = project("rpd,pfd->rpf", upstream_rows, back_down)
    term_down = project("rpf,rpd->pfd", hidden, upstream_rows)
    grad_upward = grad_hidden * gate * gate_sig
    grad_gate = grad_hidden * upward * gate_sig * (1.0 + gate * (1.0 - gate_sig))
    grad_gate_up = jnp.concatenate([grad_gate, grad_upward], axis=-1).astype(jnp.bfloat16)
    grad_normed_two = project("rpe,pde->rpd", grad_gate_up, back_ffn)
    term_ffn = project("rpd,rpe->pde", normed_two_low, grad_gate_up)
    grad_middle_norm, term_gain_f = rms_backward(grad_normed_two, normed_two, inverse_two, gain_two)
    grad_middle = upstream_rows.astype(jnp.float32) + grad_middle_norm
    sum_ffn, sum_down, sum_gain_f = (
        lax.psum_scatter(
            term_ffn.astype(jnp.bfloat16), "frames", scatter_dimension=1, tiled=True
        ).astype(jnp.float32),
        lax.psum_scatter(
            term_down.astype(jnp.bfloat16), "frames", scatter_dimension=1, tiled=True
        ).astype(jnp.float32),
        lax.psum_scatter(
            term_gain_f.astype(jnp.bfloat16), "frames", scatter_dimension=1, tiled=True
        ).astype(jnp.float32),
    )
    back_qkv, back_out = (
        lax.all_gather(weight_qkv, "frames", axis=1, tiled=True),
        lax.all_gather(weight_out, "frames", axis=1, tiled=True),
    )
    grad_branch = grad_middle.astype(jnp.bfloat16)
    grad_mixed = project("rpe,pde->rpd", grad_branch, back_out).astype(jnp.bfloat16)
    term_out = project("rpd,rpe->pde", mixed_rows, grad_branch)
    grad_mixed_frames = lax.all_to_all(grad_mixed, "pos", split_axis=0, concat_axis=1, tiled=True)
    grad_heads = grad_mixed_frames.reshape(query.shape)
    again_scores = masked_scores(query, key_part)
    attend = jnp.exp(again_scores - log_total)
    grad_value = project("fhqk,fqhe->fkhe", attend.astype(jnp.bfloat16), grad_heads)
    grad_attend = project("fqhe,fkhe->fhqk", grad_heads, value_part)
    row_inner = jnp.sum(attend * grad_attend, axis=-1, keepdims=True)
    grad_scores = (attend * (grad_attend - row_inner)).astype(jnp.bfloat16)
    grad_query = project("fhqk,fkhe->fqhe", grad_scores, key_part) * scale
    grad_key = project("fhqk,fqhe->fkhe", grad_scores, query) * scale
    grad_qkv_frames = (
        jnp.stack([grad_query, grad_key, grad_value], axis=2)
        .reshape(qkv_frames.shape)
        .astype(jnp.bfloat16)
    )
    grad_qkv_rows = lax.all_to_all(grad_qkv_frames, "pos", split_axis=1, concat_axis=0, tiled=True)
    grad_normed_one = project("rpe,pde->rpd", grad_qkv_rows, back_qkv)
    term_qkv = project("rpd,rpe->pde", normed_one_low, grad_qkv_rows)
    grad_input_norm, term_gain_a = rms_backward(grad_normed_one, normed_one, inverse_one, gain_one)
    grad_rows = (grad_middle + grad_input_norm).astype(jnp.bfloat16)
    grad_frames = lax.all_to_all(grad_rows, "pos", split_axis=0, concat_axis=1, tiled=True)
    sum_qkv, sum_out, sum_gain_a = (
        lax.psum_scatter(
            term_qkv.astype(jnp.bfloat16), "frames", scatter_dimension=1, tiled=True
        ).astype(jnp.float32),
        lax.psum_scatter(
            term_out.astype(jnp.bfloat16), "frames", scatter_dimension=1, tiled=True
        ).astype(jnp.float32),
        lax.psum_scatter(
            term_gain_a.astype(jnp.bfloat16), "frames", scatter_dimension=1, tiled=True
        ).astype(jnp.float32),
    )
    return (output, grad_frames, sum_qkv, sum_out, sum_ffn, sum_down, sum_gain_a, sum_gain_f)


ROWS = ("pos", "spot")
PLANE = ("spot", "half")


def plain(left, right):
    return lax.dot_general(left, right, (((1,), (0,)), ((), ())), preferred_element_type=jnp.float32)


def by_columns(left, right):
    return lax.dot_general(left, right, (((1,), (1,)), ((), ())), preferred_element_type=jnp.float32)


def over_rows(left, right):
    return lax.dot_general(left, right, (((0,), (0,)), ((), ())), preferred_element_type=jnp.float32)


def tie(*values):
    return lax.optimization_barrier(values)


def pick(stack, index):
    return lax.dynamic_index_in_dim(stack, index, 0, keepdims=False)


def hop(value, k, spots):
    return value if k == 0 else lax.ppermute(value, "spot", [(i, i ^ k) for i in range(spots)])


def trade(value):
    return lax.ppermute(value, "half", [(0, 1), (1, 0)])


def swap(values, blocks):
    return lax.all_to_all(
        values.reshape(blocks, -1, values.shape[-1]), ROWS, split_axis=0, concat_axis=0, tiled=True
    )


def rows_from_spots(values, blocks):
    return swap(values, blocks).swapaxes(0, 1)


def head_runs(width, groups, spots):
    size = width // groups // spots // 2
    return [((g * spots + a) * 2 * size, ((g * spots + a) * 2 + 1) * size) for g in range(groups) for a in range(spots)], size


def unit_runs(width, groups):
    size = width // groups // 2
    return [(g * 2 * size, (g * 2 + 1) * size) for g in range(groups)], size


def call(kernel, name, grid, inputs, outputs, scalars, scratch=()):
    moved = sum(a.size * a.dtype.itemsize for a, _, _ in inputs)
    return pl.pallas_call(
        kernel,
        grid_spec=pltpu.PrefetchScalarGridSpec(
            num_scalar_prefetch=1,
            grid=grid,
            in_specs=[pl.BlockSpec(block, where) for _, block, where in inputs],
            out_specs=[pl.BlockSpec(block, where) for _, _, block, where in outputs],
            scratch_shapes=list(scratch),
        ),
        out_shape=[jax.ShapeDtypeStruct(shape, dtype) for shape, dtype, _, _ in outputs],
        compiler_params=pltpu.CompilerParams(vmem_limit_bytes=48 << 20),
        cost_estimate=pl.CostEstimate(flops=0, transcendentals=0, bytes_accessed=moved // 8),
        name=name,
    )(scalars, *[a for a, _, _ in inputs])


def aligned(start, size):
    return pl.ds(pl.multiple_of(start, LANES), size)


def collect_kernel(widths, scalars, *refs):
    parts, outs = refs[: len(widths)], refs[len(widths) :]
    for k, out in enumerate(outs):

        @pl.when(pl.program_id(0) == k)
        def _():
            start = 0
            for part, width in zip(parts, widths):
                out[:, start : start + width] = part[0]
                start += width


def collect(parts, widths, scalars):
    count, rows = scalars.shape[0] - 1, parts[0].shape[1]
    cuts = 2
    step, width = rows // cuts, sum(widths)

    def spec(k):
        return lambda j, r, s: (jnp.where(j == k, r, jnp.where(j < k, 0, cuts - 1)), 0)

    return call(
        functools.partial(collect_kernel, widths),
        "collect",
        (count, cuts),
        [(a, (1, step, n), lambda j, r, s: (s[1 + j], r, 0)) for a, n in zip(parts, widths)],
        [((rows, width), parts[0].dtype, (step, width), spec(k)) for k in range(count)],
        scalars,
    )


def split_kernel(runs, count, per, whose, rests, scalars, *refs):
    starts, size = runs
    pieces, outs = refs[: count * per], refs[count * per :]
    half = scalars[0]
    for k in range(count):
        at = scalars[1 + k]
        for i, pair in enumerate(starts):
            piece = pieces[k * per + (i if per > 1 else 0)]
            for out, other in zip(outs, whose):
                first, second = pair[::-1] if other else pair
                columns = aligned(first + half * (second - first), size)
                out[pl.ds(at, 1), :, i * size : (i + 1) * size] = piece[:, columns][None]
        for out, (start, width) in zip(outs[len(whose) :], rests):
            out[pl.ds(at, 1)] = pieces[k][:, start : start + width][None]


def split_columns(pieces, runs, scalars, whose=(False, True), width=None, rests=()):
    starts, size = runs
    per = len(pieces[0])
    rows = pieces[0][0].shape[0]
    count, step = len(pieces), rows // 2
    widths = [len(starts) * size] * len(whose) + [n for _, n in rests]
    outs = call(
        functools.partial(split_kernel, runs, count, per, whose, rests),
        "split_columns",
        (2,),
        [
            (a, (step, width or a.shape[1]), lambda r, s: (r, 0))
            for piece in pieces
            for a in piece
        ],
        [
            ((count, rows, n), pieces[0][0].dtype, (count, step, n), lambda r, s: (0, r, 0))
            for n in widths
        ],
        scalars,
    )
    return [out.reshape(count * rows, -1) for out in outs]


def place_kernel(runs, parts, skip, count, weighted, scalars, *refs):
    pieces, out = refs[: count * parts], refs[count * parts + weighted]
    half = scalars[0]
    for k in range(count):

        @pl.when(pl.program_id(0) == k)
        def _():
            for p in range(parts):
                ref = pieces[k * parts + p]
                if runs is None:
                    out[0] = ref[:, skip:].astype(out.dtype)
                    continue
                starts, size = runs
                for i, pair in enumerate(starts):
                    first, second = pair[::-1] if p else pair
                    columns = aligned(first + half * (second - first), size)
                    out[0, :, columns] = ref[:, i * size : (i + 1) * size].astype(out.dtype)

    if weighted:
        products = out[0] * refs[count * parts][0].astype(jnp.float32)
        refs[-1][0] = jnp.sum(products, axis=-1, keepdims=True)


def place(pieces, scalars, rows, width, runs=None, skip=0, dtype=jnp.float32, weight=None):
    count, parts = len(pieces), len(pieces[0])
    cuts = 2 if rows * width > (1 << 19) else 1
    step = rows // cuts

    def spec(k, first):
        base = first // step
        return lambda j, r, s: (base + jnp.where(j == k, r, jnp.where(j < k, 0, cuts - 1)), 0)

    entry = lambda j, r, s: (s[1 + j], r, 0)
    inputs = [
        (a, (step, a.shape[1]), spec(k, first))
        for k, piece in enumerate(pieces)
        for a, first in piece
    ]
    outputs = [((count, rows, width), dtype, (1, step, width), entry)]
    if weight is not None:
        inputs.append((weight, (1, step, width), entry))
        outputs.append(((count, rows, 1), jnp.float32, (1, step, 1), entry))
    outs = call(
        functools.partial(place_kernel, runs, parts, skip, count, int(weight is not None)),
        "place",
        (count, cuts),
        inputs,
        outputs,
        scalars,
    )
    return outs[0] if weight is None else outs


def halves_rows(step, own):
    count = own.shape[0] // step
    return (
        lambda r, *s: (jnp.minimum(r, count - 1), 0),
        lambda r, *s: (jnp.maximum(r - count, 0), 0),
    )


def unit_of(values):
    inverse = lax.rsqrt(jnp.mean(values * values, axis=-1, keepdims=True) + EPSILON)
    return values * inverse, inverse


def spread(values, scratch, half, own, other):
    scratch[...] = values.astype(scratch.dtype)
    for a in range(own.shape[1] // LANES):
        own[:, a * LANES : (a + 1) * LANES] = scratch[:, aligned((2 * a + half) * LANES, LANES)]
        other[:, a * LANES : (a + 1) * LANES] = scratch[:, aligned((2 * a + 1 - half) * LANES, LANES)]


def gather(own, other, scratch, half):
    for a in range(own[0].shape[1] // LANES):
        block = slice(a * LANES, (a + 1) * LANES)
        scratch[:, aligned((2 * a + half) * LANES, LANES)] = own[0][:, block] + own[1][:, block]
        scratch[:, aligned((2 * a + 1 - half) * LANES, LANES)] = other[0][:, block] + other[1][:, block]
    return scratch[...]


def either(own_ref, got_ref):
    mine = pl.program_id(0) < pl.num_programs(0) // 2
    return jnp.where(mine, own_ref[...].astype(jnp.float32), got_ref[...].astype(jnp.float32))


def norm_kernel(scalars, own_rows, got_rows, gain, own, other, scratch):
    unit, _ = unit_of(either(own_rows, got_rows))
    spread(unit * gain[...], scratch, scalars[0], own, other)


def middle_kernel(scalars, own_rows, got_rows, branch, got_branch, gain, middle, own, other, scratch):
    values = either(own_rows, got_rows) + (branch[...] + got_branch[...])
    middle[...] = values
    unit, _ = unit_of(values)
    spread(unit * gain[...], scratch, scalars[0], own, other)


def pull(values, upstream, gain):
    unit, inverse = unit_of(values)
    scaled = upstream * gain
    inner = jnp.mean(scaled * unit, axis=-1, keepdims=True)
    return inverse * (scaled - unit * inner)


def middle_back_kernel(
    scalars, middle, own, other, got_own, got_other, own_up, got_up, gain, whole, low, scratch
):
    upstream = gather((own, got_other), (other, got_own), scratch, scalars[0])
    grad = pull(middle[...], upstream, gain[...]) + either(own_up, got_up)
    whole[...] = grad
    low[...] = grad.astype(low.dtype)


def input_back_kernel(
    scalars, rows, own, other, got_own, got_other, grad_middle, gain, out, scratch
):
    upstream = gather((own, got_other), (other, got_own), scratch, scalars[0])
    grad = pull(rows[...].astype(jnp.float32), upstream, gain[...])
    out[...] = (grad_middle[...] + grad).astype(out.dtype)


def softmax_of(query, keys, allowed):
    scores = jnp.where(allowed, by_columns(query, keys) * HEAD ** (-0.5), NEGATIVE)
    exponent = jnp.exp(scores - jnp.max(scores, axis=-1, keepdims=True))
    return exponent / jnp.sum(exponent, axis=-1, keepdims=True)


def frame_mask(positions, frames):
    count = positions * frames
    row = lax.broadcasted_iota(jnp.int32, (count, count), 0)
    column = lax.broadcasted_iota(jnp.int32, (count, count), 1)
    return (row % frames == column % frames) & (row >= column)


def attend_kernel(qkv_ref, mixed_ref):
    positions, frames, width = qkv_ref.shape
    count, third = positions * frames, width // 3
    allowed = frame_mask(positions, frames)
    lane = lax.broadcasted_iota(jnp.int32, (count, LANES), 1)
    for first in range(0, third, LANES):
        query, keys, values = (
            qkv_ref[:, :, part * third + first : part * third + first + LANES].reshape(count, LANES)
            for part in range(3)
        )
        mixed = jnp.zeros((count, LANES), jnp.float32)
        for start in range(0, LANES, HEAD):
            inside = (lane >= start) & (lane < start + HEAD)
            probs = softmax_of(jnp.where(inside, query, jnp.zeros_like(query)), keys, allowed)
            mixed = jnp.where(inside, plain(probs.astype(jnp.bfloat16), values), mixed)
        mixed_ref[:, :, first : first + LANES] = mixed.astype(mixed_ref.dtype).reshape(
            positions, frames, LANES
        )


def attend_back_kernel(qkv_ref, grad_ref, out_ref):
    positions, frames, width = qkv_ref.shape
    count, third = positions * frames, width // 3
    scale = HEAD ** (-0.5)
    allowed = frame_mask(positions, frames)
    lane = lax.broadcasted_iota(jnp.int32, (count, LANES), 1)
    for first in range(0, third, LANES):
        query, keys, values = (
            qkv_ref[:, :, part * third + first : part * third + first + LANES].reshape(count, LANES)
            for part in range(3)
        )
        upstream = grad_ref[:, :, first : first + LANES].reshape(count, LANES)
        grads = [jnp.zeros((count, LANES), jnp.float32)] * 3
        for start in range(0, LANES, HEAD):
            inside = (lane >= start) & (lane < start + HEAD)
            probs = softmax_of(jnp.where(inside, query, jnp.zeros_like(query)), keys, allowed)
            grad_probs = by_columns(jnp.where(inside, upstream, jnp.zeros_like(upstream)), values)
            inner = jnp.sum(probs * grad_probs, axis=-1, keepdims=True)
            grad_scores = (probs * (grad_probs - inner)).astype(jnp.bfloat16)
            new = (
                plain(grad_scores, keys) * scale,
                over_rows(grad_scores, query) * scale,
                over_rows(probs.astype(jnp.bfloat16), upstream),
            )
            grads = [jnp.where(inside, value, old) for value, old in zip(new, grads)]
        for part, grad in enumerate(grads):
            out_ref[:, :, part * third + first : part * third + first + LANES] = grad.astype(
                out_ref.dtype
            ).reshape(positions, frames, LANES)


def over_frames(kernel, out_width, *arrays):
    positions, frames, width = arrays[0].shape
    step = min(frames, 256 // positions)
    heads = width // 3 // HEAD
    work = frames // step * heads * (step * positions) ** 2
    return pl.pallas_call(
        kernel,
        grid=(frames // step,),
        in_specs=[
            pl.BlockSpec((positions, step, a.shape[2]), lambda i: (0, i, 0)) for a in arrays
        ],
        out_specs=pl.BlockSpec((positions, step, out_width), lambda i: (0, i, 0)),
        out_shape=jax.ShapeDtypeStruct((positions, frames, out_width), arrays[0].dtype),
        compiler_params=pltpu.CompilerParams(vmem_limit_bytes=48 << 20),
        cost_estimate=pl.CostEstimate(
            flops=4 * LANES * work,
            transcendentals=work,
            bytes_accessed=2 * positions * frames * (width + out_width),
        ),
        name=kernel.__name__,
    )(*arrays)


def spots_plan(
    frames_in,
    frame_valid,
    last_position,
    weight_qkv,
    weight_out,
    weight_ffn,
    weight_down,
    gain_attn,
    gain_ffn,
    grad_out,
):
    f32, bf16 = jnp.float32, jnp.bfloat16
    frames, positions, depth = frames_in.shape
    spots, slice_rows = weight_qkv.shape[:2]
    plane, near = spots * 2, spots - 1
    spot, half = lax.axis_index("spot"), lax.axis_index("half")
    heads = head_runs(3 * depth, 3, spots)
    units = unit_runs(weight_ffn.shape[2], 2)
    hidden_units = weight_ffn.shape[2] // 2
    down_index = lax.axis_index(PLANE) % spots
    down_pairs = [
        [(f, (f % spots ^ k) * 2 + f // spots) for f in range(plane)] for k in range(spots)
    ]
    early = spots // 2
    by_spot = jnp.stack([half] + [spot ^ k for k in range(spots)]).astype(jnp.int32)
    by_slice = jnp.stack([half] + [down_index ^ k for k in range(spots)]).astype(jnp.int32)
    slot = lax.broadcasted_iota(jnp.int32, (frames, positions), 1)
    live = ((frame_valid[:, None] > 0) & (slot <= last_position[:, None]))[:, :, None]

    gains = jnp.pad(jnp.stack([gain_attn, gain_ffn], axis=2), ((0, 0), (0, 0), (0, LANES - 2)))
    parts = (weight_qkv, weight_out, gains, weight_ffn)
    widths = (3 * depth, depth, LANES, hidden_units)
    first = collect(parts, widths, jnp.concatenate([by_spot[:1], by_spot[2:]]))
    first = list(collect(parts, widths, by_spot[:2])) + [hop(p, k + 1, spots) for k, p in enumerate(first)]
    upstream = jnp.where(live, grad_out, jnp.zeros_like(grad_out))
    rows_in = jnp.concatenate([frames_in.swapaxes(0, 1), upstream.swapaxes(0, 1)], axis=1)
    own_rows = swap(rows_in, positions)
    ups = [pick(weight_ffn, spot ^ k)[:, hidden_units:] for k in range(spots)]
    third = [pick(weight_down, down_index ^ k) for k in range(spots)]
    tied = tie(*first, *ups, *third)
    first, ups, third = tied[:spots], tied[spots : 2 * spots], tied[2 * spots :]
    ups = [hop(piece, k, spots) for k, piece in enumerate(ups)]
    own_rows, own_up = (
        own_rows[:, part * frames : (part + 1) * frames].reshape(-1, depth) for part in range(2)
    )
    got_rows, got_up = trade(own_rows), trade(own_up)

    own_count = own_rows.shape[0]
    count = own_count * 2
    step = own_count // 2
    pieces = [[piece] for piece in first]
    (qkv_sent,) = split_columns(pieces, heads, by_spot, (True,), 3 * depth)
    qkv_other = trade(qkv_sent)
    whole = 4 * depth + LANES
    qkv_own, full_out, gains = split_columns(
        pieces, heads, by_spot, (False,), whole, ((3 * depth, depth), (4 * depth, LANES))
    )
    gains = gains[:, :2]
    pair = [part.reshape(spots, slice_rows, 2) for part in (gains, trade(gains))]
    even, odd = (jnp.where(half == h, *pair) for h in range(2))
    gains = jnp.stack([even, odd], axis=1).reshape(depth, 2).T.astype(f32)
    gain_one, gain_two = gains[:1], gains[1:]
    mine, theirs = halves_rows(step, own_rows)
    straight = lambda r, *s: (r, 0)
    crossed = lambda r, *s: ((r + 2) % 4, 0)
    top = lambda r, *s: (0, 0)
    lower = lambda blocks, where: lambda *r: (where(*r)[0] + blocks, 0)
    rows = [(own_rows, (step, depth), mine), (got_rows, (step, depth), theirs)]
    split_rows = [((count, depth // 2), bf16, (step, depth // 2), straight)] * 2
    low_scratch, scratch = pltpu.VMEM((step, depth), bf16), pltpu.VMEM((step, depth), f32)
    one_own, one_other = call(
        norm_kernel, "norm", (4,), rows + [(gain_one, (1, depth), top)], split_rows, by_spot, [low_scratch]
    )
    qkv_rows = (plain(one_own, qkv_own) + plain(one_other, qkv_other)).astype(bf16)
    qkv_rows, *ups[:near] = tie(qkv_rows, *ups[:near])
    qkv = swap(qkv_rows, positions)
    mixed = over_frames(attend_kernel, depth // 2, qkv)
    third = [lax.ppermute(p, PLANE, down_pairs[k]) for k, p in enumerate(third)]
    mixed, *third[:early] = tie(mixed, *third[:early])
    mixed = swap(mixed, positions).reshape(count, -1)
    branch = plain(mixed, full_out)
    got_branch = trade(branch)
    middle, two_own, two_other = call(
        middle_kernel,
        "middle",
        (4,),
        rows
        + [(branch, (step, depth), straight), (got_branch, (step, depth), crossed)]
        + [(gain_two, (1, depth), top)],
        [((count, depth), f32, (step, depth), straight)] + split_rows,
        by_spot,
        [low_scratch],
    )

    gate_run = tuple(start + whole for start in units[0][0])
    up_run = tuple(start - hidden_units for start in units[0][1])
    ffn_own, ffn_sent = split_columns(
        list(zip(first, ups)), ([gate_run, up_run], units[1]), by_spot
    )
    ffn_other = trade(ffn_sent)
    gate_up = plain(two_own, ffn_own) + plain(two_other, ffn_other)
    gate_up, *third[early:] = tie(gate_up, *third[early:])
    width = gate_up.shape[1] // 2
    gate, upward = gate_up[:, :width], gate_up[:, width:]
    gate_sig = jax.nn.sigmoid(gate)
    hidden = (gate * gate_sig * upward).astype(bf16)
    upstream = jnp.concatenate([own_up, got_up])
    down_grad = over_rows(hidden, upstream).astype(bf16).reshape(spots, -1, depth)
    down_sent = [pick(down_grad, spot ^ k) for k in range(spots)]
    down_back = [[(b, a) for a, b in pairs] for pairs in down_pairs]
    down_sent = [lax.ppermute(p, PLANE, pairs) for p, pairs in zip(down_sent, down_back)]
    full_down = place([[(piece, 0)] for piece in third], by_spot, *weight_down.shape[1:], dtype=bf16)
    full_down = full_down.reshape(-1, depth)

    grad_hidden = by_columns(upstream, full_down)
    grad_upward = grad_hidden * gate * gate_sig
    grad_gate = grad_hidden * upward * gate_sig * (1.0 + gate * (1.0 - gate_sig))
    grad_gate_up = jnp.concatenate([grad_gate, grad_upward], axis=-1).astype(bf16)
    back = jnp.concatenate([by_columns(grad_gate_up, ffn_own), by_columns(grad_gate_up, ffn_other)])
    back, *down_sent[::2] = tie(back, *down_sent[::2])
    got_back, grad_gate_up = tie(trade(back), grad_gate_up)
    wide, narrow = (step, depth), (step, depth // 2)
    grad_middle, grad_branch = call(
        middle_back_kernel,
        "middle_back",
        (4,),
        [(middle, wide, straight), (back, narrow, straight), (back, narrow, lower(4, straight))]
        + [(got_back, narrow, crossed), (got_back, narrow, lower(4, crossed))]
        + [(own_up, wide, mine), (got_up, wide, theirs), (gain_two, (1, depth), top)],
        [
            ((count, depth), f32, wide, straight),
            ((count, depth), bf16, wide, straight),
        ],
        by_spot,
        [scratch],
    )

    cut = lambda grad: [pick(grad.reshape(spots, slice_rows, -1), spot ^ k) for k in range(spots)]
    grad_mixed = by_columns(grad_branch, full_out).astype(bf16)
    grad_mixed, *down_sent = tie(grad_mixed, *down_sent)
    grad_mixed_frames = swap(grad_mixed, positions)
    ffn_grad_own = cut(over_rows(two_own, grad_gate_up).astype(bf16))
    ffn_grad_got = cut(trade(over_rows(two_other, grad_gate_up).astype(bf16)))
    ffn_grad_own = [hop(piece, k, spots) for k, piece in enumerate(ffn_grad_own)]
    grad_qkv = over_frames(attend_back_kernel, 3 * depth // 2, qkv, grad_mixed_frames)
    late = [
        jnp.concatenate(pair, axis=1)
        for pair in zip(ffn_grad_got, cut(over_rows(mixed, grad_branch).astype(bf16)))
    ]
    grad_qkv, *ffn_grad_own[:near] = tie(grad_qkv, *ffn_grad_own[:near])
    late = [hop(piece, k, spots) for k, piece in enumerate(late)]
    result = plain(hidden, full_down)
    result = (middle[:own_count] + result[:own_count] + trade(result[own_count:])).astype(bf16)
    sum_down = place([[(piece, 0)] for piece in down_sent], by_slice, *weight_down.shape[1:])
    grad_qkv_rows = swap(grad_qkv, positions).reshape(count, -1)
    grad_qkv_rows, result, sum_down, ffn_grad_own[near], *late[:near] = tie(
        grad_qkv_rows, result, sum_down, ffn_grad_own[near], *late[:near]
    )
    result = rows_from_spots(result, positions)
    qkv_grad_got = trade(over_rows(one_other, grad_qkv_rows).astype(bf16))
    qkv_grad_own = over_rows(one_own, grad_qkv_rows).astype(bf16)
    qkv_sent = [jnp.concatenate(pair) for pair in zip(cut(qkv_grad_own), cut(qkv_grad_got))]
    *qkv_sent, grad_qkv_rows = tie(*qkv_sent, grad_qkv_rows)
    qkv_sent = [hop(piece, k, spots) for k, piece in enumerate(qkv_sent)]
    back_own = by_columns(grad_qkv_rows, qkv_own)
    back_other = by_columns(grad_qkv_rows, qkv_other)
    back_own, back_other, result, late[near], *qkv_sent[:near] = tie(
        back_own, back_other, result, late[near], *qkv_sent[:near]
    )
    got_back = trade(jnp.concatenate([back_own[own_count:], back_other[own_count:]]))
    (grad_rows,) = call(
        input_back_kernel,
        "input_back",
        (2,),
        [(own_rows, wide, straight), (back_own, narrow, straight), (back_other, narrow, straight)]
        + [(got_back, narrow, straight), (got_back, narrow, lower(2, straight))]
        + [(grad_middle, wide, straight), (gain_one, (1, depth), top)],
        [((own_count, depth), bf16, wide, straight)],
        by_spot,
        [scratch],
    )
    grad_input = rows_from_spots(grad_rows, positions)
    output = jnp.where(live, result, jnp.zeros_like(result))

    sum_ffn, term_ffn = place(
        [[(own, 0), (got, 0)] for own, got in zip(ffn_grad_own, late)],
        by_spot,
        slice_rows,
        2 * hidden_units,
        units,
        weight=weight_ffn,
    )
    sum_out = place([[(piece, 0)] for piece in late], by_spot, slice_rows, depth, skip=hidden_units)
    qkv_sent[near], sum_ffn, sum_out = tie(qkv_sent[near], sum_ffn, sum_out)
    sum_qkv, term_attn = place(
        [[(piece, 0), (piece, slice_rows)] for piece in qkv_sent],
        by_spot,
        slice_rows,
        3 * depth,
        heads,
        weight=weight_qkv,
    )
    gain_terms = [
        term.reshape(spots, slice_rows) / gain.astype(f32)
        for term, gain in ((term_attn, gain_attn), (term_ffn, gain_ffn))
    ]
    return (output, grad_input, sum_qkv, sum_out, sum_ffn, sum_down, *gain_terms)


def solution(mesh):
    plane, lines = mesh.shape["frames"], mesh.shape["pos"]

    def run(*arrays):
        positions, depth = arrays[0].shape[1:]
        spots = positions // lines
        slice_rows = depth // plane
        shares = arrays[5].shape[2] // 4
        fits = plane == 2 * spots and spots & (spots - 1) == 0
        fits = fits and slice_rows % LANES == 0 and shares % LANES == 0
        if fits:
            inner = Mesh(mesh.devices.reshape(spots, 2, lines), PLANE + ("pos",))
            by_frame, weight, plan = P(PLANE + ("pos",)), P("pos", PLANE), spots_plan
        else:
            inner, plan = mesh, gathered_plan
            by_frame, weight = P(("frames", "pos")), P("pos", "frames")
        return jax.shard_map(
            plan,
            mesh=inner,
            in_specs=(by_frame,) * 3 + (weight,) * 6 + (by_frame,),
            out_specs=(by_frame,) * 2 + (weight,) * 6,
            check_vma=False,
        )(*arrays)

    return run
```

```python
import functools

import jax
import jax.numpy as jnp
from jax import lax
from jax.experimental import pallas as pl
from jax.experimental.pallas import tpu as pltpu
from jax.sharding import Mesh, PartitionSpec as P

HEADS = 16
HEAD = 64
LANES = 128
EPSILON = 1e-06
NEGATIVE = -1e30


def rms_forward(values, gain_row):
    inverse = lax.rsqrt(jnp.mean(values * values, axis=-1, keepdims=True) + EPSILON)
    normed = values * inverse
    return (normed * gain_row[None], normed, inverse)


def rms_backward(upstream, normed, inverse, gain_row):
    scaled = upstream * gain_row[None]
    row_inner = jnp.mean(scaled * normed, axis=-1, keepdims=True)
    return (inverse * (scaled - normed * row_inner), jnp.sum(upstream * normed, axis=0))


def project(pattern, left_side, right_side):
    return jnp.einsum(pattern, left_side, right_side, preferred_element_type=jnp.float32)


def split_heads(qkv_frames):
    frames = qkv_frames.shape[0]
    length = qkv_frames.shape[1]
    pieces = qkv_frames.reshape(frames, length, 3, HEADS, HEAD)
    return (pieces[:, :, 0], pieces[:, :, 1], pieces[:, :, 2])


def masked_scores(query, key_part):
    raw_scores = project("fqhe,fkhe->fhqk", query, key_part) * HEAD ** (-0.5)
    length = raw_scores.shape[-1]
    allowed = lax.broadcasted_iota(jnp.int32, (length, length), 0) >= lax.broadcasted_iota(
        jnp.int32, (length, length), 1
    )
    return jnp.where(allowed, raw_scores, NEGATIVE)


def gathered_plan(
    frames_in,
    frame_valid,
    last_position,
    weight_qkv,
    weight_out,
    weight_ffn,
    weight_down,
    gain_attn,
    gain_ffn,
    grad_out,
):
    scale = HEAD ** (-0.5)
    slot_index = lax.broadcasted_iota(jnp.int32, (frames_in.shape[0], frames_in.shape[1]), 1)
    live_mask = (frame_valid[:, None] > 0) & (slot_index <= last_position[:, None])
    pos_rows = lax.all_to_all(frames_in, "pos", split_axis=1, concat_axis=0, tiled=True)
    full_qkv, full_out, full_gain_a = (
        lax.all_gather(weight_qkv, "frames", axis=1, tiled=True),
        lax.all_gather(weight_out, "frames", axis=1, tiled=True),
        lax.all_gather(gain_attn, "frames", axis=1, tiled=True),
    )
    gain_one = full_gain_a.astype(jnp.float32)
    residual = pos_rows.astype(jnp.float32)
    scaled_one, normed_one, inverse_one = rms_forward(residual, gain_one)
    normed_one_low = scaled_one.astype(jnp.bfloat16)
    qkv_rows = project("rpd,pde->rpe", normed_one_low, full_qkv).astype(jnp.bfloat16)
    qkv_frames = lax.all_to_all(qkv_rows, "pos", split_axis=0, concat_axis=1, tiled=True)
    query, key_part, value_part = split_heads(qkv_frames)
    scores = masked_scores(query, key_part)
    row_top = jnp.max(scores, axis=-1, keepdims=True)
    exponent = jnp.exp(scores - row_top)
    row_total = jnp.sum(exponent, axis=-1, keepdims=True)
    log_total = row_top + jnp.log(row_total)
    attend_low = (exponent / row_total).astype(jnp.bfloat16)
    mixed_heads = project("fhqk,fkhe->fqhe", attend_low, value_part)
    mixed_low = mixed_heads.reshape(frames_in.shape).astype(jnp.bfloat16)
    mixed_rows = lax.all_to_all(mixed_low, "pos", split_axis=1, concat_axis=0, tiled=True)
    middle = residual + project("rpd,pde->rpe", mixed_rows, full_out)
    full_ffn, full_down, full_gain_f = (
        lax.all_gather(weight_ffn, "frames", axis=1, tiled=True),
        lax.all_gather(weight_down, "frames", axis=1, tiled=True),
        lax.all_gather(gain_ffn, "frames", axis=1, tiled=True),
    )
    gain_two = full_gain_f.astype(jnp.float32)
    scaled_two, normed_two, inverse_two = rms_forward(middle, gain_two)
    normed_two_low = scaled_two.astype(jnp.bfloat16)
    gate_up = project("rpd,pde->rpe", normed_two_low, full_ffn)
    width = gate_up.shape[-1] // 2
    gate = gate_up[..., :width]
    upward = gate_up[..., width:]
    gate_sig = jax.nn.sigmoid(gate)
    hidden = (gate * gate_sig * upward).astype(jnp.bfloat16)
    result = middle + project("rpf,pfd->rpd", hidden, full_down)
    result_frames = lax.all_to_all(
        result.astype(jnp.bfloat16), "pos", split_axis=0, concat_axis=1, tiled=True
    )
    output = jnp.where(live_mask[:, :, None], result_frames, jnp.zeros_like(result_frames))
    upstream = jnp.where(live_mask[:, :, None], grad_out, jnp.zeros_like(grad_out))
    upstream_rows = lax.all_to_all(upstream, "pos", split_axis=1, concat_axis=0, tiled=True)
    back_ffn, back_down = (
        lax.all_gather(weight_ffn, "frames", axis=1, tiled=True),
        lax.all_gather(weight_down, "frames", axis=1, tiled=True),
    )
    grad_hidden = project("rpd,pfd->rpf", upstream_rows, back_down)
    term_down = project("rpf,rpd->pfd", hidden, upstream_rows)
    grad_upward = grad_hidden * gate * gate_sig
    grad_gate = grad_hidden * upward * gate_sig * (1.0 + gate * (1.0 - gate_sig))
    grad_gate_up = jnp.concatenate([grad_gate, grad_upward], axis=-1).astype(jnp.bfloat16)
    grad_normed_two = project("rpe,pde->rpd", grad_gate_up, back_ffn)
    term_ffn = project("rpd,rpe->pde", normed_two_low, grad_gate_up)
    grad_middle_norm, term_gain_f = rms_backward(grad_normed_two, normed_two, inverse_two, gain_two)
    grad_middle = upstream_rows.astype(jnp.float32) + grad_middle_norm
    sum_ffn, sum_down, sum_gain_f = (
        lax.psum_scatter(
            term_ffn.astype(jnp.bfloat16), "frames", scatter_dimension=1, tiled=True
        ).astype(jnp.float32),
        lax.psum_scatter(
            term_down.astype(jnp.bfloat16), "frames", scatter_dimension=1, tiled=True
        ).astype(jnp.float32),
        lax.psum_scatter(
            term_gain_f.astype(jnp.bfloat16), "frames", scatter_dimension=1, tiled=True
        ).astype(jnp.float32),
    )
    back_qkv, back_out = (
        lax.all_gather(weight_qkv, "frames", axis=1, tiled=True),
        lax.all_gather(weight_out, "frames", axis=1, tiled=True),
    )
    grad_branch = grad_middle.astype(jnp.bfloat16)
    grad_mixed = project("rpe,pde->rpd", grad_branch, back_out).astype(jnp.bfloat16)
    term_out = project("rpd,rpe->pde", mixed_rows, grad_branch)
    grad_mixed_frames = lax.all_to_all(grad_mixed, "pos", split_axis=0, concat_axis=1, tiled=True)
    grad_heads = grad_mixed_frames.reshape(query.shape)
    again_scores = masked_scores(query, key_part)
    attend = jnp.exp(again_scores - log_total)
    grad_value = project("fhqk,fqhe->fkhe", attend.astype(jnp.bfloat16), grad_heads)
    grad_attend = project("fqhe,fkhe->fhqk", grad_heads, value_part)
    row_inner = jnp.sum(attend * grad_attend, axis=-1, keepdims=True)
    grad_scores = (attend * (grad_attend - row_inner)).astype(jnp.bfloat16)
    grad_query = project("fhqk,fkhe->fqhe", grad_scores, key_part) * scale
    grad_key = project("fhqk,fqhe->fkhe", grad_scores, query) * scale
    grad_qkv_frames = (
        jnp.stack([grad_query, grad_key, grad_value], axis=2)
        .reshape(qkv_frames.shape)
        .astype(jnp.bfloat16)
    )
    grad_qkv_rows = lax.all_to_all(grad_qkv_frames, "pos", split_axis=1, concat_axis=0, tiled=True)
    grad_normed_one = project("rpe,pde->rpd", grad_qkv_rows, back_qkv)
    term_qkv = project("rpd,rpe->pde", normed_one_low, grad_qkv_rows)
    grad_input_norm, term_gain_a = rms_backward(grad_normed_one, normed_one, inverse_one, gain_one)
    grad_rows = (grad_middle + grad_input_norm).astype(jnp.bfloat16)
    grad_frames = lax.all_to_all(grad_rows, "pos", split_axis=0, concat_axis=1, tiled=True)
    sum_qkv, sum_out, sum_gain_a = (
        lax.psum_scatter(
            term_qkv.astype(jnp.bfloat16), "frames", scatter_dimension=1, tiled=True
        ).astype(jnp.float32),
        lax.psum_scatter(
            term_out.astype(jnp.bfloat16), "frames", scatter_dimension=1, tiled=True
        ).astype(jnp.float32),
        lax.psum_scatter(
            term_gain_a.astype(jnp.bfloat16), "frames", scatter_dimension=1, tiled=True
        ).astype(jnp.float32),
    )
    return (output, grad_frames, sum_qkv, sum_out, sum_ffn, sum_down, sum_gain_a, sum_gain_f)


ROWS = ("pos", "spot")
PLANE = ("spot", "half")


def plain(left, right):
    return lax.dot_general(left, right, (((1,), (0,)), ((), ())), preferred_element_type=jnp.float32)


def by_columns(left, right):
    return lax.dot_general(left, right, (((1,), (1,)), ((), ())), preferred_element_type=jnp.float32)


def over_rows(left, right):
    return lax.dot_general(left, right, (((0,), (0,)), ((), ())), preferred_element_type=jnp.float32)


def tie(*values):
    return lax.optimization_barrier(values)


(
    UPS_NEAR, UPS_FAR, THIRD_A, THIRD_B, DOWN_A, DOWN_B, OWN_NEAR, OWN_FAR, LATE_NEAR, LATE_FAR,
    QKV_NEAR, QKV_FAR, RESULT, SUMS, SUM_DOWN,
) = range(15)
(
    AT_QKV_MOVED, AT_QKV, AT_MIXED, AT_MIXED_MOVED, AT_BRANCH, AT_GOT_BRANCH, AT_MIDDLE,
    AT_FFN_OTHER, AT_GATE_UP, AT_BACK, AT_GOT_BACK, AT_GRAD_BRANCH, AT_GRAD_MIXED,
    AT_GRAD_MIXED_MOVED, AT_GRAD_QKV, AT_GRAD_QKV_MOVED, AT_QKV_GRAD, AT_LAST_BACK, AT_GOT_LAST,
    AT_GRAD_ROWS, AT_GRAD_INPUT, AT_QKV_FAR,
) = range(22)
DUE = {
    UPS_NEAR: AT_QKV,
    UPS_FAR: None,
    THIRD_A: AT_QKV_MOVED,
    THIRD_B: AT_GATE_UP,
    DOWN_A: AT_GRAD_MIXED_MOVED,
    DOWN_B: AT_GRAD_BRANCH,
    OWN_NEAR: AT_GRAD_QKV,
    OWN_FAR: AT_QKV_GRAD,
    LATE_NEAR: AT_LAST_BACK,
    LATE_FAR: AT_QKV_GRAD,
    QKV_NEAR: None,
    QKV_FAR: None,
    RESULT: AT_LAST_BACK,
    SUMS: AT_GRAD_INPUT,
    SUM_DOWN: None,
}


class Flow:
    def __init__(self):
        self.moving = {}

    def send(self, name, *values):
        self.moving[name] = values

    def at(self, point, *values):
        names = [name for name in self.moving if DUE[name] == point]
        if names:
            tied = tie(*values, *[v for name in names for v in self.moving[name]])
            values, rest = tied[: len(values)], tied[len(values) :]
            for name in names:
                size = len(self.moving[name])
                self.moving[name], rest = rest[:size], rest[size:]
        return values if len(values) > 1 else values[0]

    def take(self, *names):
        return [v for name in names for v in self.moving[name]]


def pick(stack, index):
    return lax.dynamic_index_in_dim(stack, index, 0, keepdims=False)


def hop(value, k, spots):
    return value if k == 0 else lax.ppermute(value, "spot", [(i, i ^ k) for i in range(spots)])


def trade(value):
    return lax.ppermute(value, "half", [(0, 1), (1, 0)])


def swap(values, blocks):
    return lax.all_to_all(
        values.reshape(blocks, -1, values.shape[-1]), ROWS, split_axis=0, concat_axis=0, tiled=True
    )


def rows_from_spots(values, blocks):
    return swap(values, blocks).swapaxes(0, 1)


def head_runs(width, groups, spots):
    size = width // groups // spots // 2
    return [((g * spots + a) * 2 * size, ((g * spots + a) * 2 + 1) * size) for g in range(groups) for a in range(spots)], size


def unit_runs(width, groups):
    size = width // groups // 2
    return [(g * 2 * size, (g * 2 + 1) * size) for g in range(groups)], size


def call(kernel, name, grid, inputs, outputs, scalars, scratch=(), share=8):
    moved = sum(a.size * a.dtype.itemsize for a, _, _ in inputs)
    return pl.pallas_call(
        kernel,
        grid_spec=pltpu.PrefetchScalarGridSpec(
            num_scalar_prefetch=1,
            grid=grid,
            in_specs=[pl.BlockSpec(block, where) for _, block, where in inputs],
            out_specs=[pl.BlockSpec(block, where) for _, _, block, where in outputs],
            scratch_shapes=list(scratch),
        ),
        out_shape=[jax.ShapeDtypeStruct(shape, dtype) for shape, dtype, _, _ in outputs],
        compiler_params=pltpu.CompilerParams(vmem_limit_bytes=48 << 20),
        cost_estimate=pl.CostEstimate(flops=0, transcendentals=0, bytes_accessed=moved // share),
        name=name,
    )(scalars, *[a for a, _, _ in inputs])


def aligned(start, size):
    return pl.ds(pl.multiple_of(start, LANES), size)


def collect_kernel(widths, scalars, *refs):
    parts, outs = refs[: len(widths)], refs[len(widths) :]
    for k, out in enumerate(outs):

        @pl.when(pl.program_id(0) == k)
        def _():
            start = 0
            for part, width in zip(parts, widths):
                out[:, start : start + width] = part[0]
                start += width


def collect(parts, widths, scalars):
    count, rows = scalars.shape[0] - 1, parts[0].shape[1]
    cuts = 2
    step, width = rows // cuts, sum(widths)

    def spec(k):
        return lambda j, r, s: (jnp.where(j == k, r, jnp.where(j < k, 0, cuts - 1)), 0)

    return call(
        functools.partial(collect_kernel, widths),
        "collect",
        (count, cuts),
        [(a, (1, step, n), lambda j, r, s: (s[1 + j], r, 0)) for a, n in zip(parts, widths)],
        [((rows, width), parts[0].dtype, (step, width), spec(k)) for k in range(count)],
        scalars,
    )


def split_kernel(runs, count, per, whose, rests, scalars, *refs):
    starts, size = runs
    pieces, outs = refs[: count * per], refs[count * per :]
    half = scalars[0]
    for k in range(count):
        at = scalars[1 + k]
        for i, pair in enumerate(starts):
            piece = pieces[k * per + (i if per > 1 else 0)]
            for out, other in zip(outs, whose):
                first, second = pair[::-1] if other else pair
                columns = aligned(first + half * (second - first), size)
                out[pl.ds(at, 1), :, i * size : (i + 1) * size] = piece[:, columns][None]
        for out, (start, width) in zip(outs[len(whose) :], rests):
            out[pl.ds(at, 1)] = pieces[k][:, start : start + width][None]


def split_columns(pieces, runs, scalars, whose=(False, True), width=None, rests=()):
    starts, size = runs
    per = len(pieces[0])
    rows = pieces[0][0].shape[0]
    count, step = len(pieces), rows // 2
    widths = [len(starts) * size] * len(whose) + [n for _, n in rests]
    outs = call(
        functools.partial(split_kernel, runs, count, per, whose, rests),
        "split_columns",
        (2,),
        [
            (a, (step, width or a.shape[1]), lambda r, s: (r, 0))
            for piece in pieces
            for a in piece
        ],
        [
            ((count, rows, n), pieces[0][0].dtype, (count, step, n), lambda r, s: (0, r, 0))
            for n in widths
        ],
        scalars,
    )
    return [out.reshape(count * rows, -1) for out in outs]


def place_kernel(runs, parts, skip, count, weighted, scalars, *refs):
    pieces, out = refs[: count * parts], refs[-1 - weighted]
    half = scalars[0]
    for k in range(count):

        @pl.when(pl.program_id(0) == k)
        def _():
            for p in range(parts):
                ref = pieces[k * parts + p]
                if runs is None:
                    out[0] = ref[:, skip:].astype(out.dtype)
                    continue
                starts, size = runs
                for i, pair in enumerate(starts):
                    first, second = pair[::-1] if p else pair
                    columns = aligned(first + half * (second - first), size)
                    out[0, :, columns] = ref[:, i * size : (i + 1) * size].astype(out.dtype)

    if weighted:
        products = out[0] * refs[count * parts][0].astype(jnp.float32)
        refs[-1][0] = jnp.sum(products, axis=-1, keepdims=True)


def place(pieces, scalars, rows, width, runs=None, skip=0, dtype=jnp.float32, weight=None):
    count, parts = len(pieces), len(pieces[0])
    total = weight.shape[0] if weight is not None else count
    cuts = 2 if rows * width > (1 << 19) else 1
    step = rows // cuts

    def spec(k, first):
        base = first // step
        return lambda j, r, s: (base + jnp.where(j == k, r, jnp.where(j < k, 0, cuts - 1)), 0)

    entry = lambda j, r, s: (s[1 + j], r, 0)
    inputs = [
        (a, (step, a.shape[1]), spec(k, first))
        for k, piece in enumerate(pieces)
        for a, first in piece
    ]
    outputs = [((total, rows, width), dtype, (1, step, width), entry)]
    if weight is not None:
        inputs.append((weight, (1, step, width), entry))
        outputs.append(((total, rows, 1), jnp.float32, (1, step, 1), entry))
    outs = call(
        functools.partial(place_kernel, runs, parts, skip, count, int(weight is not None)),
        "place",
        (count, cuts),
        inputs,
        outputs,
        scalars,
        share=8,
    )
    return outs[0] if weight is None else outs


def halves_rows(step, own):
    count = own.shape[0] // step
    return (
        lambda r, *s: (jnp.minimum(r, count - 1), 0),
        lambda r, *s: (jnp.maximum(r - count, 0), 0),
    )


def unit_of(values):
    inverse = lax.rsqrt(jnp.mean(values * values, axis=-1, keepdims=True) + EPSILON)
    return values * inverse, inverse


def spread(values, scratch, half, own, other):
    scratch[...] = values.astype(scratch.dtype)
    for a in range(own.shape[1] // LANES):
        own[:, a * LANES : (a + 1) * LANES] = scratch[:, aligned((2 * a + half) * LANES, LANES)]
        other[:, a * LANES : (a + 1) * LANES] = scratch[:, aligned((2 * a + 1 - half) * LANES, LANES)]


def gather(own, other, scratch, half):
    for a in range(own[0].shape[1] // LANES):
        block = slice(a * LANES, (a + 1) * LANES)
        scratch[:, aligned((2 * a + half) * LANES, LANES)] = own[0][:, block] + own[1][:, block]
        scratch[:, aligned((2 * a + 1 - half) * LANES, LANES)] = other[0][:, block] + other[1][:, block]
    return scratch[...]


def either(own_ref, got_ref):
    mine = pl.program_id(0) < pl.num_programs(0) // 2
    return jnp.where(mine, own_ref[...].astype(jnp.float32), got_ref[...].astype(jnp.float32))


def norm_kernel(scalars, own_rows, got_rows, gain, own, other, scratch):
    unit, _ = unit_of(either(own_rows, got_rows))
    spread(unit * gain[...], scratch, scalars[0], own, other)


def middle_kernel(scalars, own_rows, got_rows, branch, got_branch, gain, middle, own, other, scratch):
    values = either(own_rows, got_rows) + (branch[...] + got_branch[...])
    middle[...] = values
    unit, _ = unit_of(values)
    spread(unit * gain[...], scratch, scalars[0], own, other)


def pull(values, upstream, gain):
    unit, inverse = unit_of(values)
    scaled = upstream * gain
    inner = jnp.mean(scaled * unit, axis=-1, keepdims=True)
    return inverse * (scaled - unit * inner)


def middle_back_kernel(
    scalars, middle, own, other, got_own, got_other, own_up, got_up, gain, whole, low, scratch
):
    upstream = gather((own, got_other), (other, got_own), scratch, scalars[0])
    grad = pull(middle[...], upstream, gain[...]) + either(own_up, got_up)
    whole[...] = grad
    low[...] = grad.astype(low.dtype)


def input_back_kernel(
    scalars, rows, own, other, got_own, got_other, grad_middle, gain, out, scratch
):
    upstream = gather((own, got_other), (other, got_own), scratch, scalars[0])
    grad = pull(rows[...].astype(jnp.float32), upstream, gain[...])
    out[...] = (grad_middle[...] + grad).astype(out.dtype)


def softmax_of(query, keys, allowed):
    scores = jnp.where(allowed, by_columns(query, keys) * HEAD ** (-0.5), NEGATIVE)
    exponent = jnp.exp(scores - jnp.max(scores, axis=-1, keepdims=True))
    return exponent / jnp.sum(exponent, axis=-1, keepdims=True)


def frame_mask(positions, frames):
    count = positions * frames
    row = lax.broadcasted_iota(jnp.int32, (count, count), 0)
    column = lax.broadcasted_iota(jnp.int32, (count, count), 1)
    return (row % frames == column % frames) & (row >= column)


def attend_kernel(qkv_ref, mixed_ref):
    positions, frames, width = qkv_ref.shape
    count, third = positions * frames, width // 3
    allowed = frame_mask(positions, frames)
    lane = lax.broadcasted_iota(jnp.int32, (count, LANES), 1)
    for first in range(0, third, LANES):
        query, keys, values = (
            qkv_ref[:, :, part * third + first : part * third + first + LANES].reshape(count, LANES)
            for part in range(3)
        )
        mixed = jnp.zeros((count, LANES), jnp.float32)
        for start in range(0, LANES, HEAD):
            inside = (lane >= start) & (lane < start + HEAD)
            probs = softmax_of(jnp.where(inside, query, jnp.zeros_like(query)), keys, allowed)
            mixed = jnp.where(inside, plain(probs.astype(jnp.bfloat16), values), mixed)
        mixed_ref[:, :, first : first + LANES] = mixed.astype(mixed_ref.dtype).reshape(
            positions, frames, LANES
        )


def attend_back_kernel(qkv_ref, grad_ref, out_ref):
    positions, frames, width = qkv_ref.shape
    count, third = positions * frames, width // 3
    scale = HEAD ** (-0.5)
    allowed = frame_mask(positions, frames)
    lane = lax.broadcasted_iota(jnp.int32, (count, LANES), 1)
    for first in range(0, third, LANES):
        query, keys, values = (
            qkv_ref[:, :, part * third + first : part * third + first + LANES].reshape(count, LANES)
            for part in range(3)
        )
        upstream = grad_ref[:, :, first : first + LANES].reshape(count, LANES)
        grads = [jnp.zeros((count, LANES), jnp.float32)] * 3
        for start in range(0, LANES, HEAD):
            inside = (lane >= start) & (lane < start + HEAD)
            probs = softmax_of(jnp.where(inside, query, jnp.zeros_like(query)), keys, allowed)
            grad_probs = by_columns(jnp.where(inside, upstream, jnp.zeros_like(upstream)), values)
            inner = jnp.sum(probs * grad_probs, axis=-1, keepdims=True)
            grad_scores = (probs * (grad_probs - inner)).astype(jnp.bfloat16)
            new = (
                plain(grad_scores, keys) * scale,
                over_rows(grad_scores, query) * scale,
                over_rows(probs.astype(jnp.bfloat16), upstream),
            )
            grads = [jnp.where(inside, value, old) for value, old in zip(new, grads)]
        for part, grad in enumerate(grads):
            out_ref[:, :, part * third + first : part * third + first + LANES] = grad.astype(
                out_ref.dtype
            ).reshape(positions, frames, LANES)


def over_frames(kernel, out_width, *arrays):
    positions, frames, width = arrays[0].shape
    step = min(frames, 256 // positions)
    heads = width // 3 // HEAD
    work = frames // step * heads * (step * positions) ** 2
    return pl.pallas_call(
        kernel,
        grid=(frames // step,),
        in_specs=[
            pl.BlockSpec((positions, step, a.shape[2]), lambda i: (0, i, 0)) for a in arrays
        ],
        out_specs=pl.BlockSpec((positions, step, out_width), lambda i: (0, i, 0)),
        out_shape=jax.ShapeDtypeStruct((positions, frames, out_width), arrays[0].dtype),
        compiler_params=pltpu.CompilerParams(vmem_limit_bytes=48 << 20),
        cost_estimate=pl.CostEstimate(
            flops=4 * LANES * work,
            transcendentals=work,
            bytes_accessed=2 * positions * frames * (width + out_width),
        ),
        name=kernel.__name__,
    )(*arrays)


def spots_plan(
    frames_in,
    frame_valid,
    last_position,
    weight_qkv,
    weight_out,
    weight_ffn,
    weight_down,
    gain_attn,
    gain_ffn,
    grad_out,
):
    f32, bf16 = jnp.float32, jnp.bfloat16
    flow = Flow()
    frames, positions, depth = frames_in.shape
    spots, slice_rows = weight_qkv.shape[:2]
    plane, near = spots * 2, spots - 1
    spot, half = lax.axis_index("spot"), lax.axis_index("half")
    heads = head_runs(3 * depth, 3, spots)
    units = unit_runs(weight_ffn.shape[2], 2)
    hidden_units = weight_ffn.shape[2] // 2
    down_index = lax.axis_index(PLANE) % spots
    down_pairs = [
        [(f, (f % spots ^ k) * 2 + f // spots) for f in range(plane)] for k in range(spots)
    ]
    early = spots // 2
    by_spot = jnp.stack([half] + [spot ^ k for k in range(spots)]).astype(jnp.int32)
    by_slice = jnp.stack([half] + [down_index ^ k for k in range(spots)]).astype(jnp.int32)
    slot = lax.broadcasted_iota(jnp.int32, (frames, positions), 1)
    live = ((frame_valid[:, None] > 0) & (slot <= last_position[:, None]))[:, :, None]

    gains = jnp.pad(jnp.stack([gain_attn, gain_ffn], axis=2), ((0, 0), (0, 0), (0, LANES - 2)))
    parts = (weight_qkv, weight_out, gains, weight_ffn)
    widths = (3 * depth, depth, LANES, hidden_units)
    first = collect(parts, widths, jnp.concatenate([by_spot[:1], by_spot[2:]]))
    first = list(collect(parts, widths, by_spot[:2])) + [hop(p, k + 1, spots) for k, p in enumerate(first)]
    upstream = jnp.where(live, grad_out, jnp.zeros_like(grad_out))
    rows_in = jnp.concatenate([frames_in.swapaxes(0, 1), upstream.swapaxes(0, 1)], axis=1)
    own_rows = swap(rows_in, positions)
    ups = [pick(weight_ffn, spot ^ k)[:, hidden_units:] for k in range(spots)]
    third = [pick(weight_down, down_index ^ k) for k in range(spots)]
    tied = tie(*first, *ups, *third)
    first, ups, third = tied[:spots], tied[spots : 2 * spots], tied[2 * spots :]
    ups = [hop(piece, k, spots) for k, piece in enumerate(ups)]
    flow.send(UPS_NEAR, *ups[:near])
    flow.send(UPS_FAR, ups[near])
    own_rows, own_up = (
        own_rows[:, part * frames : (part + 1) * frames].reshape(-1, depth) for part in range(2)
    )
    got_rows, got_up = trade(own_rows), trade(own_up)

    own_count = own_rows.shape[0]
    count = own_count * 2
    step = own_count // 2
    pieces = [[piece] for piece in first]
    (qkv_sent,) = split_columns(pieces, heads, by_spot, (True,), 3 * depth)
    qkv_other = trade(qkv_sent)
    whole = 4 * depth + LANES
    qkv_own, full_out, gains = split_columns(
        pieces, heads, by_spot, (False,), whole, ((3 * depth, depth), (4 * depth, LANES))
    )
    gains = gains[:, :2]
    pair = [part.reshape(spots, slice_rows, 2) for part in (gains, trade(gains))]
    even, odd = (jnp.where(half == h, *pair) for h in range(2))
    gains = jnp.stack([even, odd], axis=1).reshape(depth, 2).T.astype(f32)
    gain_one, gain_two = gains[:1], gains[1:]
    mine, theirs = halves_rows(step, own_rows)
    straight = lambda r, *s: (r, 0)
    crossed = lambda r, *s: ((r + 2) % 4, 0)
    top = lambda r, *s: (0, 0)
    lower = lambda blocks, where: lambda *r: (where(*r)[0] + blocks, 0)
    rows = [(own_rows, (step, depth), mine), (got_rows, (step, depth), theirs)]
    split_rows = [((count, depth // 2), bf16, (step, depth // 2), straight)] * 2
    low_scratch, scratch = pltpu.VMEM((step, depth), bf16), pltpu.VMEM((step, depth), f32)
    one_own, one_other = call(
        norm_kernel, "norm", (4,), rows + [(gain_one, (1, depth), top)], split_rows, by_spot, [low_scratch]
    )
    qkv_rows = (plain(one_own, qkv_own) + plain(one_other, qkv_other)).astype(bf16)
    third = [lax.ppermute(p, PLANE, down_pairs[k]) for k, p in enumerate(third)]
    flow.send(THIRD_A, *third[:early])
    flow.send(THIRD_B, *third[early:])
    qkv = flow.at(AT_QKV_MOVED, swap(flow.at(AT_QKV, qkv_rows), positions))
    mixed = flow.at(AT_MIXED, over_frames(attend_kernel, depth // 2, qkv))
    mixed = flow.at(AT_MIXED_MOVED, swap(mixed, positions)).reshape(count, -1)
    branch = flow.at(AT_BRANCH, plain(mixed, full_out))
    got_branch = flow.at(AT_GOT_BRANCH, trade(branch))
    middle, two_own, two_other = call(
        middle_kernel,
        "middle",
        (4,),
        rows
        + [(branch, (step, depth), straight), (got_branch, (step, depth), crossed)]
        + [(gain_two, (1, depth), top)],
        [((count, depth), f32, (step, depth), straight)] + split_rows,
        by_spot,
        [low_scratch],
    )

    two_own, two_other = flow.at(AT_MIDDLE, two_own, two_other)
    ups = flow.take(UPS_NEAR, UPS_FAR)
    gate_run = tuple(start + whole for start in units[0][0])
    up_run = tuple(start - hidden_units for start in units[0][1])
    ffn_own, ffn_sent = split_columns(
        list(zip(first, ups)), ([gate_run, up_run], units[1]), by_spot
    )
    ffn_other = flow.at(AT_FFN_OTHER, trade(ffn_sent))
    gate_up = flow.at(AT_GATE_UP, plain(two_own, ffn_own) + plain(two_other, ffn_other))
    width = gate_up.shape[1] // 2
    gate, upward = gate_up[:, :width], gate_up[:, width:]
    gate_sig = jax.nn.sigmoid(gate)
    hidden = (gate * gate_sig * upward).astype(bf16)
    upstream = jnp.concatenate([own_up, got_up])
    down_grad = over_rows(hidden, upstream).astype(bf16).reshape(spots, -1, depth)
    down_sent = [pick(down_grad, spot ^ k) for k in range(spots)]
    down_back = [[(b, a) for a, b in pairs] for pairs in down_pairs]
    down_sent = [lax.ppermute(p, PLANE, pairs) for p, pairs in zip(down_sent, down_back)]
    flow.send(DOWN_A, *down_sent[::2])
    flow.send(DOWN_B, *down_sent[1::2])
    third = flow.take(THIRD_A, THIRD_B)
    full_down = place([[(piece, 0)] for piece in third], by_spot, *weight_down.shape[1:], dtype=bf16)
    full_down = full_down.reshape(-1, depth)

    grad_hidden = by_columns(upstream, full_down)
    grad_upward = grad_hidden * gate * gate_sig
    grad_gate = grad_hidden * upward * gate_sig * (1.0 + gate * (1.0 - gate_sig))
    grad_gate_up = jnp.concatenate([grad_gate, grad_upward], axis=-1).astype(bf16)
    back = jnp.concatenate([by_columns(grad_gate_up, ffn_own), by_columns(grad_gate_up, ffn_other)])
    back = flow.at(AT_BACK, back)
    got_back = trade(back)
    got_back = flow.at(AT_GOT_BACK, got_back)
    wide, narrow = (step, depth), (step, depth // 2)
    grad_middle, grad_branch = call(
        middle_back_kernel,
        "middle_back",
        (4,),
        [(middle, wide, straight), (back, narrow, straight), (back, narrow, lower(4, straight))]
        + [(got_back, narrow, crossed), (got_back, narrow, lower(4, crossed))]
        + [(own_up, wide, mine), (got_up, wide, theirs), (gain_two, (1, depth), top)],
        [
            ((count, depth), f32, wide, straight),
            ((count, depth), bf16, wide, straight),
        ],
        by_spot,
        [scratch],
    )

    cut = lambda grad: [pick(grad.reshape(spots, slice_rows, -1), spot ^ k) for k in range(spots)]
    grad_branch = flow.at(AT_GRAD_BRANCH, grad_branch)
    ffn_grad_own = cut(over_rows(two_own, grad_gate_up).astype(bf16))
    ffn_grad_got = cut(trade(over_rows(two_other, grad_gate_up).astype(bf16)))
    ffn_grad_own = [hop(piece, k, spots) for k, piece in enumerate(ffn_grad_own)]
    flow.send(OWN_NEAR, *ffn_grad_own[:near])
    flow.send(OWN_FAR, ffn_grad_own[near])
    late = [
        hop(jnp.concatenate(pair, axis=1), k, spots)
        for k, pair in enumerate(
            zip(ffn_grad_got, cut(over_rows(mixed, grad_branch).astype(bf16)))
        )
    ]
    flow.send(LATE_NEAR, *late[:near])
    flow.send(LATE_FAR, late[near])
    grad_mixed = flow.at(AT_GRAD_MIXED, by_columns(grad_branch, full_out).astype(bf16))
    grad_mixed_frames = flow.at(AT_GRAD_MIXED_MOVED, swap(grad_mixed, positions))
    grad_qkv = over_frames(attend_back_kernel, 3 * depth // 2, qkv, grad_mixed_frames)
    grad_qkv = flow.at(AT_GRAD_QKV, grad_qkv)
    result = plain(hidden, full_down)
    result = (middle[:own_count] + result[:own_count] + trade(result[own_count:])).astype(bf16)
    down_sent = [v for pair in zip(flow.take(DOWN_A), flow.take(DOWN_B)) for v in pair]
    flow.send(
        SUM_DOWN, place([[(piece, 0)] for piece in down_sent], by_slice, *weight_down.shape[1:])
    )
    grad_qkv_rows = swap(grad_qkv, positions).reshape(count, -1)
    grad_qkv_rows = flow.at(AT_GRAD_QKV_MOVED, grad_qkv_rows)
    grad_qkv_rows, result = tie(grad_qkv_rows, result)
    flow.send(RESULT, rows_from_spots(result, positions))
    qkv_grad_got = trade(over_rows(one_other, grad_qkv_rows).astype(bf16))
    qkv_grad_own = flow.at(AT_QKV_GRAD, over_rows(one_own, grad_qkv_rows).astype(bf16))
    qkv_sent = [jnp.concatenate(pair) for pair in zip(cut(qkv_grad_own), cut(qkv_grad_got))]
    *qkv_sent, grad_qkv_rows = tie(*qkv_sent, grad_qkv_rows)
    qkv_sent = [hop(piece, k, spots) for k, piece in enumerate(qkv_sent)]
    flow.send(QKV_NEAR, *qkv_sent[:near])
    flow.send(QKV_FAR, qkv_sent[near])
    back_own = by_columns(grad_qkv_rows, qkv_own)
    back_other = by_columns(grad_qkv_rows, qkv_other)
    back_own, back_other = flow.at(AT_LAST_BACK, back_own, back_other)
    ffn_grad_own, late = flow.take(OWN_NEAR, OWN_FAR), flow.take(LATE_NEAR, LATE_FAR)
    sum_ffn, term_ffn = place(
        [[(own, 0), (got, 0)] for own, got in zip(ffn_grad_own, late)],
        by_spot,
        slice_rows,
        2 * hidden_units,
        units,
        weight=weight_ffn,
    )
    sum_out = place([[(piece, 0)] for piece in late], by_spot, slice_rows, depth, skip=hidden_units)
    flow.send(SUMS, sum_ffn, sum_out)
    got_back = trade(jnp.concatenate([back_own[own_count:], back_other[own_count:]]))
    got_back = flow.at(AT_GOT_LAST, got_back)
    (grad_rows,) = call(
        input_back_kernel,
        "input_back",
        (2,),
        [(own_rows, wide, straight), (back_own, narrow, straight), (back_other, narrow, straight)]
        + [(got_back, narrow, straight), (got_back, narrow, lower(2, straight))]
        + [(grad_middle, wide, straight), (gain_one, (1, depth), top)],
        [((own_count, depth), bf16, wide, straight)],
        by_spot,
        [scratch],
    )
    grad_rows = flow.at(AT_GRAD_ROWS, grad_rows)
    grad_input = flow.at(AT_GRAD_INPUT, rows_from_spots(grad_rows, positions))
    (result,) = flow.take(RESULT)
    output = jnp.where(live, result, jnp.zeros_like(result))
    qkv_sent = flow.take(QKV_NEAR, QKV_FAR)
    qkv_sent[near] = flow.at(AT_QKV_FAR, qkv_sent[near])
    sum_ffn, sum_out = flow.take(SUMS)
    (sum_down,) = flow.take(SUM_DOWN)
    sum_qkv, term_attn = place(
        [[(piece, 0), (piece, slice_rows)] for piece in qkv_sent],
        by_spot,
        slice_rows,
        3 * depth,
        heads,
        weight=weight_qkv,
    )
    gain_terms = [
        term.reshape(spots, slice_rows) / gain.astype(f32)
        for term, gain in ((term_attn, gain_attn), (term_ffn, gain_ffn))
    ]
    return (output, grad_input, sum_qkv, sum_out, sum_ffn, sum_down, *gain_terms)


def solution(mesh):
    plane, lines = mesh.shape["frames"], mesh.shape["pos"]

    def run(*arrays):
        positions, depth = arrays[0].shape[1:]
        spots = positions // lines
        slice_rows = depth // plane
        shares = arrays[5].shape[2] // 4
        fits = plane == 2 * spots and spots & (spots - 1) == 0
        fits = fits and slice_rows % LANES == 0 and shares % LANES == 0
        if fits:
            inner = Mesh(mesh.devices.reshape(spots, 2, lines), PLANE + ("pos",))
            by_frame, weight, plan = P(PLANE + ("pos",)), P("pos", PLANE), spots_plan
        else:
            inner, plan = mesh, gathered_plan
            by_frame, weight = P(("frames", "pos")), P("pos", "frames")
        return jax.shard_map(
            plan,
            mesh=inner,
            in_specs=(by_frame,) * 3 + (weight,) * 6 + (by_frame,),
            out_specs=(by_frame,) * 2 + (weight,) * 6,
            check_vma=False,
        )(*arrays)

    return run
```

```python
import functools

import jax
import jax.numpy as jnp
from jax import lax
from jax.experimental import pallas as pl
from jax.experimental.pallas import tpu as pltpu
from jax.sharding import Mesh, PartitionSpec as P

HEADS = 16
HEAD = 64
LANES = 128
EPSILON = 1e-06
NEGATIVE = -1e30


def rms_forward(values, gain_row):
    inverse = lax.rsqrt(jnp.mean(values * values, axis=-1, keepdims=True) + EPSILON)
    normed = values * inverse
    return (normed * gain_row[None], normed, inverse)


def rms_backward(upstream, normed, inverse, gain_row):
    scaled = upstream * gain_row[None]
    row_inner = jnp.mean(scaled * normed, axis=-1, keepdims=True)
    return (inverse * (scaled - normed * row_inner), jnp.sum(upstream * normed, axis=0))


def project(pattern, left_side, right_side):
    return jnp.einsum(pattern, left_side, right_side, preferred_element_type=jnp.float32)


def split_heads(qkv_frames):
    frames = qkv_frames.shape[0]
    length = qkv_frames.shape[1]
    pieces = qkv_frames.reshape(frames, length, 3, HEADS, HEAD)
    return (pieces[:, :, 0], pieces[:, :, 1], pieces[:, :, 2])


def masked_scores(query, key_part):
    raw_scores = project("fqhe,fkhe->fhqk", query, key_part) * HEAD ** (-0.5)
    length = raw_scores.shape[-1]
    allowed = lax.broadcasted_iota(jnp.int32, (length, length), 0) >= lax.broadcasted_iota(
        jnp.int32, (length, length), 1
    )
    return jnp.where(allowed, raw_scores, NEGATIVE)


def gathered_plan(
    frames_in,
    frame_valid,
    last_position,
    weight_qkv,
    weight_out,
    weight_ffn,
    weight_down,
    gain_attn,
    gain_ffn,
    grad_out,
):
    scale = HEAD ** (-0.5)
    slot_index = lax.broadcasted_iota(jnp.int32, (frames_in.shape[0], frames_in.shape[1]), 1)
    live_mask = (frame_valid[:, None] > 0) & (slot_index <= last_position[:, None])
    pos_rows = lax.all_to_all(frames_in, "pos", split_axis=1, concat_axis=0, tiled=True)
    full_qkv, full_out, full_gain_a = (
        lax.all_gather(weight_qkv, "frames", axis=1, tiled=True),
        lax.all_gather(weight_out, "frames", axis=1, tiled=True),
        lax.all_gather(gain_attn, "frames", axis=1, tiled=True),
    )
    gain_one = full_gain_a.astype(jnp.float32)
    residual = pos_rows.astype(jnp.float32)
    scaled_one, normed_one, inverse_one = rms_forward(residual, gain_one)
    normed_one_low = scaled_one.astype(jnp.bfloat16)
    qkv_rows = project("rpd,pde->rpe", normed_one_low, full_qkv).astype(jnp.bfloat16)
    qkv_frames = lax.all_to_all(qkv_rows, "pos", split_axis=0, concat_axis=1, tiled=True)
    query, key_part, value_part = split_heads(qkv_frames)
    scores = masked_scores(query, key_part)
    row_top = jnp.max(scores, axis=-1, keepdims=True)
    exponent = jnp.exp(scores - row_top)
    row_total = jnp.sum(exponent, axis=-1, keepdims=True)
    log_total = row_top + jnp.log(row_total)
    attend_low = (exponent / row_total).astype(jnp.bfloat16)
    mixed_heads = project("fhqk,fkhe->fqhe", attend_low, value_part)
    mixed_low = mixed_heads.reshape(frames_in.shape).astype(jnp.bfloat16)
    mixed_rows = lax.all_to_all(mixed_low, "pos", split_axis=1, concat_axis=0, tiled=True)
    middle = residual + project("rpd,pde->rpe", mixed_rows, full_out)
    full_ffn, full_down, full_gain_f = (
        lax.all_gather(weight_ffn, "frames", axis=1, tiled=True),
        lax.all_gather(weight_down, "frames", axis=1, tiled=True),
        lax.all_gather(gain_ffn, "frames", axis=1, tiled=True),
    )
    gain_two = full_gain_f.astype(jnp.float32)
    scaled_two, normed_two, inverse_two = rms_forward(middle, gain_two)
    normed_two_low = scaled_two.astype(jnp.bfloat16)
    gate_up = project("rpd,pde->rpe", normed_two_low, full_ffn)
    width = gate_up.shape[-1] // 2
    gate = gate_up[..., :width]
    upward = gate_up[..., width:]
    gate_sig = jax.nn.sigmoid(gate)
    hidden = (gate * gate_sig * upward).astype(jnp.bfloat16)
    result = middle + project("rpf,pfd->rpd", hidden, full_down)
    result_frames = lax.all_to_all(
        result.astype(jnp.bfloat16), "pos", split_axis=0, concat_axis=1, tiled=True
    )
    output = jnp.where(live_mask[:, :, None], result_frames, jnp.zeros_like(result_frames))
    upstream = jnp.where(live_mask[:, :, None], grad_out, jnp.zeros_like(grad_out))
    upstream_rows = lax.all_to_all(upstream, "pos", split_axis=1, concat_axis=0, tiled=True)
    back_ffn, back_down = (
        lax.all_gather(weight_ffn, "frames", axis=1, tiled=True),
        lax.all_gather(weight_down, "frames", axis=1, tiled=True),
    )
    grad_hidden = project("rpd,pfd->rpf", upstream_rows, back_down)
    term_down = project("rpf,rpd->pfd", hidden, upstream_rows)
    grad_upward = grad_hidden * gate * gate_sig
    grad_gate = grad_hidden * upward * gate_sig * (1.0 + gate * (1.0 - gate_sig))
    grad_gate_up = jnp.concatenate([grad_gate, grad_upward], axis=-1).astype(jnp.bfloat16)
    grad_normed_two = project("rpe,pde->rpd", grad_gate_up, back_ffn)
    term_ffn = project("rpd,rpe->pde", normed_two_low, grad_gate_up)
    grad_middle_norm, term_gain_f = rms_backward(grad_normed_two, normed_two, inverse_two, gain_two)
    grad_middle = upstream_rows.astype(jnp.float32) + grad_middle_norm
    sum_ffn, sum_down, sum_gain_f = (
        lax.psum_scatter(
            term_ffn.astype(jnp.bfloat16), "frames", scatter_dimension=1, tiled=True
        ).astype(jnp.float32),
        lax.psum_scatter(
            term_down.astype(jnp.bfloat16), "frames", scatter_dimension=1, tiled=True
        ).astype(jnp.float32),
        lax.psum_scatter(
            term_gain_f.astype(jnp.bfloat16), "frames", scatter_dimension=1, tiled=True
        ).astype(jnp.float32),
    )
    back_qkv, back_out = (
        lax.all_gather(weight_qkv, "frames", axis=1, tiled=True),
        lax.all_gather(weight_out, "frames", axis=1, tiled=True),
    )
    grad_branch = grad_middle.astype(jnp.bfloat16)
    grad_mixed = project("rpe,pde->rpd", grad_branch, back_out).astype(jnp.bfloat16)
    term_out = project("rpd,rpe->pde", mixed_rows, grad_branch)
    grad_mixed_frames = lax.all_to_all(grad_mixed, "pos", split_axis=0, concat_axis=1, tiled=True)
    grad_heads = grad_mixed_frames.reshape(query.shape)
    again_scores = masked_scores(query, key_part)
    attend = jnp.exp(again_scores - log_total)
    grad_value = project("fhqk,fqhe->fkhe", attend.astype(jnp.bfloat16), grad_heads)
    grad_attend = project("fqhe,fkhe->fhqk", grad_heads, value_part)
    row_inner = jnp.sum(attend * grad_attend, axis=-1, keepdims=True)
    grad_scores = (attend * (grad_attend - row_inner)).astype(jnp.bfloat16)
    grad_query = project("fhqk,fkhe->fqhe", grad_scores, key_part) * scale
    grad_key = project("fhqk,fqhe->fkhe", grad_scores, query) * scale
    grad_qkv_frames = (
        jnp.stack([grad_query, grad_key, grad_value], axis=2)
        .reshape(qkv_frames.shape)
        .astype(jnp.bfloat16)
    )
    grad_qkv_rows = lax.all_to_all(grad_qkv_frames, "pos", split_axis=1, concat_axis=0, tiled=True)
    grad_normed_one = project("rpe,pde->rpd", grad_qkv_rows, back_qkv)
    term_qkv = project("rpd,rpe->pde", normed_one_low, grad_qkv_rows)
    grad_input_norm, term_gain_a = rms_backward(grad_normed_one, normed_one, inverse_one, gain_one)
    grad_rows = (grad_middle + grad_input_norm).astype(jnp.bfloat16)
    grad_frames = lax.all_to_all(grad_rows, "pos", split_axis=0, concat_axis=1, tiled=True)
    sum_qkv, sum_out, sum_gain_a = (
        lax.psum_scatter(
            term_qkv.astype(jnp.bfloat16), "frames", scatter_dimension=1, tiled=True
        ).astype(jnp.float32),
        lax.psum_scatter(
            term_out.astype(jnp.bfloat16), "frames", scatter_dimension=1, tiled=True
        ).astype(jnp.float32),
        lax.psum_scatter(
            term_gain_a.astype(jnp.bfloat16), "frames", scatter_dimension=1, tiled=True
        ).astype(jnp.float32),
    )
    return (output, grad_frames, sum_qkv, sum_out, sum_ffn, sum_down, sum_gain_a, sum_gain_f)


ROWS = ("pos", "spot")
PLANE = ("spot", "half")


def plain(left, right):
    return lax.dot_general(left, right, (((1,), (0,)), ((), ())), preferred_element_type=jnp.float32)


def by_columns(left, right):
    return lax.dot_general(left, right, (((1,), (1,)), ((), ())), preferred_element_type=jnp.float32)


def over_rows(left, right):
    return lax.dot_general(left, right, (((0,), (0,)), ((), ())), preferred_element_type=jnp.float32)


def tie(*values):
    return lax.optimization_barrier(values)


(
    UPS_NEAR, UPS_FAR, THIRD_A, THIRD_B, DOWN_A, DOWN_B, OWN_NEAR, OWN_FAR, LATE_NEAR, LATE_FAR,
    QKV_NEAR, QKV_FAR, RESULT, SUMS, SUM_DOWN,
) = range(15)
(
    AT_QKV_MOVED, AT_QKV, AT_MIXED, AT_MIXED_MOVED, AT_BRANCH, AT_GOT_BRANCH, AT_MIDDLE,
    AT_FFN_OTHER, AT_GATE_UP, AT_BACK, AT_GOT_BACK, AT_GRAD_BRANCH, AT_GRAD_MIXED,
    AT_GRAD_MIXED_MOVED, AT_GRAD_QKV, AT_GRAD_QKV_MOVED, AT_QKV_GRAD, AT_LAST_BACK, AT_GOT_LAST,
    AT_GRAD_ROWS, AT_GRAD_INPUT, AT_QKV_FAR,
) = range(22)
DUE = {
    UPS_NEAR: AT_QKV,
    UPS_FAR: None,
    THIRD_A: AT_QKV_MOVED,
    THIRD_B: AT_GATE_UP,
    DOWN_A: AT_GRAD_MIXED_MOVED,
    DOWN_B: AT_GRAD_BRANCH,
    OWN_NEAR: AT_GRAD_QKV,
    OWN_FAR: AT_QKV_GRAD,
    LATE_NEAR: AT_LAST_BACK,
    LATE_FAR: AT_QKV_GRAD,
    QKV_NEAR: None,
    QKV_FAR: None,
    RESULT: AT_LAST_BACK,
    SUMS: AT_GRAD_ROWS,
    SUM_DOWN: None,
}


class Flow:
    def __init__(self):
        self.moving = {}

    def send(self, name, *values):
        self.moving[name] = values

    def at(self, point, *values):
        names = [name for name in self.moving if DUE[name] == point]
        if names:
            tied = tie(*values, *[v for name in names for v in self.moving[name]])
            values, rest = tied[: len(values)], tied[len(values) :]
            for name in names:
                size = len(self.moving[name])
                self.moving[name], rest = rest[:size], rest[size:]
        return values if len(values) > 1 else values[0]

    def take(self, *names):
        return [v for name in names for v in self.moving[name]]


def pick(stack, index):
    return lax.dynamic_index_in_dim(stack, index, 0, keepdims=False)


def hop(value, k, spots):
    return value if k == 0 else lax.ppermute(value, "spot", [(i, i ^ k) for i in range(spots)])


def trade(value):
    return lax.ppermute(value, "half", [(0, 1), (1, 0)])


def swap(values, blocks):
    return lax.all_to_all(
        values.reshape(blocks, -1, values.shape[-1]), ROWS, split_axis=0, concat_axis=0, tiled=True
    )


def rows_from_spots(values, blocks):
    return swap(values, blocks).swapaxes(0, 1)


def head_runs(width, groups, spots):
    size = width // groups // spots // 2
    return [((g * spots + a) * 2 * size, ((g * spots + a) * 2 + 1) * size) for g in range(groups) for a in range(spots)], size


def unit_runs(width, groups):
    size = width // groups // 2
    return [(g * 2 * size, (g * 2 + 1) * size) for g in range(groups)], size


def call(kernel, name, grid, inputs, outputs, scalars, scratch=(), share=8):
    moved = sum(a.size * a.dtype.itemsize for a, _, _ in inputs)
    return pl.pallas_call(
        kernel,
        grid_spec=pltpu.PrefetchScalarGridSpec(
            num_scalar_prefetch=1,
            grid=grid,
            in_specs=[pl.BlockSpec(block, where) for _, block, where in inputs],
            out_specs=[pl.BlockSpec(block, where) for _, _, block, where in outputs],
            scratch_shapes=list(scratch),
        ),
        out_shape=[jax.ShapeDtypeStruct(shape, dtype) for shape, dtype, _, _ in outputs],
        compiler_params=pltpu.CompilerParams(vmem_limit_bytes=48 << 20),
        cost_estimate=pl.CostEstimate(flops=0, transcendentals=0, bytes_accessed=moved // share),
        name=name,
    )(scalars, *[a for a, _, _ in inputs])


def aligned(start, size):
    return pl.ds(pl.multiple_of(start, LANES), size)


def collect_kernel(widths, scalars, *refs):
    parts, outs = refs[: len(widths)], refs[len(widths) :]
    for k, out in enumerate(outs):

        @pl.when(pl.program_id(0) == k)
        def _():
            start = 0
            for part, width in zip(parts, widths):
                out[:, start : start + width] = part[0]
                start += width


def collect(parts, widths, scalars):
    count, rows = scalars.shape[0] - 1, parts[0].shape[1]
    cuts = 2
    step, width = rows // cuts, sum(widths)

    def spec(k):
        return lambda j, r, s: (jnp.where(j == k, r, jnp.where(j < k, 0, cuts - 1)), 0)

    return call(
        functools.partial(collect_kernel, widths),
        "collect",
        (count, cuts),
        [(a, (1, step, n), lambda j, r, s: (s[1 + j], r, 0)) for a, n in zip(parts, widths)],
        [((rows, width), parts[0].dtype, (step, width), spec(k)) for k in range(count)],
        scalars,
    )


def split_kernel(runs, count, per, whose, rests, scalars, *refs):
    starts, size = runs
    pieces, outs = refs[: count * per], refs[count * per :]
    half = scalars[0]
    for k in range(count):
        at = scalars[1 + k]
        for i, pair in enumerate(starts):
            piece = pieces[k * per + (i if per > 1 else 0)]
            for out, other in zip(outs, whose):
                first, second = pair[::-1] if other else pair
                columns = aligned(first + half * (second - first), size)
                out[pl.ds(at, 1), :, i * size : (i + 1) * size] = piece[:, columns][None]
        for out, (start, width) in zip(outs[len(whose) :], rests):
            out[pl.ds(at, 1)] = pieces[k][:, start : start + width][None]


def split_columns(pieces, runs, scalars, whose=(False, True), width=None, rests=()):
    starts, size = runs
    per = len(pieces[0])
    rows = pieces[0][0].shape[0]
    count, step = len(pieces), rows // 2
    widths = [len(starts) * size] * len(whose) + [n for _, n in rests]
    outs = call(
        functools.partial(split_kernel, runs, count, per, whose, rests),
        "split_columns",
        (2,),
        [
            (a, (step, width or a.shape[1]), lambda r, s: (r, 0))
            for piece in pieces
            for a in piece
        ],
        [
            ((count, rows, n), pieces[0][0].dtype, (count, step, n), lambda r, s: (0, r, 0))
            for n in widths
        ],
        scalars,
    )
    return [out.reshape(count * rows, -1) for out in outs]


def place_kernel(runs, parts, skip, count, weighted, scalars, *refs):
    pieces, out = refs[: count * parts], refs[-1 - weighted]
    half = scalars[0]
    for k in range(count):

        @pl.when(pl.program_id(0) == k)
        def _():
            for p in range(parts):
                ref = pieces[k * parts + p]
                if runs is None:
                    out[0] = ref[:, skip:].astype(out.dtype)
                    continue
                starts, size = runs
                for i, pair in enumerate(starts):
                    first, second = pair[::-1] if p else pair
                    columns = aligned(first + half * (second - first), size)
                    out[0, :, columns] = ref[:, i * size : (i + 1) * size].astype(out.dtype)

    if weighted:
        products = out[0] * refs[count * parts][0].astype(jnp.float32)
        refs[-1][0] = jnp.sum(products, axis=-1, keepdims=True)


def place(pieces, scalars, rows, width, runs=None, skip=0, dtype=jnp.float32, weight=None):
    count, parts = len(pieces), len(pieces[0])
    total = weight.shape[0] if weight is not None else count
    cuts = 2 if rows * width > (1 << 19) else 1
    step = rows // cuts

    def spec(k, first):
        base = first // step
        return lambda j, r, s: (base + jnp.where(j == k, r, jnp.where(j < k, 0, cuts - 1)), 0)

    entry = lambda j, r, s: (s[1 + j], r, 0)
    inputs = [
        (a, (step, a.shape[1]), spec(k, first))
        for k, piece in enumerate(pieces)
        for a, first in piece
    ]
    outputs = [((total, rows, width), dtype, (1, step, width), entry)]
    if weight is not None:
        inputs.append((weight, (1, step, width), entry))
        outputs.append(((total, rows, 1), jnp.float32, (1, step, 1), entry))
    outs = call(
        functools.partial(place_kernel, runs, parts, skip, count, int(weight is not None)),
        "place",
        (count, cuts),
        inputs,
        outputs,
        scalars,
        share=8,
    )
    return outs[0] if weight is None else outs


def halves_rows(step, own):
    count = own.shape[0] // step
    return (
        lambda r, *s: (jnp.minimum(r, count - 1), 0),
        lambda r, *s: (jnp.maximum(r - count, 0), 0),
    )


def unit_of(values):
    inverse = lax.rsqrt(jnp.mean(values * values, axis=-1, keepdims=True) + EPSILON)
    return values * inverse, inverse


def spread(values, scratch, half, own, other):
    scratch[...] = values.astype(scratch.dtype)
    for a in range(own.shape[1] // LANES):
        own[:, a * LANES : (a + 1) * LANES] = scratch[:, aligned((2 * a + half) * LANES, LANES)]
        other[:, a * LANES : (a + 1) * LANES] = scratch[:, aligned((2 * a + 1 - half) * LANES, LANES)]


def gather(own, other, scratch, half):
    for a in range(own[0].shape[1] // LANES):
        block = slice(a * LANES, (a + 1) * LANES)
        scratch[:, aligned((2 * a + half) * LANES, LANES)] = own[0][:, block] + own[1][:, block]
        scratch[:, aligned((2 * a + 1 - half) * LANES, LANES)] = other[0][:, block] + other[1][:, block]
    return scratch[...]


def either(own_ref, got_ref):
    mine = pl.program_id(0) < pl.num_programs(0) // 2
    return jnp.where(mine, own_ref[...].astype(jnp.float32), got_ref[...].astype(jnp.float32))


def norm_kernel(scalars, own_rows, got_rows, gain, own, other, scratch):
    unit, _ = unit_of(either(own_rows, got_rows))
    spread(unit * gain[...], scratch, scalars[0], own, other)


def middle_kernel(scalars, own_rows, got_rows, branch, got_branch, gain, middle, own, other, scratch):
    values = either(own_rows, got_rows) + (branch[...] + got_branch[...])
    middle[...] = values
    unit, _ = unit_of(values)
    spread(unit * gain[...], scratch, scalars[0], own, other)


def pull(values, upstream, gain):
    unit, inverse = unit_of(values)
    scaled = upstream * gain
    inner = jnp.mean(scaled * unit, axis=-1, keepdims=True)
    return inverse * (scaled - unit * inner)


def middle_back_kernel(
    scalars, middle, own, other, got_own, got_other, own_up, got_up, gain, whole, low, scratch
):
    upstream = gather((own, got_other), (other, got_own), scratch, scalars[0])
    grad = pull(middle[...], upstream, gain[...]) + either(own_up, got_up)
    whole[...] = grad
    low[...] = grad.astype(low.dtype)


def input_back_kernel(
    scalars, rows, own, other, got_own, got_other, grad_middle, gain, out, scratch
):
    upstream = gather((own, got_other), (other, got_own), scratch, scalars[0])
    grad = pull(rows[...].astype(jnp.float32), upstream, gain[...])
    out[...] = (grad_middle[...] + grad).astype(out.dtype)


def softmax_of(query, keys, allowed):
    scores = jnp.where(allowed, by_columns(query, keys) * HEAD ** (-0.5), NEGATIVE)
    exponent = jnp.exp(scores - jnp.max(scores, axis=-1, keepdims=True))
    return exponent / jnp.sum(exponent, axis=-1, keepdims=True)


def frame_mask(positions, frames):
    count = positions * frames
    row = lax.broadcasted_iota(jnp.int32, (count, count), 0)
    column = lax.broadcasted_iota(jnp.int32, (count, count), 1)
    return (row % frames == column % frames) & (row >= column)


def attend_kernel(qkv_ref, mixed_ref):
    positions, frames, width = qkv_ref.shape
    count, third = positions * frames, width // 3
    allowed = frame_mask(positions, frames)
    lane = lax.broadcasted_iota(jnp.int32, (count, LANES), 1)
    for first in range(0, third, LANES):
        query, keys, values = (
            qkv_ref[:, :, part * third + first : part * third + first + LANES].reshape(count, LANES)
            for part in range(3)
        )
        mixed = jnp.zeros((count, LANES), jnp.float32)
        for start in range(0, LANES, HEAD):
            inside = (lane >= start) & (lane < start + HEAD)
            probs = softmax_of(jnp.where(inside, query, jnp.zeros_like(query)), keys, allowed)
            mixed = jnp.where(inside, plain(probs.astype(jnp.bfloat16), values), mixed)
        mixed_ref[:, :, first : first + LANES] = mixed.astype(mixed_ref.dtype).reshape(
            positions, frames, LANES
        )


def attend_back_kernel(qkv_ref, grad_ref, out_ref):
    positions, frames, width = qkv_ref.shape
    count, third = positions * frames, width // 3
    scale = HEAD ** (-0.5)
    allowed = frame_mask(positions, frames)
    lane = lax.broadcasted_iota(jnp.int32, (count, LANES), 1)
    for first in range(0, third, LANES):
        query, keys, values = (
            qkv_ref[:, :, part * third + first : part * third + first + LANES].reshape(count, LANES)
            for part in range(3)
        )
        upstream = grad_ref[:, :, first : first + LANES].reshape(count, LANES)
        grads = [jnp.zeros((count, LANES), jnp.float32)] * 3
        for start in range(0, LANES, HEAD):
            inside = (lane >= start) & (lane < start + HEAD)
            probs = softmax_of(jnp.where(inside, query, jnp.zeros_like(query)), keys, allowed)
            grad_probs = by_columns(jnp.where(inside, upstream, jnp.zeros_like(upstream)), values)
            inner = jnp.sum(probs * grad_probs, axis=-1, keepdims=True)
            grad_scores = (probs * (grad_probs - inner)).astype(jnp.bfloat16)
            new = (
                plain(grad_scores, keys) * scale,
                over_rows(grad_scores, query) * scale,
                over_rows(probs.astype(jnp.bfloat16), upstream),
            )
            grads = [jnp.where(inside, value, old) for value, old in zip(new, grads)]
        for part, grad in enumerate(grads):
            out_ref[:, :, part * third + first : part * third + first + LANES] = grad.astype(
                out_ref.dtype
            ).reshape(positions, frames, LANES)


def over_frames(kernel, out_width, *arrays):
    positions, frames, _ = arrays[0].shape
    step = min(frames, 256 // positions)
    return pl.pallas_call(
        kernel,
        grid=(frames // step,),
        in_specs=[
            pl.BlockSpec((positions, step, a.shape[2]), lambda i: (0, i, 0)) for a in arrays
        ],
        out_specs=pl.BlockSpec((positions, step, out_width), lambda i: (0, i, 0)),
        out_shape=jax.ShapeDtypeStruct((positions, frames, out_width), arrays[0].dtype),
        compiler_params=pltpu.CompilerParams(vmem_limit_bytes=48 << 20),
        cost_estimate=pl.CostEstimate(
            flops=0, transcendentals=0, bytes_accessed=0
        ),
        name=kernel.__name__,
    )(*arrays)


def spots_plan(
    frames_in,
    frame_valid,
    last_position,
    weight_qkv,
    weight_out,
    weight_ffn,
    weight_down,
    gain_attn,
    gain_ffn,
    grad_out,
):
    f32, bf16 = jnp.float32, jnp.bfloat16
    flow = Flow()
    frames, positions, depth = frames_in.shape
    spots, slice_rows = weight_qkv.shape[:2]
    plane, near = spots * 2, spots - 1
    spot, half = lax.axis_index("spot"), lax.axis_index("half")
    heads = head_runs(3 * depth, 3, spots)
    units = unit_runs(weight_ffn.shape[2], 2)
    hidden_units = weight_ffn.shape[2] // 2
    down_index = lax.axis_index(PLANE) % spots
    down_pairs = [
        [(f, (f % spots ^ k) * 2 + f // spots) for f in range(plane)] for k in range(spots)
    ]
    early = spots // 2
    by_spot = jnp.stack([half] + [spot ^ k for k in range(spots)]).astype(jnp.int32)
    by_slice = jnp.stack([half] + [down_index ^ k for k in range(spots)]).astype(jnp.int32)
    slot = lax.broadcasted_iota(jnp.int32, (frames, positions), 1)
    live = ((frame_valid[:, None] > 0) & (slot <= last_position[:, None]))[:, :, None]

    gains = jnp.pad(jnp.stack([gain_attn, gain_ffn], axis=2), ((0, 0), (0, 0), (0, LANES - 2)))
    parts = (weight_qkv, weight_out, gains, weight_ffn)
    widths = (3 * depth, depth, LANES, hidden_units)
    first = collect(parts, widths, jnp.concatenate([by_spot[:1], by_spot[2:]]))
    first = list(collect(parts, widths, by_spot[:2])) + [hop(p, k + 1, spots) for k, p in enumerate(first)]
    upstream = jnp.where(live, grad_out, jnp.zeros_like(grad_out))
    rows_in = jnp.concatenate([frames_in.swapaxes(0, 1), upstream.swapaxes(0, 1)], axis=1)
    own_rows = swap(rows_in, positions)
    ups = [pick(weight_ffn, spot ^ k)[:, hidden_units:] for k in range(spots)]
    third = [pick(weight_down, down_index ^ k) for k in range(spots)]
    tied = tie(*first, *ups, *third)
    first, ups, third = tied[:spots], tied[spots : 2 * spots], tied[2 * spots :]
    ups = [hop(piece, k, spots) for k, piece in enumerate(ups)]
    flow.send(UPS_NEAR, *ups[:near])
    flow.send(UPS_FAR, ups[near])
    own_rows, own_up = (
        own_rows[:, part * frames : (part + 1) * frames].reshape(-1, depth) for part in range(2)
    )
    got_rows, got_up = trade(own_rows), trade(own_up)

    own_count = own_rows.shape[0]
    count = own_count * 2
    step = own_count // 2
    pieces = [[piece] for piece in first]
    (qkv_sent,) = split_columns(pieces, heads, by_spot, (True,), 3 * depth)
    qkv_other = trade(qkv_sent)
    whole = 4 * depth + LANES
    qkv_own, full_out, gains = split_columns(
        pieces, heads, by_spot, (False,), whole, ((3 * depth, depth), (4 * depth, LANES))
    )
    gains = gains[:, :2]
    pair = [part.reshape(spots, slice_rows, 2) for part in (gains, trade(gains))]
    even, odd = (jnp.where(half == h, *pair) for h in range(2))
    gains = jnp.stack([even, odd], axis=1).reshape(depth, 2).T.astype(f32)
    gain_one, gain_two = gains[:1], gains[1:]
    mine, theirs = halves_rows(step, own_rows)
    straight = lambda r, *s: (r, 0)
    crossed = lambda r, *s: ((r + 2) % 4, 0)
    top = lambda r, *s: (0, 0)
    lower = lambda blocks, where: lambda *r: (where(*r)[0] + blocks, 0)
    rows = [(own_rows, (step, depth), mine), (got_rows, (step, depth), theirs)]
    split_rows = [((count, depth // 2), bf16, (step, depth // 2), straight)] * 2
    low_scratch, scratch = pltpu.VMEM((step, depth), bf16), pltpu.VMEM((step, depth), f32)
    one_own, one_other = call(
        norm_kernel, "norm", (4,), rows + [(gain_one, (1, depth), top)], split_rows, by_spot, [low_scratch]
    )
    qkv_rows = (plain(one_own, qkv_own) + plain(one_other, qkv_other)).astype(bf16)
    third = [lax.ppermute(p, PLANE, down_pairs[k]) for k, p in enumerate(third)]
    flow.send(THIRD_A, *third[:early])
    flow.send(THIRD_B, *third[early:])
    qkv = flow.at(AT_QKV_MOVED, swap(flow.at(AT_QKV, qkv_rows), positions))
    mixed = flow.at(AT_MIXED, over_frames(attend_kernel, depth // 2, qkv))
    mixed = flow.at(AT_MIXED_MOVED, swap(mixed, positions)).reshape(count, -1)
    branch = flow.at(AT_BRANCH, plain(mixed, full_out))
    got_branch = flow.at(AT_GOT_BRANCH, trade(branch))
    middle, two_own, two_other = call(
        middle_kernel,
        "middle",
        (4,),
        rows
        + [(branch, (step, depth), straight), (got_branch, (step, depth), crossed)]
        + [(gain_two, (1, depth), top)],
        [((count, depth), f32, (step, depth), straight)] + split_rows,
        by_spot,
        [low_scratch],
    )

    two_own, two_other = flow.at(AT_MIDDLE, two_own, two_other)
    ups = flow.take(UPS_NEAR, UPS_FAR)
    gate_run = tuple(start + whole for start in units[0][0])
    up_run = tuple(start - hidden_units for start in units[0][1])
    ffn_own, ffn_sent = split_columns(
        list(zip(first, ups)), ([gate_run, up_run], units[1]), by_spot
    )
    ffn_other = flow.at(AT_FFN_OTHER, trade(ffn_sent))
    gate_up = flow.at(AT_GATE_UP, plain(two_own, ffn_own) + plain(two_other, ffn_other))
    width = gate_up.shape[1] // 2
    gate, upward = gate_up[:, :width], gate_up[:, width:]
    gate_sig = jax.nn.sigmoid(gate)
    hidden = (gate * gate_sig * upward).astype(bf16)
    upstream = jnp.concatenate([own_up, got_up])
    down_grad = over_rows(hidden, upstream).astype(bf16).reshape(spots, -1, depth)
    down_sent = [pick(down_grad, spot ^ k) for k in range(spots)]
    down_back = [[(b, a) for a, b in pairs] for pairs in down_pairs]
    down_sent = [lax.ppermute(p, PLANE, pairs) for p, pairs in zip(down_sent, down_back)]
    flow.send(DOWN_A, *down_sent[::2])
    flow.send(DOWN_B, *down_sent[1::2])
    third = flow.take(THIRD_A, THIRD_B)
    full_down = place([[(piece, 0)] for piece in third], by_spot, *weight_down.shape[1:], dtype=bf16)
    full_down = full_down.reshape(-1, depth)

    grad_hidden = by_columns(upstream, full_down)
    grad_upward = grad_hidden * gate * gate_sig
    grad_gate = grad_hidden * upward * gate_sig * (1.0 + gate * (1.0 - gate_sig))
    grad_gate_up = jnp.concatenate([grad_gate, grad_upward], axis=-1).astype(bf16)
    back = jnp.concatenate([by_columns(grad_gate_up, ffn_own), by_columns(grad_gate_up, ffn_other)])
    back = flow.at(AT_BACK, back)
    got_back = trade(back)
    got_back = flow.at(AT_GOT_BACK, got_back)
    wide, narrow = (step, depth), (step, depth // 2)
    grad_middle, grad_branch = call(
        middle_back_kernel,
        "middle_back",
        (4,),
        [(middle, wide, straight), (back, narrow, straight), (back, narrow, lower(4, straight))]
        + [(got_back, narrow, crossed), (got_back, narrow, lower(4, crossed))]
        + [(own_up, wide, mine), (got_up, wide, theirs), (gain_two, (1, depth), top)],
        [
            ((count, depth), f32, wide, straight),
            ((count, depth), bf16, wide, straight),
        ],
        by_spot,
        [scratch],
    )

    cut = lambda grad: [pick(grad.reshape(spots, slice_rows, -1), spot ^ k) for k in range(spots)]
    grad_branch = flow.at(AT_GRAD_BRANCH, grad_branch)
    ffn_grad_own = cut(over_rows(two_own, grad_gate_up).astype(bf16))
    ffn_grad_got = cut(trade(over_rows(two_other, grad_gate_up).astype(bf16)))
    ffn_grad_own = [hop(piece, k, spots) for k, piece in enumerate(ffn_grad_own)]
    flow.send(OWN_NEAR, *ffn_grad_own[:near])
    flow.send(OWN_FAR, ffn_grad_own[near])
    late = [
        hop(jnp.concatenate(pair, axis=1), k, spots)
        for k, pair in enumerate(
            zip(ffn_grad_got, cut(over_rows(mixed, grad_branch).astype(bf16)))
        )
    ]
    flow.send(LATE_NEAR, *late[:near])
    flow.send(LATE_FAR, late[near])
    grad_mixed = flow.at(AT_GRAD_MIXED, by_columns(grad_branch, full_out).astype(bf16))
    grad_mixed_frames = flow.at(AT_GRAD_MIXED_MOVED, swap(grad_mixed, positions))
    grad_qkv = over_frames(attend_back_kernel, 3 * depth // 2, qkv, grad_mixed_frames)
    grad_qkv = flow.at(AT_GRAD_QKV, grad_qkv)
    result = plain(hidden, full_down)
    result = (middle[:own_count] + result[:own_count] + trade(result[own_count:])).astype(bf16)
    down_sent = [v for pair in zip(flow.take(DOWN_A), flow.take(DOWN_B)) for v in pair]
    flow.send(
        SUM_DOWN, place([[(piece, 0)] for piece in down_sent], by_slice, *weight_down.shape[1:])
    )
    grad_qkv_rows = swap(grad_qkv, positions).reshape(count, -1)
    grad_qkv_rows = flow.at(AT_GRAD_QKV_MOVED, grad_qkv_rows)
    grad_qkv_rows, result = tie(grad_qkv_rows, result)
    flow.send(RESULT, rows_from_spots(result, positions))
    qkv_grad_got = trade(over_rows(one_other, grad_qkv_rows).astype(bf16))
    qkv_grad_own = flow.at(AT_QKV_GRAD, over_rows(one_own, grad_qkv_rows).astype(bf16))
    qkv_sent = [jnp.concatenate(pair) for pair in zip(cut(qkv_grad_own), cut(qkv_grad_got))]
    *qkv_sent, grad_qkv_rows = tie(*qkv_sent, grad_qkv_rows)
    qkv_sent = [hop(piece, k, spots) for k, piece in enumerate(qkv_sent)]
    flow.send(QKV_NEAR, *qkv_sent[:near])
    flow.send(QKV_FAR, qkv_sent[near])
    back_own = by_columns(grad_qkv_rows, qkv_own)
    back_other = by_columns(grad_qkv_rows, qkv_other)
    back_own, back_other = flow.at(AT_LAST_BACK, back_own, back_other)
    ffn_grad_own, late = flow.take(OWN_NEAR, OWN_FAR), flow.take(LATE_NEAR, LATE_FAR)
    sum_ffn, term_ffn = place(
        [[(own, 0), (got, 0)] for own, got in zip(ffn_grad_own, late)],
        by_spot,
        slice_rows,
        2 * hidden_units,
        units,
        weight=weight_ffn,
    )
    sum_out = place([[(piece, 0)] for piece in late], by_spot, slice_rows, depth, skip=hidden_units)
    flow.send(SUMS, sum_ffn, sum_out)
    got_back = trade(jnp.concatenate([back_own[own_count:], back_other[own_count:]]))
    got_back = flow.at(AT_GOT_LAST, got_back)
    (grad_rows,) = call(
        input_back_kernel,
        "input_back",
        (2,),
        [(own_rows, wide, straight), (back_own, narrow, straight), (back_other, narrow, straight)]
        + [(got_back, narrow, straight), (got_back, narrow, lower(2, straight))]
        + [(grad_middle, wide, straight), (gain_one, (1, depth), top)],
        [((own_count, depth), bf16, wide, straight)],
        by_spot,
        [scratch],
    )
    grad_rows = flow.at(AT_GRAD_ROWS, grad_rows)
    grad_input = flow.at(AT_GRAD_INPUT, rows_from_spots(grad_rows, positions))
    (result,) = flow.take(RESULT)
    output = jnp.where(live, result, jnp.zeros_like(result))
    qkv_sent = flow.take(QKV_NEAR, QKV_FAR)
    qkv_sent[near] = flow.at(AT_QKV_FAR, qkv_sent[near])
    sum_ffn, sum_out = flow.take(SUMS)
    (sum_down,) = flow.take(SUM_DOWN)
    sum_qkv, term_attn = place(
        [[(piece, 0), (piece, slice_rows)] for piece in qkv_sent],
        by_spot,
        slice_rows,
        3 * depth,
        heads,
        weight=weight_qkv,
    )
    gain_terms = [
        term.reshape(spots, slice_rows) / gain.astype(f32)
        for term, gain in ((term_attn, gain_attn), (term_ffn, gain_ffn))
    ]
    return (output, grad_input, sum_qkv, sum_out, sum_ffn, sum_down, *gain_terms)


def solution(mesh):
    plane, lines = mesh.shape["frames"], mesh.shape["pos"]

    def run(*arrays):
        positions, depth = arrays[0].shape[1:]
        spots = positions // lines
        slice_rows = depth // plane
        shares = arrays[5].shape[2] // 4
        fits = plane == 2 * spots and spots & (spots - 1) == 0
        fits = fits and slice_rows % LANES == 0 and shares % LANES == 0
        if fits:
            inner = Mesh(mesh.devices.reshape(spots, 2, lines), PLANE + ("pos",))
            by_frame, weight, plan = P(PLANE + ("pos",)), P("pos", PLANE), spots_plan
        else:
            inner, plan = mesh, gathered_plan
            by_frame, weight = P(("frames", "pos")), P("pos", "frames")
        return jax.shard_map(
            plan,
            mesh=inner,
            in_specs=(by_frame,) * 3 + (weight,) * 6 + (by_frame,),
            out_specs=(by_frame,) * 2 + (weight,) * 6,
            check_vma=False,
        )(*arrays)

    return run
```

```python
import functools

import jax
import jax.numpy as jnp
from jax import lax
from jax.experimental import pallas as pl
from jax.experimental.pallas import tpu as pltpu
from jax.sharding import Mesh, PartitionSpec as P

HEADS = 16
HEAD = 64
LANES = 128
EPSILON = 1e-06
NEGATIVE = -1e30


def rms_forward(values, gain_row):
    inverse = lax.rsqrt(jnp.mean(values * values, axis=-1, keepdims=True) + EPSILON)
    normed = values * inverse
    return (normed * gain_row[None], normed, inverse)


def rms_backward(upstream, normed, inverse, gain_row):
    scaled = upstream * gain_row[None]
    row_inner = jnp.mean(scaled * normed, axis=-1, keepdims=True)
    return (inverse * (scaled - normed * row_inner), jnp.sum(upstream * normed, axis=0))


def project(pattern, left_side, right_side):
    return jnp.einsum(pattern, left_side, right_side, preferred_element_type=jnp.float32)


def split_heads(qkv_frames):
    frames = qkv_frames.shape[0]
    length = qkv_frames.shape[1]
    pieces = qkv_frames.reshape(frames, length, 3, HEADS, HEAD)
    return (pieces[:, :, 0], pieces[:, :, 1], pieces[:, :, 2])


def masked_scores(query, key_part):
    raw_scores = project("fqhe,fkhe->fhqk", query, key_part) * HEAD ** (-0.5)
    length = raw_scores.shape[-1]
    allowed = lax.broadcasted_iota(jnp.int32, (length, length), 0) >= lax.broadcasted_iota(
        jnp.int32, (length, length), 1
    )
    return jnp.where(allowed, raw_scores, NEGATIVE)


def gathered_plan(
    frames_in,
    frame_valid,
    last_position,
    weight_qkv,
    weight_out,
    weight_ffn,
    weight_down,
    gain_attn,
    gain_ffn,
    grad_out,
):
    scale = HEAD ** (-0.5)
    slot_index = lax.broadcasted_iota(jnp.int32, (frames_in.shape[0], frames_in.shape[1]), 1)
    live_mask = (frame_valid[:, None] > 0) & (slot_index <= last_position[:, None])
    pos_rows = lax.all_to_all(frames_in, "pos", split_axis=1, concat_axis=0, tiled=True)
    full_qkv, full_out, full_gain_a = (
        lax.all_gather(weight_qkv, "frames", axis=1, tiled=True),
        lax.all_gather(weight_out, "frames", axis=1, tiled=True),
        lax.all_gather(gain_attn, "frames", axis=1, tiled=True),
    )
    gain_one = full_gain_a.astype(jnp.float32)
    residual = pos_rows.astype(jnp.float32)
    scaled_one, normed_one, inverse_one = rms_forward(residual, gain_one)
    normed_one_low = scaled_one.astype(jnp.bfloat16)
    qkv_rows = project("rpd,pde->rpe", normed_one_low, full_qkv).astype(jnp.bfloat16)
    qkv_frames = lax.all_to_all(qkv_rows, "pos", split_axis=0, concat_axis=1, tiled=True)
    query, key_part, value_part = split_heads(qkv_frames)
    scores = masked_scores(query, key_part)
    row_top = jnp.max(scores, axis=-1, keepdims=True)
    exponent = jnp.exp(scores - row_top)
    row_total = jnp.sum(exponent, axis=-1, keepdims=True)
    log_total = row_top + jnp.log(row_total)
    attend_low = (exponent / row_total).astype(jnp.bfloat16)
    mixed_heads = project("fhqk,fkhe->fqhe", attend_low, value_part)
    mixed_low = mixed_heads.reshape(frames_in.shape).astype(jnp.bfloat16)
    mixed_rows = lax.all_to_all(mixed_low, "pos", split_axis=1, concat_axis=0, tiled=True)
    middle = residual + project("rpd,pde->rpe", mixed_rows, full_out)
    full_ffn, full_down, full_gain_f = (
        lax.all_gather(weight_ffn, "frames", axis=1, tiled=True),
        lax.all_gather(weight_down, "frames", axis=1, tiled=True),
        lax.all_gather(gain_ffn, "frames", axis=1, tiled=True),
    )
    gain_two = full_gain_f.astype(jnp.float32)
    scaled_two, normed_two, inverse_two = rms_forward(middle, gain_two)
    normed_two_low = scaled_two.astype(jnp.bfloat16)
    gate_up = project("rpd,pde->rpe", normed_two_low, full_ffn)
    width = gate_up.shape[-1] // 2
    gate = gate_up[..., :width]
    upward = gate_up[..., width:]
    gate_sig = jax.nn.sigmoid(gate)
    hidden = (gate * gate_sig * upward).astype(jnp.bfloat16)
    result = middle + project("rpf,pfd->rpd", hidden, full_down)
    result_frames = lax.all_to_all(
        result.astype(jnp.bfloat16), "pos", split_axis=0, concat_axis=1, tiled=True
    )
    output = jnp.where(live_mask[:, :, None], result_frames, jnp.zeros_like(result_frames))
    upstream = jnp.where(live_mask[:, :, None], grad_out, jnp.zeros_like(grad_out))
    upstream_rows = lax.all_to_all(upstream, "pos", split_axis=1, concat_axis=0, tiled=True)
    back_ffn, back_down = (
        lax.all_gather(weight_ffn, "frames", axis=1, tiled=True),
        lax.all_gather(weight_down, "frames", axis=1, tiled=True),
    )
    grad_hidden = project("rpd,pfd->rpf", upstream_rows, back_down)
    term_down = project("rpf,rpd->pfd", hidden, upstream_rows)
    grad_upward = grad_hidden * gate * gate_sig
    grad_gate = grad_hidden * upward * gate_sig * (1.0 + gate * (1.0 - gate_sig))
    grad_gate_up = jnp.concatenate([grad_gate, grad_upward], axis=-1).astype(jnp.bfloat16)
    grad_normed_two = project("rpe,pde->rpd", grad_gate_up, back_ffn)
    term_ffn = project("rpd,rpe->pde", normed_two_low, grad_gate_up)
    grad_middle_norm, term_gain_f = rms_backward(grad_normed_two, normed_two, inverse_two, gain_two)
    grad_middle = upstream_rows.astype(jnp.float32) + grad_middle_norm
    sum_ffn, sum_down, sum_gain_f = (
        lax.psum_scatter(
            term_ffn.astype(jnp.bfloat16), "frames", scatter_dimension=1, tiled=True
        ).astype(jnp.float32),
        lax.psum_scatter(
            term_down.astype(jnp.bfloat16), "frames", scatter_dimension=1, tiled=True
        ).astype(jnp.float32),
        lax.psum_scatter(
            term_gain_f.astype(jnp.bfloat16), "frames", scatter_dimension=1, tiled=True
        ).astype(jnp.float32),
    )
    back_qkv, back_out = (
        lax.all_gather(weight_qkv, "frames", axis=1, tiled=True),
        lax.all_gather(weight_out, "frames", axis=1, tiled=True),
    )
    grad_branch = grad_middle.astype(jnp.bfloat16)
    grad_mixed = project("rpe,pde->rpd", grad_branch, back_out).astype(jnp.bfloat16)
    term_out = project("rpd,rpe->pde", mixed_rows, grad_branch)
    grad_mixed_frames = lax.all_to_all(grad_mixed, "pos", split_axis=0, concat_axis=1, tiled=True)
    grad_heads = grad_mixed_frames.reshape(query.shape)
    again_scores = masked_scores(query, key_part)
    attend = jnp.exp(again_scores - log_total)
    grad_value = project("fhqk,fqhe->fkhe", attend.astype(jnp.bfloat16), grad_heads)
    grad_attend = project("fqhe,fkhe->fhqk", grad_heads, value_part)
    row_inner = jnp.sum(attend * grad_attend, axis=-1, keepdims=True)
    grad_scores = (attend * (grad_attend - row_inner)).astype(jnp.bfloat16)
    grad_query = project("fhqk,fkhe->fqhe", grad_scores, key_part) * scale
    grad_key = project("fhqk,fqhe->fkhe", grad_scores, query) * scale
    grad_qkv_frames = (
        jnp.stack([grad_query, grad_key, grad_value], axis=2)
        .reshape(qkv_frames.shape)
        .astype(jnp.bfloat16)
    )
    grad_qkv_rows = lax.all_to_all(grad_qkv_frames, "pos", split_axis=1, concat_axis=0, tiled=True)
    grad_normed_one = project("rpe,pde->rpd", grad_qkv_rows, back_qkv)
    term_qkv = project("rpd,rpe->pde", normed_one_low, grad_qkv_rows)
    grad_input_norm, term_gain_a = rms_backward(grad_normed_one, normed_one, inverse_one, gain_one)
    grad_rows = (grad_middle + grad_input_norm).astype(jnp.bfloat16)
    grad_frames = lax.all_to_all(grad_rows, "pos", split_axis=0, concat_axis=1, tiled=True)
    sum_qkv, sum_out, sum_gain_a = (
        lax.psum_scatter(
            term_qkv.astype(jnp.bfloat16), "frames", scatter_dimension=1, tiled=True
        ).astype(jnp.float32),
        lax.psum_scatter(
            term_out.astype(jnp.bfloat16), "frames", scatter_dimension=1, tiled=True
        ).astype(jnp.float32),
        lax.psum_scatter(
            term_gain_a.astype(jnp.bfloat16), "frames", scatter_dimension=1, tiled=True
        ).astype(jnp.float32),
    )
    return (output, grad_frames, sum_qkv, sum_out, sum_ffn, sum_down, sum_gain_a, sum_gain_f)


ROWS = ("pos", "spot")
PLANE = ("spot", "half")


def plain(left, right):
    return lax.dot_general(left, right, (((1,), (0,)), ((), ())), preferred_element_type=jnp.float32)


def by_columns(left, right):
    return lax.dot_general(left, right, (((1,), (1,)), ((), ())), preferred_element_type=jnp.float32)


def over_rows(left, right):
    return lax.dot_general(left, right, (((0,), (0,)), ((), ())), preferred_element_type=jnp.float32)


def tie(*values):
    return lax.optimization_barrier(values)


(
    UPS_NEAR, UPS_FAR, THIRD_A, THIRD_B, DOWN_A, DOWN_B, OWN_NEAR, OWN_FAR, LATE_NEAR, LATE_FAR,
    QKV_NEAR, QKV_FAR, RESULT, SUMS, SUM_DOWN,
) = range(15)
(
    AT_QKV_MOVED, AT_QKV, AT_MIXED, AT_MIXED_MOVED, AT_BRANCH, AT_GOT_BRANCH, AT_MIDDLE,
    AT_FFN_OTHER, AT_GATE_UP, AT_BACK, AT_GOT_BACK, AT_GRAD_BRANCH, AT_GRAD_MIXED,
    AT_GRAD_MIXED_MOVED, AT_GRAD_QKV, AT_GRAD_QKV_MOVED, AT_QKV_GRAD, AT_LAST_BACK, AT_GOT_LAST,
    AT_GRAD_ROWS, AT_GRAD_INPUT, AT_QKV_FAR,
) = range(22)
DUE = {
    UPS_NEAR: AT_QKV,
    UPS_FAR: None,
    THIRD_A: AT_QKV_MOVED,
    THIRD_B: AT_GATE_UP,
    DOWN_A: AT_GRAD_MIXED_MOVED,
    DOWN_B: AT_GRAD_BRANCH,
    OWN_NEAR: AT_GRAD_QKV,
    OWN_FAR: AT_QKV_GRAD,
    LATE_NEAR: AT_LAST_BACK,
    LATE_FAR: AT_QKV_GRAD,
    QKV_NEAR: None,
    QKV_FAR: None,
    RESULT: AT_LAST_BACK,
    SUMS: AT_GRAD_ROWS,
    SUM_DOWN: None,
}


class Flow:
    def __init__(self):
        self.moving = {}

    def send(self, name, *values):
        self.moving[name] = values

    def at(self, point, *values):
        names = [name for name in self.moving if DUE[name] == point]
        if names:
            tied = tie(*values, *[v for name in names for v in self.moving[name]])
            values, rest = tied[: len(values)], tied[len(values) :]
            for name in names:
                size = len(self.moving[name])
                self.moving[name], rest = rest[:size], rest[size:]
        return values if len(values) > 1 else values[0]

    def take(self, *names):
        return [v for name in names for v in self.moving[name]]


def pick(stack, index):
    return lax.dynamic_index_in_dim(stack, index, 0, keepdims=False)


def hop(value, k, spots):
    return value if k == 0 else lax.ppermute(value, "spot", [(i, i ^ k) for i in range(spots)])


def trade(value):
    return lax.ppermute(value, "half", [(0, 1), (1, 0)])


def swap(values, blocks):
    return lax.all_to_all(
        values.reshape(blocks, -1, values.shape[-1]), ROWS, split_axis=0, concat_axis=0, tiled=True
    )


def rows_from_spots(values, blocks):
    return swap(values, blocks).swapaxes(0, 1)


def head_runs(width, groups, spots):
    size = width // groups // spots // 2
    return [((g * spots + a) * 2 * size, ((g * spots + a) * 2 + 1) * size) for g in range(groups) for a in range(spots)], size


def unit_runs(width, groups):
    size = width // groups // 2
    return [(g * 2 * size, (g * 2 + 1) * size) for g in range(groups)], size


def call(kernel, name, grid, inputs, outputs, scalars, scratch=(), share=8):
    moved = sum(a.size * a.dtype.itemsize for a, _, _ in inputs)
    return pl.pallas_call(
        kernel,
        grid_spec=pltpu.PrefetchScalarGridSpec(
            num_scalar_prefetch=1,
            grid=grid,
            in_specs=[pl.BlockSpec(block, where) for _, block, where in inputs],
            out_specs=[pl.BlockSpec(block, where) for _, _, block, where in outputs],
            scratch_shapes=list(scratch),
        ),
        out_shape=[jax.ShapeDtypeStruct(shape, dtype) for shape, dtype, _, _ in outputs],
        compiler_params=pltpu.CompilerParams(vmem_limit_bytes=48 << 20),
        cost_estimate=pl.CostEstimate(flops=0, transcendentals=0, bytes_accessed=moved // share),
        name=name,
    )(scalars, *[a for a, _, _ in inputs])


def aligned(start, size):
    return pl.ds(pl.multiple_of(start, LANES), size)


def collect_kernel(widths, scalars, *refs):
    parts, outs = refs[: len(widths)], refs[len(widths) :]
    for k, out in enumerate(outs):

        @pl.when(pl.program_id(0) == k)
        def _():
            start = 0
            for part, width in zip(parts, widths):
                out[:, start : start + width] = part[0]
                start += width


def collect(parts, widths, scalars):
    count, rows = scalars.shape[0] - 1, parts[0].shape[1]
    cuts = 4
    step, width = rows // cuts, sum(widths)

    def spec(k):
        return lambda j, r, s: (jnp.where(j == k, r, jnp.where(j < k, 0, cuts - 1)), 0)

    return call(
        functools.partial(collect_kernel, widths),
        "collect",
        (count, cuts),
        [(a, (1, step, n), lambda j, r, s: (s[1 + j], r, 0)) for a, n in zip(parts, widths)],
        [((rows, width), parts[0].dtype, (step, width), spec(k)) for k in range(count)],
        scalars,
    )


def split_kernel(runs, count, per, whose, rests, scalars, *refs):
    starts, size = runs
    pieces, outs = refs[: count * per], refs[count * per :]
    half = scalars[0]
    for k in range(count):
        at = scalars[1 + k]
        for i, pair in enumerate(starts):
            piece = pieces[k * per + (i if per > 1 else 0)]
            for out, other in zip(outs, whose):
                first, second = pair[::-1] if other else pair
                columns = aligned(first + half * (second - first), size)
                out[pl.ds(at, 1), :, i * size : (i + 1) * size] = piece[:, columns][None]
        for out, (start, width) in zip(outs[len(whose) :], rests):
            out[pl.ds(at, 1)] = pieces[k][:, start : start + width][None]


def split_columns(pieces, runs, scalars, whose=(False, True), width=None, rests=()):
    starts, size = runs
    per = len(pieces[0])
    rows = pieces[0][0].shape[0]
    count, step = len(pieces), rows // 2
    widths = [len(starts) * size] * len(whose) + [n for _, n in rests]
    outs = call(
        functools.partial(split_kernel, runs, count, per, whose, rests),
        "split_columns",
        (2,),
        [
            (a, (step, width or a.shape[1]), lambda r, s: (r, 0))
            for piece in pieces
            for a in piece
        ],
        [
            ((count, rows, n), pieces[0][0].dtype, (count, step, n), lambda r, s: (0, r, 0))
            for n in widths
        ],
        scalars,
    )
    return [out.reshape(count * rows, -1) for out in outs]


def place_kernel(runs, parts, skip, count, weighted, scalars, *refs):
    pieces, out = refs[: count * parts], refs[-1 - weighted]
    half = scalars[0]
    for k in range(count):

        @pl.when(pl.program_id(0) == k)
        def _():
            for p in range(parts):
                ref = pieces[k * parts + p]
                if runs is None:
                    out[0] = ref[:, skip:].astype(out.dtype)
                    continue
                starts, size = runs
                for i, pair in enumerate(starts):
                    first, second = pair[::-1] if p else pair
                    columns = aligned(first + half * (second - first), size)
                    out[0, :, columns] = ref[:, i * size : (i + 1) * size].astype(out.dtype)

    if weighted:
        products = out[0] * refs[count * parts][0].astype(jnp.float32)
        refs[-1][0] = jnp.sum(products, axis=-1, keepdims=True)


def place(pieces, scalars, rows, width, runs=None, skip=0, dtype=jnp.float32, weight=None):
    count, parts = len(pieces), len(pieces[0])
    total = weight.shape[0] if weight is not None else count
    cuts = 2 if rows * width > (1 << 19) else 1
    step = rows // cuts

    def spec(k, first):
        base = first // step
        return lambda j, r, s: (base + jnp.where(j == k, r, jnp.where(j < k, 0, cuts - 1)), 0)

    entry = lambda j, r, s: (s[1 + j], r, 0)
    inputs = [
        (a, (step, a.shape[1]), spec(k, first))
        for k, piece in enumerate(pieces)
        for a, first in piece
    ]
    outputs = [((total, rows, width), dtype, (1, step, width), entry)]
    if weight is not None:
        inputs.append((weight, (1, step, width), entry))
        outputs.append(((total, rows, 1), jnp.float32, (1, step, 1), entry))
    outs = call(
        functools.partial(place_kernel, runs, parts, skip, count, int(weight is not None)),
        "place",
        (count, cuts),
        inputs,
        outputs,
        scalars,
        share=8,
    )
    return outs[0] if weight is None else outs


def halves_rows(step, own):
    count = own.shape[0] // step
    return (
        lambda r, *s: (jnp.minimum(r, count - 1), 0),
        lambda r, *s: (jnp.maximum(r - count, 0), 0),
    )


def unit_of(values):
    inverse = lax.rsqrt(jnp.mean(values * values, axis=-1, keepdims=True) + EPSILON)
    return values * inverse, inverse


def spread(values, scratch, half, own, other):
    scratch[...] = values.astype(scratch.dtype)
    for a in range(own.shape[1] // LANES):
        own[:, a * LANES : (a + 1) * LANES] = scratch[:, aligned((2 * a + half) * LANES, LANES)]
        other[:, a * LANES : (a + 1) * LANES] = scratch[:, aligned((2 * a + 1 - half) * LANES, LANES)]


def gather(own, other, scratch, half):
    for a in range(own[0].shape[1] // LANES):
        block = slice(a * LANES, (a + 1) * LANES)
        scratch[:, aligned((2 * a + half) * LANES, LANES)] = own[0][:, block] + own[1][:, block]
        scratch[:, aligned((2 * a + 1 - half) * LANES, LANES)] = other[0][:, block] + other[1][:, block]
    return scratch[...]


def either(own_ref, got_ref):
    mine = pl.program_id(0) < pl.num_programs(0) // 2
    return jnp.where(mine, own_ref[...].astype(jnp.float32), got_ref[...].astype(jnp.float32))


def norm_kernel(scalars, own_rows, got_rows, gain, own, other, scratch):
    unit, _ = unit_of(either(own_rows, got_rows))
    spread(unit * gain[...], scratch, scalars[0], own, other)


def middle_kernel(scalars, own_rows, got_rows, branch, got_branch, gain, middle, own, other, scratch):
    values = either(own_rows, got_rows) + (branch[...] + got_branch[...])
    middle[...] = values
    unit, _ = unit_of(values)
    spread(unit * gain[...], scratch, scalars[0], own, other)


def pull(values, upstream, gain):
    unit, inverse = unit_of(values)
    scaled = upstream * gain
    inner = jnp.mean(scaled * unit, axis=-1, keepdims=True)
    return inverse * (scaled - unit * inner)


def middle_back_kernel(
    scalars, middle, own, other, got_own, got_other, own_up, got_up, gain, whole, low, scratch
):
    upstream = gather((own, got_other), (other, got_own), scratch, scalars[0])
    grad = pull(middle[...], upstream, gain[...]) + either(own_up, got_up)
    low[...] = grad.astype(low.dtype)

    @pl.when(pl.program_id(0) < pl.num_programs(0) // 2)
    def _():
        whole[...] = grad


def input_back_kernel(
    scalars, rows, own, other, got_own, got_other, grad_middle, gain, out, scratch
):
    upstream = gather((own, got_other), (other, got_own), scratch, scalars[0])
    grad = pull(rows[...].astype(jnp.float32), upstream, gain[...])
    out[...] = (grad_middle[...] + grad).astype(out.dtype)


def softmax_of(query, keys, allowed):
    scores = jnp.where(allowed, by_columns(query, keys) * HEAD ** (-0.5), NEGATIVE)
    exponent = jnp.exp(scores - jnp.max(scores, axis=-1, keepdims=True))
    return exponent / jnp.sum(exponent, axis=-1, keepdims=True)


def frame_mask(positions, frames):
    count = positions * frames
    row = lax.broadcasted_iota(jnp.int32, (count, count), 0)
    column = lax.broadcasted_iota(jnp.int32, (count, count), 1)
    return (row % frames == column % frames) & (row >= column)


def attend_kernel(qkv_ref, mixed_ref):
    positions, frames, width = qkv_ref.shape
    count, third = positions * frames, width // 3
    allowed = frame_mask(positions, frames)
    lane = lax.broadcasted_iota(jnp.int32, (count, LANES), 1)
    for first in range(0, third, LANES):
        query, keys, values = (
            qkv_ref[:, :, part * third + first : part * third + first + LANES].reshape(count, LANES)
            for part in range(3)
        )
        mixed = jnp.zeros((count, LANES), jnp.float32)
        for start in range(0, LANES, HEAD):
            inside = (lane >= start) & (lane < start + HEAD)
            probs = softmax_of(jnp.where(inside, query, jnp.zeros_like(query)), keys, allowed)
            mixed = jnp.where(inside, plain(probs.astype(jnp.bfloat16), values), mixed)
        mixed_ref[:, :, first : first + LANES] = mixed.astype(mixed_ref.dtype).reshape(
            positions, frames, LANES
        )


def attend_back_kernel(qkv_ref, grad_ref, out_ref):
    positions, frames, width = qkv_ref.shape
    count, third = positions * frames, width // 3
    scale = HEAD ** (-0.5)
    allowed = frame_mask(positions, frames)
    lane = lax.broadcasted_iota(jnp.int32, (count, LANES), 1)
    for first in range(0, third, LANES):
        query, keys, values = (
            qkv_ref[:, :, part * third + first : part * third + first + LANES].reshape(count, LANES)
            for part in range(3)
        )
        upstream = grad_ref[:, :, first : first + LANES].reshape(count, LANES)
        grads = [jnp.zeros((count, LANES), jnp.float32)] * 3
        for start in range(0, LANES, HEAD):
            inside = (lane >= start) & (lane < start + HEAD)
            probs = softmax_of(jnp.where(inside, query, jnp.zeros_like(query)), keys, allowed)
            grad_probs = by_columns(jnp.where(inside, upstream, jnp.zeros_like(upstream)), values)
            inner = jnp.sum(probs * grad_probs, axis=-1, keepdims=True)
            grad_scores = (probs * (grad_probs - inner)).astype(jnp.bfloat16)
            new = (
                plain(grad_scores, keys) * scale,
                over_rows(grad_scores, query) * scale,
                over_rows(probs.astype(jnp.bfloat16), upstream),
            )
            grads = [jnp.where(inside, value, old) for value, old in zip(new, grads)]
        for part, grad in enumerate(grads):
            out_ref[:, :, part * third + first : part * third + first + LANES] = grad.astype(
                out_ref.dtype
            ).reshape(positions, frames, LANES)


def over_frames(kernel, out_width, *arrays):
    positions, frames, _ = arrays[0].shape
    step = min(frames, 256 // positions)
    return pl.pallas_call(
        kernel,
        grid=(frames // step,),
        in_specs=[
            pl.BlockSpec((positions, step, a.shape[2]), lambda i: (0, i, 0)) for a in arrays
        ],
        out_specs=pl.BlockSpec((positions, step, out_width), lambda i: (0, i, 0)),
        out_shape=jax.ShapeDtypeStruct((positions, frames, out_width), arrays[0].dtype),
        compiler_params=pltpu.CompilerParams(vmem_limit_bytes=48 << 20),
        cost_estimate=pl.CostEstimate(
            flops=0, transcendentals=0, bytes_accessed=0
        ),
        name=kernel.__name__,
    )(*arrays)


def spots_plan(
    frames_in,
    frame_valid,
    last_position,
    weight_qkv,
    weight_out,
    weight_ffn,
    weight_down,
    gain_attn,
    gain_ffn,
    grad_out,
):
    f32, bf16 = jnp.float32, jnp.bfloat16
    flow = Flow()
    frames, positions, depth = frames_in.shape
    spots, slice_rows = weight_qkv.shape[:2]
    plane, near = spots * 2, spots - 1
    spot, half = lax.axis_index("spot"), lax.axis_index("half")
    heads = head_runs(3 * depth, 3, spots)
    units = unit_runs(weight_ffn.shape[2], 2)
    hidden_units = weight_ffn.shape[2] // 2
    down_index = lax.axis_index(PLANE) % spots
    down_pairs = [
        [(f, (f % spots ^ k) * 2 + f // spots) for f in range(plane)] for k in range(spots)
    ]
    early = spots // 2
    by_spot = jnp.stack([half] + [spot ^ k for k in range(spots)]).astype(jnp.int32)
    by_slice = jnp.stack([half] + [down_index ^ k for k in range(spots)]).astype(jnp.int32)
    slot = lax.broadcasted_iota(jnp.int32, (frames, positions), 1)
    live = ((frame_valid[:, None] > 0) & (slot <= last_position[:, None]))[:, :, None]

    gains = jnp.pad(jnp.stack([gain_attn, gain_ffn], axis=2), ((0, 0), (0, 0), (0, LANES - 2)))
    parts = (weight_qkv, weight_out, gains, weight_ffn)
    widths = (3 * depth, depth, LANES, hidden_units)
    first = collect(parts, widths, jnp.concatenate([by_spot[:1], by_spot[2:]]))
    first = list(collect(parts, widths, by_spot[:2])) + [hop(p, k + 1, spots) for k, p in enumerate(first)]
    upstream = jnp.where(live, grad_out, jnp.zeros_like(grad_out))
    rows_in = jnp.concatenate([frames_in.swapaxes(0, 1), upstream.swapaxes(0, 1)], axis=1)
    own_rows = swap(rows_in, positions)
    ups = [pick(weight_ffn, spot ^ k)[:, hidden_units:] for k in range(spots)]
    third = [pick(weight_down, down_index ^ k) for k in range(spots)]
    tied = tie(*first, *ups, *third)
    first, ups, third = tied[:spots], tied[spots : 2 * spots], tied[2 * spots :]
    ups = [hop(piece, k, spots) for k, piece in enumerate(ups)]
    flow.send(UPS_NEAR, *ups[:near])
    flow.send(UPS_FAR, ups[near])
    own_rows, own_up = (
        own_rows[:, part * frames : (part + 1) * frames].reshape(-1, depth) for part in range(2)
    )
    got_rows, got_up = trade(own_rows), trade(own_up)

    own_count = own_rows.shape[0]
    count = own_count * 2
    step = own_count // 2
    pieces = [[piece] for piece in first]
    (qkv_sent,) = split_columns(pieces, heads, by_spot, (True,), 3 * depth)
    qkv_other = trade(qkv_sent)
    whole = 4 * depth + LANES
    qkv_own, full_out, gains = split_columns(
        pieces, heads, by_spot, (False,), whole, ((3 * depth, depth), (4 * depth, LANES))
    )
    gains = gains[:, :2]
    pair = [part.reshape(spots, slice_rows, 2) for part in (gains, trade(gains))]
    even, odd = (jnp.where(half == h, *pair) for h in range(2))
    gains = jnp.stack([even, odd], axis=1).reshape(depth, 2).T.astype(f32)
    gain_one, gain_two = gains[:1], gains[1:]
    mine, theirs = halves_rows(step, own_rows)
    straight = lambda r, *s: (r, 0)
    crossed = lambda r, *s: ((r + 2) % 4, 0)
    top = lambda r, *s: (0, 0)
    lower = lambda blocks, where: lambda *r: (where(*r)[0] + blocks, 0)
    rows = [(own_rows, (step, depth), mine), (got_rows, (step, depth), theirs)]
    split_rows = [((count, depth // 2), bf16, (step, depth // 2), straight)] * 2
    low_scratch, scratch = pltpu.VMEM((step, depth), bf16), pltpu.VMEM((step, depth), f32)
    one_own, one_other = call(
        norm_kernel, "norm", (4,), rows + [(gain_one, (1, depth), top)], split_rows, by_spot, [low_scratch]
    )
    qkv_rows = (plain(one_own, qkv_own) + plain(one_other, qkv_other)).astype(bf16)
    third = [lax.ppermute(p, PLANE, down_pairs[k]) for k, p in enumerate(third)]
    flow.send(THIRD_A, *third[:early])
    flow.send(THIRD_B, *third[early:])
    qkv = flow.at(AT_QKV_MOVED, swap(flow.at(AT_QKV, qkv_rows), positions))
    mixed = flow.at(AT_MIXED, over_frames(attend_kernel, depth // 2, qkv))
    mixed = flow.at(AT_MIXED_MOVED, swap(mixed, positions)).reshape(count, -1)
    branch = flow.at(AT_BRANCH, plain(mixed, full_out))
    got_branch = flow.at(AT_GOT_BRANCH, trade(branch))
    middle, two_own, two_other = call(
        middle_kernel,
        "middle",
        (4,),
        rows
        + [(branch, (step, depth), straight), (got_branch, (step, depth), crossed)]
        + [(gain_two, (1, depth), top)],
        [((count, depth), f32, (step, depth), straight)] + split_rows,
        by_spot,
        [low_scratch],
    )

    two_own, two_other = flow.at(AT_MIDDLE, two_own, two_other)
    ups = flow.take(UPS_NEAR, UPS_FAR)
    gate_run = tuple(start + whole for start in units[0][0])
    up_run = tuple(start - hidden_units for start in units[0][1])
    ffn_own, ffn_sent = split_columns(
        list(zip(first, ups)), ([gate_run, up_run], units[1]), by_spot
    )
    ffn_other = flow.at(AT_FFN_OTHER, trade(ffn_sent))
    gate_up = flow.at(AT_GATE_UP, plain(two_own, ffn_own) + plain(two_other, ffn_other))
    width = gate_up.shape[1] // 2
    gate, upward = gate_up[:, :width], gate_up[:, width:]
    gate_sig = jax.nn.sigmoid(gate)
    hidden = (gate * gate_sig * upward).astype(bf16)
    upstream = jnp.concatenate([own_up, got_up])
    down_grad = over_rows(hidden, upstream).astype(bf16).reshape(spots, -1, depth)
    down_sent = [pick(down_grad, spot ^ k) for k in range(spots)]
    down_back = [[(b, a) for a, b in pairs] for pairs in down_pairs]
    down_sent = [lax.ppermute(p, PLANE, pairs) for p, pairs in zip(down_sent, down_back)]
    flow.send(DOWN_A, *down_sent[::2])
    flow.send(DOWN_B, *down_sent[1::2])
    third = flow.take(THIRD_A, THIRD_B)
    full_down = place([[(piece, 0)] for piece in third], by_spot, *weight_down.shape[1:], dtype=bf16)
    full_down = full_down.reshape(-1, depth)

    grad_hidden = by_columns(upstream, full_down)
    grad_upward = grad_hidden * gate * gate_sig
    grad_gate = grad_hidden * upward * gate_sig * (1.0 + gate * (1.0 - gate_sig))
    grad_gate_up = jnp.concatenate([grad_gate, grad_upward], axis=-1).astype(bf16)
    back = jnp.concatenate([by_columns(grad_gate_up, ffn_own), by_columns(grad_gate_up, ffn_other)])
    back = flow.at(AT_BACK, back)
    got_back = trade(back)
    got_back = flow.at(AT_GOT_BACK, got_back)
    wide, narrow = (step, depth), (step, depth // 2)
    grad_middle, grad_branch = call(
        middle_back_kernel,
        "middle_back",
        (4,),
        [(middle, wide, straight), (back, narrow, straight), (back, narrow, lower(4, straight))]
        + [(got_back, narrow, crossed), (got_back, narrow, lower(4, crossed))]
        + [(own_up, wide, mine), (got_up, wide, theirs), (gain_two, (1, depth), top)],
        [
            ((own_count, depth), f32, wide, mine),
            ((count, depth), bf16, wide, straight),
        ],
        by_spot,
        [scratch],
    )

    cut = lambda grad: [pick(grad.reshape(spots, slice_rows, -1), spot ^ k) for k in range(spots)]
    grad_branch = flow.at(AT_GRAD_BRANCH, grad_branch)
    ffn_grad_own = cut(over_rows(two_own, grad_gate_up).astype(bf16))
    ffn_grad_got = cut(trade(over_rows(two_other, grad_gate_up).astype(bf16)))
    ffn_grad_own = [hop(piece, k, spots) for k, piece in enumerate(ffn_grad_own)]
    flow.send(OWN_NEAR, *ffn_grad_own[:near])
    flow.send(OWN_FAR, ffn_grad_own[near])
    late = [
        hop(jnp.concatenate(pair, axis=1), k, spots)
        for k, pair in enumerate(
            zip(ffn_grad_got, cut(over_rows(mixed, grad_branch).astype(bf16)))
        )
    ]
    flow.send(LATE_NEAR, *late[:near])
    flow.send(LATE_FAR, late[near])
    grad_mixed = flow.at(AT_GRAD_MIXED, by_columns(grad_branch, full_out).astype(bf16))
    grad_mixed_frames = flow.at(AT_GRAD_MIXED_MOVED, swap(grad_mixed, positions))
    grad_qkv = over_frames(attend_back_kernel, 3 * depth // 2, qkv, grad_mixed_frames)
    grad_qkv = flow.at(AT_GRAD_QKV, grad_qkv)
    result = plain(hidden, full_down)
    result = (middle[:own_count] + result[:own_count] + trade(result[own_count:])).astype(bf16)
    down_sent = [v for pair in zip(flow.take(DOWN_A), flow.take(DOWN_B)) for v in pair]
    flow.send(
        SUM_DOWN, place([[(piece, 0)] for piece in down_sent], by_slice, *weight_down.shape[1:])
    )
    grad_qkv_rows = swap(grad_qkv, positions).reshape(count, -1)
    grad_qkv_rows = flow.at(AT_GRAD_QKV_MOVED, grad_qkv_rows)
    grad_qkv_rows, result = tie(grad_qkv_rows, result)
    flow.send(RESULT, rows_from_spots(result, positions))
    qkv_grad_got = trade(over_rows(one_other, grad_qkv_rows).astype(bf16))
    qkv_grad_own = flow.at(AT_QKV_GRAD, over_rows(one_own, grad_qkv_rows).astype(bf16))
    qkv_sent = [jnp.concatenate(pair) for pair in zip(cut(qkv_grad_own), cut(qkv_grad_got))]
    *qkv_sent, grad_qkv_rows = tie(*qkv_sent, grad_qkv_rows)
    qkv_sent = [hop(piece, k, spots) for k, piece in enumerate(qkv_sent)]
    flow.send(QKV_NEAR, *qkv_sent[:near])
    flow.send(QKV_FAR, qkv_sent[near])
    back_own = by_columns(grad_qkv_rows, qkv_own)
    back_other = by_columns(grad_qkv_rows, qkv_other)
    back_own, back_other = flow.at(AT_LAST_BACK, back_own, back_other)
    ffn_grad_own, late = flow.take(OWN_NEAR, OWN_FAR), flow.take(LATE_NEAR, LATE_FAR)
    sum_ffn, term_ffn = place(
        [[(own, 0), (got, 0)] for own, got in zip(ffn_grad_own, late)],
        by_spot,
        slice_rows,
        2 * hidden_units,
        units,
        weight=weight_ffn,
    )
    sum_out = place([[(piece, 0)] for piece in late], by_spot, slice_rows, depth, skip=hidden_units)
    flow.send(SUMS, sum_ffn, sum_out)
    got_back = trade(jnp.concatenate([back_own[own_count:], back_other[own_count:]]))
    got_back = flow.at(AT_GOT_LAST, got_back)
    (grad_rows,) = call(
        input_back_kernel,
        "input_back",
        (2,),
        [(own_rows, wide, straight), (back_own, narrow, straight), (back_other, narrow, straight)]
        + [(got_back, narrow, straight), (got_back, narrow, lower(2, straight))]
        + [(grad_middle, wide, straight), (gain_one, (1, depth), top)],
        [((own_count, depth), bf16, wide, straight)],
        by_spot,
        [scratch],
    )
    grad_rows = flow.at(AT_GRAD_ROWS, grad_rows)
    grad_input = flow.at(AT_GRAD_INPUT, rows_from_spots(grad_rows, positions))
    (result,) = flow.take(RESULT)
    output = jnp.where(live, result, jnp.zeros_like(result))
    qkv_sent = flow.take(QKV_NEAR, QKV_FAR)
    qkv_sent[near] = flow.at(AT_QKV_FAR, qkv_sent[near])
    sum_ffn, sum_out = flow.take(SUMS)
    (sum_down,) = flow.take(SUM_DOWN)
    sum_qkv, term_attn = place(
        [[(piece, 0), (piece, slice_rows)] for piece in qkv_sent],
        by_spot,
        slice_rows,
        3 * depth,
        heads,
        weight=weight_qkv,
    )
    gain_terms = [
        term.reshape(spots, slice_rows) / gain.astype(f32)
        for term, gain in ((term_attn, gain_attn), (term_ffn, gain_ffn))
    ]
    return (output, grad_input, sum_qkv, sum_out, sum_ffn, sum_down, *gain_terms)


def solution(mesh):
    plane, lines = mesh.shape["frames"], mesh.shape["pos"]

    def run(*arrays):
        positions, depth = arrays[0].shape[1:]
        spots = positions // lines
        slice_rows = depth // plane
        shares = arrays[5].shape[2] // 4
        fits = plane == 2 * spots and spots & (spots - 1) == 0
        fits = fits and slice_rows % LANES == 0 and shares % LANES == 0
        if fits:
            inner = Mesh(mesh.devices.reshape(spots, 2, lines), PLANE + ("pos",))
            by_frame, weight, plan = P(PLANE + ("pos",)), P("pos", PLANE), spots_plan
        else:
            inner, plan = mesh, gathered_plan
            by_frame, weight = P(("frames", "pos")), P("pos", "frames")
        return jax.shard_map(
            plan,
            mesh=inner,
            in_specs=(by_frame,) * 3 + (weight,) * 6 + (by_frame,),
            out_specs=(by_frame,) * 2 + (weight,) * 6,
            check_vma=False,
        )(*arrays)

    return run
```
